32 devices in a mesh: member: 4 (over y, x), lon: 8 (over z, core).
Axes of the slice: x: 2, y: 2, z: 4, core: 2. Of those that a mesh axis runs over, the one named last changes fastest.
Arguments:
- fields: bfloat16 [4, 641, 20, 360], P('member', None, None, 'lon'), may hold values from -6 to 6
- weight: bfloat16 [5, 5, 73, 641], replicated, may hold values from -0.046875 to 0.046875
- out_bias: float32 [73], replicated, may hold values from -3 to 3
- observed: float32 [73, 16, 360], P(None, None, 'lon'), may hold values from -6 to 6
- widths: float32 [73], replicated, may hold values from 0.5 to 2
- owner_start: int32 [8, 5], P('lon'), may hold values from 0 to 16, as said below
Outputs:
- out_grad: bfloat16 [4, 73, 16, 360], P('member', None, None, 'lon')
- owned_score: float32 [8, 4, 540], P('lon', 'member')
- weight_grad: float32 [5, 5, 73, 641], replicated
- bias_grad: float32 [73], replicated
The draws below stay inside these ranges and needn't reach their ends.
Inputs may be any that keep to these rules, and one draw needn't show every extreme that they name: Each row owner_start[l] starts at 0, never falls and ends at 16; owner r of longitude group l holds blocks owner_start[l, r] to owner_start[l, r + 1] - 1, at most 12 of them, and in every group some owner holds exactly 12.
All inputs are finite; a program needn't handle non-finite values.
Results may differ from the reference program's by a relative error of at most 0.0063.
Values may be sent and summed in bfloat16 or wider, within the bound.
No kernel may reach another device: no remote copies, remote signals or barrier semaphores. Data moves between devices by JAX's collectives and lax.ppermute only.
A program may use at most 128 MiB of HBM per device.

```python
import math
import jax
import jax.numpy as jnp
from jax import lax

CIN = 641
COUT = 73
LAT = 16
LON_DEV = 45
BLOCK = 45
MEMBERS = 4
LON = 360
PB = 16
CAP = 12
N_MEMBER = 4
N_LON = 8


def draw_owner_start(key, part):

    def one_group(group_key):
        first_key = jax.random.fold_in(group_key, 11)
        second_key = jax.random.fold_in(group_key, 23)
        busiest = jax.random.randint(first_key, (), 0, N_MEMBER)
        counts = jnp.where(jnp.arange(N_MEMBER) == busiest, CAP, 0).astype(jnp.int32)

        def place_block(index, current):
            ranks = jax.random.randint(jax.random.fold_in(second_key, index), (N_MEMBER,), 0, 1 << 20)
            ranks = ranks * N_MEMBER + jnp.arange(N_MEMBER, dtype=jnp.int32)
            ranks = jnp.where(current < CAP, ranks, -1)
            winner = jnp.argmax(ranks)
            return current + (jnp.arange(N_MEMBER) == winner).astype(jnp.int32)
        counts = lax.fori_loop(0, PB - CAP, place_block, counts)
        return jnp.concatenate([jnp.zeros((1,), jnp.int32), jnp.cumsum(counts).astype(jnp.int32)])
    group_keys = jax.random.split(jax.random.fold_in(key, 7), N_LON)
    return jax.vmap(one_group)(group_keys).astype(jnp.int32)


def steps_of(own_key, extent, shards, low, high):
    def one(position, shards_of):
        heights = jax.random.uniform(jax.random.fold_in(jax.random.fold_in(own_key, 6), position), (shards_of,), jnp.float32, low / len(shards), high / len(shards))
        return jnp.repeat(jnp.exp(heights), extent[position] // shards_of).reshape((-1,) + (1,) * (len(extent) - position - 1))

    factor_of = one(*shards[0])
    for cut in shards[1:]:
        factor_of = factor_of * one(*cut)
    return factor_of


def gaussian(key, extent, deviation, most, cuts=(), kind=jnp.bfloat16):
    array = jax.random.normal(key, extent, jnp.float32) * deviation
    if len(cuts) > 0:
        array = steps_of(key, extent, cuts, -0.22, 0.18) * array
    return jnp.clip(array, min=-most, max=most).astype(kind)


def setup_inputs(seed: int = 0) -> dict:
    arg_keys = jax.random.split(jax.random.key(seed), 7)
    fields = gaussian(arg_keys[0], (MEMBERS, CIN, LAT + 4, LON), 1.0, 6.0, ((0, 4), (3, 8)))
    weight = gaussian(arg_keys[1], (5, 5, COUT, CIN), (25 * CIN) ** -0.5, 0.046875)
    out_bias = gaussian(arg_keys[2], (COUT,), 0.5, 3.0, (), jnp.float32)
    observed = gaussian(arg_keys[3], (COUT, LAT, LON), 1.0, 6.0, ((2, 8),), jnp.float32)
    widths = jnp.clip(jnp.exp(jax.random.uniform(arg_keys[4], (COUT,), jnp.float32, math.log(0.5), math.log(2.0))), 0.5, 2.0)
    owner_start = draw_owner_start(jax.random.fold_in(arg_keys[6], 71), 0)
    return {"fields": fields, "weight": weight, "out_bias": out_bias, "observed": observed, "widths": widths, "owner_start": owner_start}


def kernel_terms(values, target, widths):
    members = values.astype(jnp.float32)
    ensemble = members.shape[0]
    inverse = (1.0 / (widths * widths))[:, None]
    spread = members[:, None] - members[None, :]
    kernel_pair = jnp.exp(-0.5 * spread * spread * inverse)
    misfit = members - target[None]
    kernel_obs = jnp.exp(-0.5 * misfit * misfit * inverse)
    per_channel = lax.optimization_barrier(jnp.sum(kernel_pair, axis=(0, 1))) / (2.0 * ensemble * ensemble) - lax.optimization_barrier(jnp.sum(kernel_obs, axis=0)) / ensemble
    scores = lax.optimization_barrier(jnp.mean(per_channel, axis=0))
    gradient = inverse * (misfit * kernel_obs - lax.optimization_barrier(jnp.sum(kernel_pair * spread, axis=1)) / ensemble)
    return (scores, gradient.astype(jnp.bfloat16))

def wrap_lon(member_field):
    return jnp.concatenate([member_field[..., -2:], member_field, member_field[..., :2]], axis=-1)

def tap_stack(gradients, rows_in, padded_width):
    leading = gradients.ndim - 2
    padded = jnp.pad(gradients, [(0, 0)] * leading + [(4, 4), (4, 4)])
    pieces = [padded[..., 4 - row_tap:4 - row_tap + rows_in, 4 - col_tap:4 - col_tap + padded_width] for row_tap in range(5) for col_tap in range(5)]
    return jnp.stack(pieces, axis=-4)

def reference(fields, weight, out_bias, observed, widths, owner_start):
    flat_weight = weight.reshape(25 * COUT, CIN)
    rows_in = LAT + 4
    padded_width = LON + 4

    def forward(member_field):
        padded = wrap_lon(member_field).reshape(CIN, rows_in * padded_width)
        tap_sums = jnp.dot(flat_weight, padded, preferred_element_type=jnp.float32).reshape(5, 5, COUT, rows_in, padded_width)
        convolved = jnp.broadcast_to(out_bias[:, None, None], (COUT, LAT, LON))
        for row_tap in range(5):
            for col_tap in range(5):
                convolved = convolved + tap_sums[row_tap, col_tap, :, row_tap:row_tap + LAT, col_tap:col_tap + LON]
        return convolved.astype(jnp.bfloat16)
    outputs = lax.map(forward, fields)
    by_channel = jnp.transpose(outputs.reshape(MEMBERS, COUT, LAT * LON), (1, 0, 2))
    truth_flat = observed.reshape(COUT, LAT * LON)

    def channel_terms(packed):
        values, target, spread_width = packed
        return kernel_terms(values[:, None, :], target[None, :], spread_width[None])
    scores, gradients = lax.map(channel_terms, (by_channel, truth_flat, widths))
    point_score = lax.optimization_barrier(jnp.mean(scores, axis=0))
    out_grad = jnp.transpose(gradients[:, :, 0, :], (1, 0, 2)).reshape(MEMBERS, COUT, LAT, LON)
    blocked = jnp.transpose(point_score.reshape(LAT, N_LON, LON_DEV), (1, 0, 2)).reshape(N_LON, PB, BLOCK)
    slot_index = jnp.arange(CAP, dtype=jnp.int32)
    starts = owner_start[:, :-1]
    owned_blocks = owner_start[:, 1:] - starts
    filled = slot_index[None, None, :] < owned_blocks[:, :, None]
    chosen = jnp.where(filled, starts[:, :, None] + slot_index[None, None, :], 0).reshape(N_LON, N_MEMBER * CAP).astype(jnp.int32)
    picked = jnp.take_along_axis(blocked, chosen[:, :, None], axis=1).reshape(N_LON, N_MEMBER, CAP, BLOCK)
    owned_score = jnp.where(filled[..., None], picked, 0.0).reshape(N_LON, N_MEMBER, CAP * BLOCK)

    def accumulate(running, packed):
        member_field, member_grad = packed
        padded = wrap_lon(member_field).reshape(CIN, rows_in * padded_width)
        stacked = tap_stack(member_grad, rows_in, padded_width).reshape(25 * COUT, rows_in * padded_width)
        weight_part = lax.dot_general(stacked, padded, (((1,), (1,)), ((), ())), preferred_element_type=jnp.float32)
        bias_part = lax.optimization_barrier(jnp.sum(member_grad.astype(jnp.float32), axis=(1, 2)))
        return ((running[0] + weight_part, running[1] + bias_part), None)
    start_sums = (jnp.zeros((25 * COUT, CIN), jnp.float32), jnp.zeros((COUT,), jnp.float32))
    (weight_sum, bias_sum), _ = lax.scan(accumulate, start_sums, (fields, out_grad))
    factor = 1.0 / math.sqrt(MEMBERS * LAT * LON)
    return (out_grad, owned_score, (weight_sum * factor).reshape(5, 5, COUT, CIN), bias_sum * factor)
```

```python
import functools
import math

import jax
import jax.numpy as jnp
from jax import lax
from jax.experimental import pallas as pl
from jax.experimental.pallas import tpu as pltpu
from jax.sharding import PartitionSpec as P

BLOCK = 45
LANES = 128
EDGE = 16


NT = (((1,), (1,)), ((), ()))
NN = (((1,), (0,)), ((), ()))


def round_up(value, unit):
    return -(-value // unit) * unit


def vmem():
    return pl.BlockSpec(memory_space=pltpu.VMEM)


def smem():
    return pl.BlockSpec(memory_space=pltpu.SMEM)


def forward_kernel(taps, lon_dev, f_ref, head_ref, tail_ref, w_ref, b_ref, o_ref, x_s, w_s, acc_s):
    rows_in, slots, wide = x_s.shape
    out_chan, in_chan = w_ref.shape[1:]
    padded_out = w_s.shape[1]
    rows_out = rows_in - taps + 1
    points = rows_out * slots
    body = lon_dev // EDGE * EDGE
    full = in_chan // LANES * LANES
    x_s[:, :, full:] = jnp.zeros((rows_in, slots, wide - full), x_s.dtype)
    w_s[:, :, full:] = jnp.zeros((taps * taps, padded_out, wide - full), w_s.dtype)
    x_s[:, :EDGE, :in_chan] = head_ref[...]
    x_s[:, EDGE : EDGE + body, :in_chan] = f_ref[:, :body, :]
    x_s[:, EDGE + body :, :in_chan] = tail_ref[...]
    w_s[:, :out_chan, :in_chan] = w_ref[...]
    for a in range(taps):
        part = lax.dot_general(
            w_s[a * taps : (a + 1) * taps].reshape(taps * padded_out, wide),
            x_s[a : a + rows_out].reshape(points, wide),
            NT,
            preferred_element_type=jnp.float32,
        )
        if a == 0:
            acc_s[...] = part
        else:
            acc_s[...] += part
    half = taps // 2
    slot = lax.broadcasted_iota(jnp.int32, (1, points), 1) % slots
    inside = (slot >= EDGE) & (slot < EDGE + lon_dev)
    for lo in range(0, padded_out, EDGE):
        total = jnp.zeros((EDGE, points), jnp.float32) + b_ref[lo : lo + EDGE, :]
        for b in range(taps):
            piece = acc_s[b * padded_out + lo : b * padded_out + lo + EDGE, :]
            shift = (half - b) % points
            total = total + (pltpu.roll(piece, shift, 1) if shift else piece)
        row = lo + lax.broadcasted_iota(jnp.int32, (EDGE, 1), 0)
        keep = inside & (row < out_chan)
        o_ref[lo : lo + EDGE, :] = jnp.where(keep, total, 0.0).astype(o_ref.dtype)


def gradient_kernel(plan, *refs):
    members = plan["members"]
    taps, out_chan, padded_out = plan["taps"], plan["out_chan"], plan["padded_out"]
    rows_out, slots = plan["rows_out"], plan["slots"]
    main, rest, pairs, all_rows = plan["main"], plan["rest"], plan["pairs"], plan["all_rows"]
    place_ref = refs[0]
    y_refs = refs[1 : 1 + members]
    x_refs = refs[1 + members : 1 + 2 * members]
    obs_ref, wid_ref, lhs_ref = refs[1 + 2 * members : 4 + 2 * members]
    g_ref, score_ref, send_ref, keep_ref, extra_ref = refs[4 + 2 * members : 9 + 2 * members]
    g_s, gs_s, wide_s = refs[9 + 2 * members :]
    points = rows_out * slots
    half = taps // 2
    stack = taps * padded_out
    step = 2 * LANES
    for left in range(0, points, step):
        tally = jnp.zeros((8, step), jnp.float32)
        for lo in range(0, padded_out, EDGE):
            rows = slice(lo, lo + EDGE)
            cols = slice(left, left + step)
            width = wid_ref[rows, :]
            inverse = 1.0 / (width * width)
            values = [y[rows, cols].astype(jnp.float32) for y in y_refs]
            target = obs_ref[rows, cols]
            pair_sum = jnp.full((EDGE, step), float(members), jnp.float32)
            pull = [jnp.zeros((EDGE, step), jnp.float32) for _ in values]
            for x in range(members):
                for y in range(x + 1, members):
                    spread = values[x] - values[y]
                    kernel_pair = jnp.exp(-0.5 * spread * spread * inverse)
                    pair_sum = pair_sum + 2.0 * kernel_pair
                    weighted = kernel_pair * spread
                    pull[x] = pull[x] + weighted
                    pull[y] = pull[y] - weighted
            obs_sum = jnp.zeros((EDGE, step), jnp.float32)
            for x in range(members):
                misfit = values[x] - target
                kernel_obs = jnp.exp(-0.5 * misfit * misfit * inverse)
                obs_sum = obs_sum + kernel_obs
                grad = inverse * (misfit * kernel_obs - pull[x] / members)
                g_s[x, rows, cols] = grad.astype(jnp.bfloat16)
            terms = pair_sum / (2.0 * members * members) - obs_sum / members
            row = lo + lax.broadcasted_iota(jnp.int32, (EDGE, 1), 0)
            terms = jnp.where(row < out_chan, terms, 0.0)
            for sub in range(0, EDGE, 8):
                tally = tally + terms[sub : sub + 8]
        score_ref[:, left : left + step] = jnp.sum(tally, axis=0, keepdims=True) / out_chan
    g_ref[...] = g_s[0]
    for x in range(members):
        for lo in range(0, padded_out, EDGE):
            grad = g_s[x, lo : lo + EDGE, :].astype(jnp.float32)
            for b in range(taps):
                shift = (b - half) % points
                moved = pltpu.roll(grad, shift, 1) if shift else grad
                start = b * padded_out + lo
                gs_s[x, start : start + EDGE, :] = moved.astype(jnp.bfloat16)
    extra_ref[...] = lax.dot_general(
        lhs_ref[...], gs_s[0], NT, preferred_element_type=jnp.float32
    )
    blocks = main + rest
    for a in range(taps):
        total = None
        for x in range(members):
            part = lax.dot_general(
                gs_s[x],
                x_refs[x][a : a + rows_out].reshape(points, blocks * LANES),
                NN,
                preferred_element_type=jnp.float32,
            )
            total = part if total is None else total + part
        for k in range(blocks):
            wide_s[k, a * stack : (a + 1) * stack, :] = total[:, k * LANES : (k + 1) * LANES]
    used = taps * stack
    if used < all_rows:
        wide_s[:, used:, :] = jnp.zeros((blocks, all_rows - used, LANES), jnp.float32)
    member, pair, core = place_ref[0], place_ref[1], place_ref[2]
    main_rows = all_rows // (2 * pairs)
    rest_rows = main_rows // members
    for s in range(pairs):
        target = lax.rem(pair + s, pairs)
        for out, side in ((keep_ref, core), (send_ref, 1 - core)):
            piece = 2 * target + side
            at = 0
            for k in range(main):
                source = pl.ds(pl.multiple_of(piece * main_rows, main_rows), main_rows)
                out[s, at : at + main_rows, :] = wide_s[k, source, :].astype(out.dtype)
                at += main_rows
            for k in range(main, blocks):
                first = member * (all_rows // members) + piece * rest_rows
                source = pl.ds(pl.multiple_of(first, rest_rows), rest_rows)
                out[s, at : at + rest_rows, :] = wide_s[k, source, :].astype(out.dtype)
                at += rest_rows


def assemble_kernel(plan, *refs):
    members = plan["members"]
    taps, out_chan, padded_out = plan["taps"], plan["out_chan"], plan["padded_out"]
    main, rest, pairs, all_rows = plan["main"], plan["rest"], plan["pairs"], plan["all_rows"]
    place_ref = refs[0]
    piece_refs = refs[1 : 1 + 2 * members]
    extra_ref, out_ref, all_s = refs[1 + 2 * members :]
    blocks = main * members + rest
    step = pl.program_id(0)
    member, pair, core = place_ref[0], place_ref[1], place_ref[2]
    main_rows = all_rows // (2 * pairs)
    rest_rows = main_rows // members

    @pl.when(step == 0)
    def _():
        for d in range(members):
            owner = member ^ d
            for which in range(2):
                ref = piece_refs[2 * d + which]
                side = core if which == 0 else 1 - core
                for s in range(pairs):
                    piece = 2 * lax.rem(pair - s + pairs, pairs) + side
                    at = 0
                    for k in range(main):
                        spot = pl.ds(pl.multiple_of(piece * main_rows, main_rows), main_rows)
                        all_s[k * members + owner, spot, :] = ref[s, at : at + main_rows, :].astype(
                            all_s.dtype
                        )
                        at += main_rows
                    for k in range(rest):
                        first = owner * (all_rows // members) + piece * rest_rows
                        spot = pl.ds(pl.multiple_of(first, rest_rows), rest_rows)
                        all_s[main * members + k, spot, :] = ref[s, at : at + rest_rows, :].astype(
                            all_s.dtype
                        )
                        at += rest_rows

    extras = extra_ref.shape[2]
    for b in range(taps):
        first = pl.multiple_of((step * taps + b) * padded_out, padded_out)
        for k in range(blocks):
            out_ref[b, :, k * LANES : (k + 1) * LANES] = all_s[
                k, pl.ds(first, padded_out), :
            ][:out_chan]
        if extras:
            column = extra_ref[0, b * padded_out : b * padded_out + out_chan, :]
            out_ref[b, :, blocks * LANES :] = column


def body(fields, weight, out_bias, observed, widths, owner_start):
    _, in_chan, rows_in, lon_dev = fields.shape
    taps, _, out_chan, _ = weight.shape
    half = taps // 2
    members = lax.axis_size("member")
    lon_count = lax.axis_size("lon")
    pairs = lon_count // 2
    rows_out = rows_in - taps + 1
    slots = round_up(EDGE + lon_dev + half, EDGE)
    points = rows_out * slots
    padded_out = round_up(out_chan, EDGE)
    full_blocks = in_chan // LANES
    main, rest = full_blocks // members, full_blocks % members
    extras = in_chan - full_blocks * LANES
    stack = taps * padded_out
    all_rows = round_up(taps * stack, 8 * members * lon_count)
    wide = round_up(in_chan, LANES)
    plan = dict(
        members=members, taps=taps, out_chan=out_chan, padded_out=padded_out, rows_out=rows_out,
        slots=slots, main=main, rest=rest, pairs=pairs, all_rows=all_rows,
    )
    own_member = lax.axis_index("member")
    own_lon = lax.axis_index("lon")
    place = jnp.stack([own_member, own_lon // 2, own_lon % 2]).astype(jnp.int32)

    def shift_lon(value, by):
        return lax.ppermute(value, "lon", [(i, (i + by) % lon_count) for i in range(lon_count)])

    def swap_core(value):
        return lax.ppermute(value, "lon", [(i, i ^ 1) for i in range(lon_count)])

    def swap_member(value, d):
        return lax.ppermute(value, "member", [(i, i ^ d) for i in range(members)])

    field = jnp.transpose(fields[0], (1, 2, 0))
    low = shift_lon(field[:, lon_dev - half :, :], 1)
    high = shift_lon(field[:, :half, :], -1)

    def blocks_for(owner):
        picked = [
            lax.dynamic_slice_in_dim(field, (k * members + owner) * LANES, LANES, 2)
            for k in range(main)
        ]
        picked.append(field[:, :, main * members * LANES : full_blocks * LANES])
        return jnp.concatenate(picked, axis=2)

    traded = [blocks_for(own_member)]
    for d in range(1, members):
        traded.append(swap_member(blocks_for(own_member ^ d), d))
    low_traded = shift_lon(jnp.stack([t[:, lon_dev - half :, :] for t in traded]), 1)
    high_traded = shift_lon(jnp.stack([t[:, :half, :] for t in traded]), -1)

    body_cols = lon_dev // EDGE * EDGE
    tail_pad = slots - EDGE - lon_dev - half

    def with_edges(own, lower, upper):
        return jnp.concatenate(
            [
                jnp.pad(lower, ((0, 0), (EDGE - half, 0), (0, 0))),
                own,
                jnp.pad(upper, ((0, 0), (0, tail_pad), (0, 0))),
            ],
            axis=1,
        )

    traded_fields = [
        with_edges(traded[d], low_traded[d], high_traded[d]) for d in range(members)
    ]

    head = jnp.pad(low, ((0, 0), (EDGE - half, 0), (0, 0)))
    tail = jnp.concatenate(
        [field[:, body_cols:, :], jnp.pad(high, ((0, 0), (0, tail_pad), (0, 0)))], axis=1
    )
    bias_column = jnp.pad(out_bias, (0, padded_out - out_chan))[:, None]
    own_outputs = pl.pallas_call(
        functools.partial(forward_kernel, taps, lon_dev),
        out_shape=jax.ShapeDtypeStruct((padded_out, points), jnp.bfloat16),
        in_specs=[vmem()] * 5,
        out_specs=vmem(),
        scratch_shapes=[
            pltpu.VMEM((rows_in, slots, wide), jnp.bfloat16),
            pltpu.VMEM((taps * taps, padded_out, wide), jnp.bfloat16),
            pltpu.VMEM((stack, points), jnp.float32),
        ],
        cost_estimate=pl.CostEstimate(
            flops=2 * taps * stack * points * wide, bytes_accessed=6_000_000, transcendentals=0
        ),
        name="forward",
    )(field, head, tail, weight.reshape(taps * taps, out_chan, in_chan), bias_column)
    outputs = [own_outputs] + [swap_member(own_outputs, d) for d in range(1, members)]

    truth = jnp.pad(
        observed,
        ((0, padded_out - out_chan), (0, 0), (EDGE, slots - EDGE - lon_dev)),
    ).reshape(padded_out, points)
    width_column = jnp.pad(widths, (0, padded_out - out_chan), constant_values=1.0)[:, None]
    last = jnp.concatenate(
        [v[:, :, full_blocks * LANES :] for v in (low, field, high)], axis=1
    )
    last = jnp.pad(last, ((0, 0), (EDGE - half, tail_pad), (0, 0)))
    last = jnp.transpose(last, (2, 0, 1)).reshape(extras, rows_in * slots)
    lhs_rows = [last[:, a * slots : a * slots + points] for a in range(taps)]
    lhs_rows.append(jnp.ones((1, points), jnp.bfloat16))
    lhs = jnp.concatenate(lhs_rows, axis=0)
    lhs_count = lhs.shape[0]
    lhs = jnp.pad(lhs, ((0, round_up(lhs_count, EDGE) - lhs_count), (0, 0)))

    main_rows = all_rows // lon_count
    rest_rows = main_rows // members
    piece_rows = main * main_rows + rest * rest_rows
    blocks = main + rest
    grad_own, score, send, keep, extra = pl.pallas_call(
        functools.partial(gradient_kernel, plan),
        out_shape=(
            jax.ShapeDtypeStruct((padded_out, points), jnp.bfloat16),
            jax.ShapeDtypeStruct((1, points), jnp.float32),
            jax.ShapeDtypeStruct((pairs, piece_rows, LANES), jnp.bfloat16),
            jax.ShapeDtypeStruct((pairs, piece_rows, LANES), jnp.float32),
            jax.ShapeDtypeStruct((lhs.shape[0], stack), jnp.float32),
        ),
        in_specs=[smem()] + [vmem()] * (2 * members + 3),
        out_specs=[vmem()] * 5,
        scratch_shapes=[
            pltpu.VMEM((members, padded_out, points), jnp.bfloat16),
            pltpu.VMEM((members, stack, points), jnp.bfloat16),
            pltpu.VMEM((blocks, all_rows, LANES), jnp.float32),
        ],
        cost_estimate=pl.CostEstimate(
            flops=2 * taps * stack * points * members * blocks * LANES,
            bytes_accessed=6_000_000,
            transcendentals=1_000_000,
        ),
        name="gradient",
    )(place, *outputs, *traded_fields, truth, width_column, lhs)

    summed = keep + swap_core(send).astype(jnp.float32)
    total = summed[0]
    for s in range(1, pairs):
        total = total + shift_lon(summed[s].astype(jnp.bfloat16), 2 * s).astype(jnp.float32)
    factor = 1.0 / math.sqrt(members * rows_out * lon_dev * lon_count)
    mine = (total * factor).astype(jnp.bfloat16)
    column = jnp.stack([mine] + [shift_lon(mine, 2 * s) for s in range(1, pairs)])
    gathered = [column] + [swap_member(column, d) for d in range(1, members)]
    pieces = []
    for value in gathered:
        pieces += [value, swap_core(value)]

    reach = 1
    while reach < lon_count:
        extra = extra + lax.ppermute(
            extra, "lon", [(i, i ^ reach) for i in range(lon_count)]
        )
        reach *= 2
    reach = 1
    while reach < members:
        extra = extra + swap_member(extra, reach)
        reach *= 2
    extra = extra * factor
    bias_grad = extra[lhs_count - 1, :out_chan]
    extra_cols = jnp.transpose(
        extra[: taps * extras].reshape(taps, extras, stack), (0, 2, 1)
    )
    weight_grad = pl.pallas_call(
        functools.partial(assemble_kernel, plan),
        out_shape=jax.ShapeDtypeStruct((taps * taps, out_chan, in_chan), jnp.float32),
        grid=(taps,),
        in_specs=[smem()]
        + [vmem()] * (2 * members)
        + [pl.BlockSpec((1, stack, extras), lambda a: (a, 0, 0))],
        out_specs=pl.BlockSpec((taps, out_chan, in_chan), lambda a: (a, 0, 0)),
        scratch_shapes=[pltpu.VMEM((full_blocks, all_rows, LANES), jnp.float32)],
        cost_estimate=pl.CostEstimate(flops=0, bytes_accessed=9_000_000, transcendentals=0),
        name="assemble",
    )(place, *pieces, extra_cols)
    weight_grad = weight_grad.reshape(taps, taps, out_chan, in_chan)

    out_grad = grad_own[:out_chan].reshape(1, out_chan, rows_out, slots)[
        :, :, :, EDGE : EDGE + lon_dev
    ]
    point_blocks = score.reshape(rows_out, slots)[:, EDGE : EDGE + lon_dev].reshape(-1, BLOCK)
    count = point_blocks.shape[0]
    capacity = max(2, 3 * count // members)
    starts = owner_start[0]
    first = lax.dynamic_slice_in_dim(starts, own_member, 1)[0]
    held = lax.dynamic_slice_in_dim(starts, own_member + 1, 1)[0] - first
    window = lax.dynamic_slice_in_dim(jnp.pad(point_blocks, ((0, capacity), (0, 0))), first, capacity, 0)
    slot_index = jnp.arange(capacity, dtype=jnp.int32)
    owned_score = jnp.where((slot_index < held)[:, None], window, 0.0).reshape(1, 1, -1)
    return (out_grad, owned_score, weight_grad, bias_grad)


def solution(mesh):
    in_specs = (P("member", None, None, "lon"), P(), P(), P(None, None, "lon"), P(), P("lon", None))
    out_specs = (P("member", None, None, "lon"), P("lon", "member", None), P(), P())
    return jax.shard_map(body, mesh=mesh, in_specs=in_specs, out_specs=out_specs, check_vma=False)
```

```python
import functools
import math

import jax
import jax.numpy as jnp
from jax import lax
from jax.experimental import pallas as pl
from jax.experimental.pallas import tpu as pltpu
from jax.sharding import PartitionSpec as P

BLOCK = 45
LANES = 128
ROWS = 8
CHUNKS = 2


NT = (((1,), (1,)), ((), ()))
NN = (((1,), (0,)), ((), ()))


def round_up(value, unit):
    return -(-value // unit) * unit


def vmem():
    return pl.BlockSpec(memory_space=pltpu.VMEM)


def smem():
    return pl.BlockSpec(memory_space=pltpu.SMEM)


def column_of(row_ref, fill):
    count = row_ref.shape[1]
    row = jnp.concatenate(
        [row_ref[...], jnp.full((1, LANES - count), fill, jnp.float32)], axis=1
    )
    return jnp.transpose(jnp.broadcast_to(row, (LANES, LANES)))[:, :1]


def forward_kernel(plan, f_ref, low_ref, high_ref, w_ref, b_ref, o_ref, x_s, w_s, acc_s):
    taps, half, offset = plan["taps"], plan["half"], plan["offset"]
    lon_dev, halo = plan["lon_dev"], 2 * plan["half"]
    rows_in, slots, wide = x_s.shape
    out_chan, in_chan = w_ref.shape[1:]
    padded_out = w_s.shape[1]
    rows_out = rows_in - taps + 1
    points = rows_out * slots
    bulk = lon_dev // ROWS * ROWS
    full = in_chan // LANES * LANES
    x_s[:, :, full:] = jnp.zeros((rows_in, slots, wide - full), x_s.dtype)
    w_s[:, :, full:] = jnp.zeros((taps * taps, padded_out, wide - full), w_s.dtype)
    w_s[:, :out_chan, :in_chan] = w_ref[...]
    x_s[:, offset : offset + bulk, :in_chan] = f_ref[:, :bulk, :]
    first = jnp.concatenate(
        [
            jnp.zeros((rows_in, offset - halo, in_chan), jnp.float32),
            low_ref[...].astype(jnp.float32),
        ],
        axis=1,
    )
    x_s[:, :offset, :in_chan] = first.astype(x_s.dtype)
    tail = slots - offset - bulk
    final = jnp.concatenate(
        [
            f_ref[:, bulk:, :].astype(jnp.float32),
            high_ref[...].astype(jnp.float32),
            jnp.zeros((rows_in, tail - (lon_dev - bulk) - halo, in_chan), jnp.float32),
        ],
        axis=1,
    )
    x_s[:, offset + bulk :, :in_chan] = final.astype(x_s.dtype)
    for a in range(taps):
        part = lax.dot_general(
            w_s[a * taps : (a + 1) * taps].reshape(taps * padded_out, wide),
            x_s[a : a + rows_out].reshape(points, wide),
            NT,
            preferred_element_type=jnp.float32,
        )
        if a == 0:
            acc_s[...] = part
        else:
            acc_s[...] += part
    slot = lax.broadcasted_iota(jnp.int32, (1, points), 1) % slots
    inside = (slot >= offset - half) & (slot < offset + lon_dev + half)
    bias = column_of(b_ref, 0.0)
    for lo in range(0, padded_out, 2 * ROWS):
        rows = slice(lo, lo + 2 * ROWS)
        total = jnp.zeros((2 * ROWS, points), jnp.float32) + bias[rows]
        for b in range(taps):
            piece = acc_s[b * padded_out + lo : b * padded_out + lo + 2 * ROWS, :]
            shift = (half - b) % points
            total = total + (pltpu.roll(piece, shift, 1) if shift else piece)
        row = lo + lax.broadcasted_iota(jnp.int32, (2 * ROWS, 1), 0)
        keep = inside & (row < out_chan)
        o_ref[rows, :] = jnp.where(keep, total, 0.0).astype(o_ref.dtype)


def traded_kernel(plan, *refs):
    members, main, rest = plan["members"], plan["main"], plan["rest"]
    pack, valid = plan["pack"], plan["valid"]
    count = (1 if main else 0) + (1 if rest else 0)
    out_ref = refs[-1]
    _, rows_in, slots, _ = out_ref.shape
    lon_dev = plan["lon_dev"]
    bulk = lon_dev // ROWS * ROWS
    out_ref[:, :, bulk:, :] = jnp.zeros(
        (members, rows_in, slots - bulk, out_ref.shape[3]), out_ref.dtype
    )
    for d in range(members):
        at = 0
        if main:
            out_ref[d, :, :lon_dev, : main * LANES] = refs[d * count][...]
            at = 1
        if rest:
            packed = refs[d * count + at]
            group_rows = rows_in // pack
            for g in range(pack):
                value = packed[...]
                if g:
                    value = pltpu.roll(value.astype(jnp.float32), LANES - g * valid, 2)
                out_ref[d, g * group_rows : (g + 1) * group_rows, :lon_dev, main * LANES :] = (
                    value.astype(out_ref.dtype)
                )


def spread_gradients(plan, g_ref, gs_s):
    taps, half, offset = plan["taps"], plan["half"], plan["offset"]
    padded_out, points = plan["padded_out"], plan["points"]
    for x in range(plan["members"]):
        for lo in range(0, padded_out, 2 * ROWS):
            grad = g_ref[x, lo : lo + 2 * ROWS, :].astype(jnp.float32)
            for b in range(taps):
                shift = (b - half - offset) % points
                moved = pltpu.roll(grad, shift, 1) if shift else grad
                start = b * padded_out + lo
                gs_s[x, start : start + 2 * ROWS, :] = moved.astype(jnp.bfloat16)


def weight_terms(plan, chunk, place_ref, x_ref, gs_s, wide_s, packed_s, send_ref, keep_ref):
    members, taps, main, rest = plan["members"], plan["taps"], plan["main"], plan["rest"]
    rows_out, points, pairs = plan["rows_out"], plan["points"], plan["pairs"]
    pack, valid, size = plan["pack"], plan["valid"], plan["chunk_rows"]
    stack = taps * plan["padded_out"]
    first, last = chunk * size, min((chunk + 1) * size, taps * stack)
    tiles = main + (1 if rest else 0)
    if last - first < size:
        wide_s[:, last - first :, :] = jnp.zeros(
            (tiles, size - (last - first), LANES), jnp.float32
        )
    for a in range(taps):
        lo, hi = max(first, a * stack), min(last, (a + 1) * stack)
        if lo >= hi:
            continue
        total = None
        for x in range(members):
            part = lax.dot_general(
                gs_s[x, lo - a * stack : hi - a * stack, :],
                x_ref[x, a : a + rows_out].reshape(points, tiles * LANES),
                NN,
                preferred_element_type=jnp.float32,
            )
            total = part if total is None else total + part
        for k in range(tiles):
            wide_s[k, lo - first : hi - first, :] = total[:, k * LANES : (k + 1) * LANES]
    short = size // pack
    if rest:
        lane = lax.broadcasted_iota(jnp.int32, (1, LANES), 1)
        packed = wide_s[main, :short, :]
        for g in range(1, pack):
            moved = pltpu.roll(wide_s[main, g * short : (g + 1) * short, :], g * valid, 1)
            packed = jnp.where(lane >= g * valid, moved, packed)
        packed_s[...] = packed
    pair, core = place_ref[1], place_ref[2]
    main_rows = size // (2 * pairs)
    rest_rows = main_rows // pack
    for s in range(pairs):
        for out, side in ((keep_ref, core), (send_ref, 1 - core)):
            piece = 2 * (pair ^ s) + side
            at = 0
            for k in range(main):
                source = pl.ds(pl.multiple_of(piece * main_rows, main_rows), main_rows)
                out[s, at : at + main_rows, :] = wide_s[k, source, :].astype(out.dtype)
                at += main_rows
            if rest:
                source = pl.ds(pl.multiple_of(piece * rest_rows, rest_rows), rest_rows)
                out[s, at : at + rest_rows, :] = packed_s[source, :].astype(out.dtype)


def gradient_kernel(plan, *refs):
    members = plan["members"]
    out_chan, padded_out, points = plan["out_chan"], plan["padded_out"], plan["points"]
    place_ref = refs[0]
    y_refs = refs[1 : 1 + members]
    x_ref, obs_ref, wid_ref, lhs_ref = refs[1 + members : 5 + members]
    g_ref, score_ref, extra_ref, send_ref, keep_ref = refs[5 + members : 10 + members]
    gs_s, wide_s, packed_s = refs[10 + members :]
    step = 2 * LANES
    width_all = column_of(wid_ref, 1.0)
    for left in range(0, points, step):
        tally = jnp.zeros((ROWS, step), jnp.float32)
        for lo in range(0, padded_out, 2 * ROWS):
            rows = slice(lo, lo + 2 * ROWS)
            cols = slice(left, left + step)
            shape = (2 * ROWS, step)
            width = width_all[rows]
            inverse = 1.0 / (width * width)
            values = [y[rows, cols].astype(jnp.float32) for y in y_refs]
            target = obs_ref[rows, cols]
            pair_sum = jnp.full(shape, float(members), jnp.float32)
            pull = [jnp.zeros(shape, jnp.float32) for _ in values]
            for x in range(members):
                for y in range(x + 1, members):
                    spread = values[x] - values[y]
                    kernel_pair = jnp.exp(-0.5 * spread * spread * inverse)
                    pair_sum = pair_sum + 2.0 * kernel_pair
                    weighted = kernel_pair * spread
                    pull[x] = pull[x] + weighted
                    pull[y] = pull[y] - weighted
            obs_sum = jnp.zeros(shape, jnp.float32)
            for x in range(members):
                misfit = values[x] - target
                kernel_obs = jnp.exp(-0.5 * misfit * misfit * inverse)
                obs_sum = obs_sum + kernel_obs
                grad = inverse * (misfit * kernel_obs - pull[x] / members)
                g_ref[x, rows, cols] = grad.astype(jnp.bfloat16)
            terms = pair_sum / (2.0 * members * members) - obs_sum / members
            row = lo + lax.broadcasted_iota(jnp.int32, (2 * ROWS, 1), 0)
            terms = jnp.where(row < out_chan, terms, 0.0)
            tally = tally + terms[:ROWS] + terms[ROWS:]
        score_ref[:, left : left + step] = jnp.sum(tally, axis=0, keepdims=True) / out_chan
    spread_gradients(plan, g_ref, gs_s)
    extra_ref[...] = lax.dot_general(
        lhs_ref[...], gs_s[0], NT, preferred_element_type=jnp.float32
    )
    weight_terms(plan, 0, place_ref, x_ref, gs_s, wide_s, packed_s, send_ref, keep_ref)


def later_kernel(plan, chunk, place_ref, g_ref, x_ref, send_ref, keep_ref, gs_s, wide_s, packed_s):
    spread_gradients(plan, g_ref, gs_s)
    weight_terms(plan, chunk, place_ref, x_ref, gs_s, wide_s, packed_s, send_ref, keep_ref)


def assemble_kernel(plan, chunk, layout, *refs):
    members, main, rest = plan["members"], plan["main"], plan["rest"]
    out_chan, padded_out, pairs = plan["out_chan"], plan["padded_out"], plan["pairs"]
    taps, pack, valid, size = plan["taps"], plan["pack"], plan["valid"], plan["chunk_rows"]
    sub = LANES // members
    total_taps = taps * taps
    place_ref, extra_ref = refs[:2]
    piece_refs = refs[2 : 2 + len(layout)]
    at = 2 + len(layout)
    if chunk:
        carry_ref = refs[at + 1]
        at += 2
    out_ref = refs[at]
    at += 1
    if chunk < CHUNKS - 1:
        next_ref = refs[at]
        at += 1
    all_s, packed_s, stage_s, sems = refs[at:]
    member, pair, core = place_ref[0], place_ref[1], place_ref[2]
    blocks = main * members + rest
    main_rows = size // (2 * pairs)
    rest_rows = main_rows // pack
    first = chunk * size
    begin = -(-first // padded_out) * padded_out if chunk == 0 else first // padded_out * padded_out
    carried = first - begin
    for ref, (d, shifts, other) in zip(piece_refs, layout):
        owner = member ^ d
        side = 1 - core if other else core
        for i, s in enumerate(shifts):
            piece = 2 * (pair ^ s) + side
            row = 0
            for k in range(main):
                spot = pl.ds(pl.multiple_of(carried + piece * main_rows, ROWS), main_rows)
                all_s[k * members + owner, spot, :] = ref[i, row : row + main_rows, :].astype(
                    jnp.float32
                )
                row += main_rows
            if rest:
                spot = pl.ds(pl.multiple_of(piece * rest_rows, ROWS), rest_rows)
                packed_s[owner, spot, :] = ref[i, row : row + rest_rows, :].astype(jnp.float32)
    if carried:
        all_s[:, :carried, :] = carry_ref[...]
    short = size // pack
    if rest:
        lane = lax.broadcasted_iota(jnp.int32, (1, LANES), 1)
        for k in range(rest):
            for g in range(pack):
                tile = None
                for owner in range(members):
                    shift = (owner * sub - g * valid - k * sub) % LANES
                    value = packed_s[owner]
                    if shift:
                        value = pltpu.roll(value, shift, 1)
                    tile = value if tile is None else jnp.where(lane >= owner * sub, value, tile)
                all_s[main * members + k, carried + g * short : carried + (g + 1) * short, :] = tile
    tap0 = begin // padded_out
    tap1 = total_taps if chunk == CHUNKS - 1 else (first + size) // padded_out
    extras = extra_ref.shape[2]
    copies = []
    for tap in range(tap0, tap1):
        a, b = tap // taps, tap % taps
        at_row = tap * padded_out - begin
        for k in range(blocks):
            stage_s[tap - tap0, :, k * LANES : (k + 1) * LANES] = all_s[
                k, at_row : at_row + out_chan, :
            ]
        if extras:
            stage_s[tap - tap0, :, blocks * LANES :] = extra_ref[
                a, b * padded_out : b * padded_out + out_chan, :
            ]
        copy = pltpu.make_async_copy(
            stage_s.at[tap - tap0], out_ref.at[tap], sems.at[tap - tap0]
        )
        copy.start()
        copies.append(copy)
    if chunk < CHUNKS - 1:
        rest_at = tap1 * padded_out - begin
        next_ref[...] = all_s[:, rest_at : rest_at + next_ref.shape[1], :]
    for copy in copies:
        copy.wait()


def body(fields, weight, out_bias, observed, widths, owner_start):
    _, in_chan, rows_in, lon_dev = fields.shape
    taps, _, out_chan, _ = weight.shape
    half = taps // 2
    halo = 2 * half
    members = lax.axis_size("member")
    lon_count = lax.axis_size("lon")
    pairs = lon_count // 2
    rows_out = rows_in - taps + 1
    offset = round_up(halo, ROWS)
    slots = round_up(offset + lon_dev + halo, 2 * ROWS)
    points = rows_out * slots
    padded_out = round_up(out_chan, 2 * ROWS)
    full_blocks = in_chan // LANES
    main, rest = full_blocks // members, full_blocks % members
    sub = LANES // members
    valid = rest * sub
    pack = LANES // valid if rest and rows_in % (LANES // valid) == 0 else 1
    extras = in_chan - full_blocks * LANES
    stack = taps * padded_out
    unit = CHUNKS * ROWS * pack * lon_count
    all_rows = round_up(taps * stack, unit)
    chunk_rows = all_rows // CHUNKS
    wide = round_up(in_chan, LANES)
    plan = dict(
        members=members, taps=taps, half=half, offset=offset, lon_dev=lon_dev, out_chan=out_chan,
        padded_out=padded_out, rows_out=rows_out, points=points, main=main, rest=rest, pairs=pairs,
        pack=pack, valid=valid, chunk_rows=chunk_rows,
    )
    own_member = lax.axis_index("member")
    own_lon = lax.axis_index("lon")
    place = jnp.stack([own_member, own_lon // 2, own_lon % 2]).astype(jnp.int32)
    factor = 1.0 / math.sqrt(members * rows_out * lon_dev * lon_count)

    def shift_lon(value, by):
        return lax.ppermute(value, "lon", [(i, (i + by) % lon_count) for i in range(lon_count)])

    def swap_lon(value, d):
        return lax.ppermute(value, "lon", [(i, i ^ d) for i in range(lon_count)])

    def swap_member(value, d):
        return lax.ppermute(value, "member", [(i, i ^ d) for i in range(members)])

    field = jnp.transpose(fields[0], (1, 2, 0))
    low = shift_lon(field[:, lon_dev - halo :, :], 1)
    high = shift_lon(field[:, :halo, :], -1)

    def main_for(owner):
        return jnp.concatenate(
            [
                lax.dynamic_slice_in_dim(field, (k * members + owner) * LANES, LANES, 2)
                for k in range(main)
            ],
            axis=2,
        )

    def rest_for(owner):
        base = main * members * LANES
        value = jnp.concatenate(
            [
                lax.dynamic_slice_in_dim(field, base + k * LANES + owner * sub, sub, 2)
                for k in range(rest)
            ],
            axis=2,
        )
        value = value.reshape(pack, rows_in // pack, lon_dev, valid)
        value = jnp.concatenate([value[g] for g in range(pack)], axis=2)
        return jnp.pad(value, ((0, 0), (0, 0), (0, LANES - pack * valid)))

    traded = []
    for d in range(members):
        parts = []
        if main:
            parts.append(main_for(own_member ^ d))
        if rest:
            parts.append(rest_for(own_member ^ d))
        if d:
            parts = [swap_member(p, d) for p in parts]
        traded += parts
    truth_low = shift_lon(observed[:, :, lon_dev - half :], 1)
    truth_high = shift_lon(observed[:, :, :half], -1)

    own_outputs = pl.pallas_call(
        functools.partial(forward_kernel, plan),
        out_shape=jax.ShapeDtypeStruct((padded_out, points), jnp.bfloat16),
        in_specs=[vmem()] * 5,
        out_specs=vmem(),
        scratch_shapes=[
            pltpu.VMEM((rows_in, slots, wide), jnp.bfloat16),
            pltpu.VMEM((taps * taps, padded_out, wide), jnp.bfloat16),
            pltpu.VMEM((stack, points), jnp.float32),
        ],
        cost_estimate=pl.CostEstimate(
            flops=2 * taps * stack * points * wide, bytes_accessed=6_000_000, transcendentals=0
        ),
        compiler_params=pltpu.CompilerParams(vmem_limit_bytes=24 << 20),
        name="forward",
    )(field, low, high, weight.reshape(taps * taps, out_chan, in_chan), out_bias[None, :])
    outputs = [own_outputs] + [swap_member(own_outputs, d) for d in range(1, members)]

    tiles = main + (1 if rest else 0)
    held_fields, truth_low, truth_high, observed_late, widths_late, field_late, _ = (
        lax.optimization_barrier(
            (traded, truth_low, truth_high, observed, widths, field, own_outputs)
        )
    )
    x_all = pl.pallas_call(
        functools.partial(traded_kernel, plan),
        out_shape=jax.ShapeDtypeStruct((members, rows_in, slots, tiles * LANES), jnp.bfloat16),
        in_specs=[vmem()] * len(held_fields),
        out_specs=vmem(),
        cost_estimate=pl.CostEstimate(flops=0, bytes_accessed=4_000_000, transcendentals=0),
        compiler_params=pltpu.CompilerParams(vmem_limit_bytes=24 << 20),
        name="traded",
    )(*held_fields)
    truth = jnp.pad(
        jnp.concatenate([truth_low, observed_late, truth_high], axis=2),
        (
            (0, padded_out - out_chan),
            (0, 0),
            (offset - half, slots - offset - lon_dev - half),
        ),
    ).reshape(padded_out, points)
    last = jnp.pad(field_late[:, :, full_blocks * LANES :], ((0, 0), (0, slots - lon_dev), (0, 0)))
    last = jnp.transpose(last, (2, 0, 1)).reshape(extras, rows_in * slots)
    lhs_rows = [last[:, a * slots : a * slots + points] for a in range(taps)]
    lhs_rows.append((jnp.arange(points)[None, :] % slots < lon_dev).astype(jnp.bfloat16))
    lhs = jnp.concatenate(lhs_rows, axis=0)
    lhs_count = lhs.shape[0]
    lhs = jnp.pad(lhs, ((0, round_up(lhs_count, 2 * ROWS) - lhs_count), (0, 0)))

    main_rows = chunk_rows // lon_count
    piece_rows = main * main_rows + (main_rows // pack if rest else 0)
    work = [
        pltpu.VMEM((members, stack, points), jnp.bfloat16),
        pltpu.VMEM((tiles, chunk_rows, LANES), jnp.float32),
        pltpu.VMEM((chunk_rows // pack, LANES), jnp.float32),
    ]
    pieces_shape = (
        jax.ShapeDtypeStruct((pairs, piece_rows, LANES), jnp.bfloat16),
        jax.ShapeDtypeStruct((pairs, piece_rows, LANES), jnp.float32),
    )
    estimate = pl.CostEstimate(
        flops=2 * stack * points * members * tiles * LANES * taps // CHUNKS,
        bytes_accessed=6_000_000,
        transcendentals=1_000_000,
    )
    grads, score, extra, send, keep = pl.pallas_call(
        functools.partial(gradient_kernel, plan),
        out_shape=(
            jax.ShapeDtypeStruct((members, padded_out, points), jnp.bfloat16),
            jax.ShapeDtypeStruct((1, points), jnp.float32),
            jax.ShapeDtypeStruct((lhs.shape[0], stack), jnp.float32),
        )
        + pieces_shape,
        in_specs=[smem()] + [vmem()] * (members + 4),
        out_specs=[vmem()] * 5,
        scratch_shapes=work,
        cost_estimate=estimate,
        compiler_params=pltpu.CompilerParams(vmem_limit_bytes=32 << 20),
        name="gradient",
    )(place, *outputs, x_all, truth, widths_late[None, :], lhs)
    terms = [(send, keep)]
    for chunk in range(1, CHUNKS):
        terms.append(
            pl.pallas_call(
                functools.partial(later_kernel, plan, chunk),
                out_shape=pieces_shape,
                in_specs=[smem(), vmem(), vmem()],
                out_specs=[vmem()] * 2,
                scratch_shapes=work,
                cost_estimate=estimate,
                compiler_params=pltpu.CompilerParams(vmem_limit_bytes=32 << 20),
                name="later",
            )(place, grads, x_all)
        )

    def reduce_and_gather(send, keep):
        part = keep + swap_lon(send, 1).astype(jnp.float32)
        stage = 1
        while stage < pairs:
            arrived = swap_lon(part[1::2].astype(jnp.bfloat16), 2 * stage)
            part = part[0::2] + arrived.astype(jnp.float32)
            stage *= 2
        near = (part * factor).astype(jnp.bfloat16)
        shifts = [0]
        stage = pairs // 2
        while stage > 1:
            near = jnp.concatenate([near, swap_lon(near, 2 * stage)])
            shifts = shifts + [s | stage for s in shifts]
            stage //= 2
        parts = [(near, tuple(shifts))]
        if pairs > 1:
            parts.append((swap_lon(near, 2), tuple(s | 1 for s in shifts)))
        held = []
        for index, (value, shifts) in enumerate(parts):
            got = {0: value}
            for d in range(1, members):
                if members == 4 and d == 3:
                    via = 1 + index % 2
                    got[d] = swap_member(got[via], 3 - via)
                else:
                    got[d] = swap_member(value, d)
            for d in range(members):
                held.append((got[d], (d, shifts, False)))
                held.append((swap_lon(got[d], 1), (d, shifts, True)))
        return held

    reach = 1
    while reach < lon_count:
        extra = extra + swap_lon(extra, reach)
        reach *= 2
    reach = 1
    while reach < members:
        extra = extra + swap_member(extra, reach)
        reach *= 2
    extra = extra * factor
    bias_grad = extra[lhs_count - 1, half * padded_out : half * padded_out + out_chan]
    extra_cols = jnp.transpose(
        extra[: taps * extras].reshape(taps, extras, stack), (0, 2, 1)
    )
    total_taps = taps * taps
    grad_shape = jax.ShapeDtypeStruct((total_taps, out_chan, in_chan), jnp.float32)
    weight_grad = carry = None
    for chunk in range(CHUNKS):
        held = reduce_and_gather(*terms[chunk])
        layout = tuple(where for _, where in held)
        begin = chunk * chunk_rows // padded_out * padded_out
        carried = chunk * chunk_rows - begin
        final = chunk == CHUNKS - 1
        tap0 = begin // padded_out
        tap1 = total_taps if final else (chunk + 1) * chunk_rows // padded_out
        inputs = [place, extra_cols] + [value for value, _ in held]
        specs = [smem()] + [vmem()] * (1 + len(held))
        aliases = {}
        if chunk:
            aliases = {len(inputs): 0}
            inputs += [weight_grad, carry]
            specs += [pl.BlockSpec(memory_space=pl.ANY), vmem()]
        shapes = [grad_shape]
        outs = [pl.BlockSpec(memory_space=pl.ANY)]
        if not final:
            left = (chunk + 1) * chunk_rows - tap1 * padded_out
            shapes.append(jax.ShapeDtypeStruct((full_blocks, max(left, ROWS), LANES), jnp.float32))
            outs.append(vmem())
        result = pl.pallas_call(
            functools.partial(assemble_kernel, plan, chunk, layout),
            out_shape=shapes,
            in_specs=specs,
            out_specs=outs,
            scratch_shapes=[
                pltpu.VMEM((full_blocks, carried + chunk_rows + ROWS, LANES), jnp.float32),
                pltpu.VMEM((members, chunk_rows // pack, LANES), jnp.float32),
                pltpu.VMEM((tap1 - tap0, out_chan, in_chan), jnp.float32),
                pltpu.SemaphoreType.DMA((tap1 - tap0,)),
            ],
            input_output_aliases=aliases,
            cost_estimate=pl.CostEstimate(flops=0, bytes_accessed=5_000_000, transcendentals=0),
            compiler_params=pltpu.CompilerParams(vmem_limit_bytes=32 << 20),
            name="assemble",
        )(*inputs)
        weight_grad = result[0]
        if not final:
            carry = result[1]
    weight_grad = weight_grad.reshape(taps, taps, out_chan, in_chan)

    out_grad = grads[0, :out_chan].reshape(1, out_chan, rows_out, slots)[
        :, :, :, offset : offset + lon_dev
    ]
    point_blocks = score.reshape(rows_out, slots)[:, offset : offset + lon_dev].reshape(-1, BLOCK)
    count = point_blocks.shape[0]
    capacity = max(2, 3 * count // members)
    starts = owner_start[0]
    first = lax.dynamic_slice_in_dim(starts, own_member, 1)[0]
    owned = lax.dynamic_slice_in_dim(starts, own_member + 1, 1)[0] - first
    window = lax.dynamic_slice_in_dim(
        jnp.pad(point_blocks, ((0, capacity), (0, 0))), first, capacity, 0
    )
    slot_index = jnp.arange(capacity, dtype=jnp.int32)
    owned_score = jnp.where((slot_index < owned)[:, None], window, 0.0).reshape(1, 1, -1)
    return (out_grad, owned_score, weight_grad, bias_grad)


def solution(mesh):
    in_specs = (P("member", None, None, "lon"), P(), P(), P(None, None, "lon"), P(), P("lon", None))
    out_specs = (P("member", None, None, "lon"), P("lon", "member", None), P(), P())
    return jax.shard_map(body, mesh=mesh, in_specs=in_specs, out_specs=out_specs, check_vma=False)
```

```python
import functools
import math

import jax
import jax.numpy as jnp
from jax import lax
from jax.experimental import pallas as pl
from jax.experimental.pallas import tpu as pltpu
from jax.sharding import PartitionSpec as P

BLOCK = 45
LANES = 128
ROWS = 8
SPECIAL = 16


NT = (((1,), (1,)), ((), ()))
NN = (((1,), (0,)), ((), ()))


def round_up(value, unit):
    return -(-value // unit) * unit


def vmem():
    return pl.BlockSpec(memory_space=pltpu.VMEM)


def smem():
    return pl.BlockSpec(memory_space=pltpu.SMEM)


def limit(mib):
    return pltpu.CompilerParams(vmem_limit_bytes=mib << 20)


def cost(flops, moved, special=0):
    return pl.CostEstimate(flops=flops, bytes_accessed=moved, transcendentals=special)


def column_of(row_ref, fill):
    count = row_ref.shape[1]
    row = jnp.concatenate(
        [row_ref[...], jnp.full((1, LANES - count), fill, jnp.float32)], axis=1
    )
    return jnp.transpose(jnp.broadcast_to(row, (LANES, LANES)))[:, :1]


def pack_kernel(plan, place_ref, f_ref, *out_refs):
    members, main, rest = plan["members"], plan["main"], plan["rest"]
    pack, valid, sub = plan["pack"], plan["valid"], plan["sub"]
    rows_in, lon_dev, in_chan = f_ref.shape
    group = rows_in // pack
    base = main * members
    lane = lax.broadcasted_iota(jnp.int32, (1, 1, LANES), 2)
    full = (base + rest) * LANES
    slab = jnp.zeros((1, lon_dev, LANES), jnp.float32)
    for e in range(in_chan - full):
        for r in range(rows_in):
            value = f_ref[r : r + 1, :, full + e : full + e + 1].astype(jnp.float32)
            slab = jnp.where(lane == e * rows_in + r, value, slab)
    for d in range(members):
        owner = place_ref[0] ^ d
        out = out_refs[d]
        for k in range(main):
            spot = pl.ds(pl.multiple_of((k * members + owner) * LANES, LANES), LANES)
            out[k * rows_in : (k + 1) * rows_in] = f_ref[:, :, spot]
        for i in range(group):
            row = None
            for g in range(pack):
                for k in range(rest):
                    tile = f_ref[
                        g * group + i, :, (base + k) * LANES : (base + k + 1) * LANES
                    ].astype(jnp.float32)
                    start = g * valid + k * sub
                    moved = pltpu.roll(tile, lax.rem(start - owner * sub + LANES, LANES), 1)
                    row = moved if row is None else jnp.where(lane[0] >= start, moved, row)
            out[main * rows_in + i] = row.astype(out.dtype)
        out[main * rows_in + group] = slab[0].astype(out.dtype)


def forward_kernel(plan, place_ref, f_ref, near_ref, far_ref, w_ref, b_ref, o_ref, x_s, w_s, acc_s):
    taps, half, offset = plan["taps"], plan["half"], plan["offset"]
    lon_dev, halo = plan["lon_dev"], 2 * plan["half"]
    rows_in, slots, wide = x_s.shape
    out_chan, in_chan = w_ref.shape[1:]
    padded_out = w_s.shape[1]
    rows_out = rows_in - taps + 1
    points = rows_out * slots
    bulk = lon_dev // ROWS * ROWS
    full = in_chan // LANES * LANES
    x_s[:, :, full:] = jnp.zeros((rows_in, slots, wide - full), x_s.dtype)
    w_s[:, :, full:] = jnp.zeros((taps * taps, padded_out, wide - full), w_s.dtype)
    w_s[:, :out_chan, :in_chan] = w_ref[...]
    x_s[:, offset : offset + bulk, :in_chan] = f_ref[:, :bulk, :]
    near = near_ref[...].astype(jnp.float32)
    far = far_ref[...].astype(jnp.float32)
    even = place_ref[2] == 0
    first = jnp.concatenate(
        [
            jnp.zeros((rows_in, offset - halo, in_chan), jnp.float32),
            jnp.where(even, far, near),
        ],
        axis=1,
    )
    x_s[:, :offset, :in_chan] = first.astype(x_s.dtype)
    tail = slots - offset - bulk
    final = jnp.concatenate(
        [
            f_ref[:, bulk:, :].astype(jnp.float32),
            jnp.where(even, near, far),
            jnp.zeros((rows_in, tail - (lon_dev - bulk) - halo, in_chan), jnp.float32),
        ],
        axis=1,
    )
    x_s[:, offset + bulk :, :in_chan] = final.astype(x_s.dtype)
    for a in range(taps):
        part = lax.dot_general(
            w_s[a * taps : (a + 1) * taps].reshape(taps * padded_out, wide),
            x_s[a : a + rows_out].reshape(points, wide),
            NT,
            preferred_element_type=jnp.float32,
        )
        if a == 0:
            acc_s[...] = part
        else:
            acc_s[...] += part
    slot = lax.broadcasted_iota(jnp.int32, (1, points), 1) % slots
    inside = (slot >= offset - half) & (slot < offset + lon_dev + half)
    bias = column_of(b_ref, 0.0)
    for lo in range(0, padded_out, 2 * ROWS):
        rows = slice(lo, lo + 2 * ROWS)
        total = jnp.zeros((2 * ROWS, points), jnp.float32) + bias[rows]
        for b in range(taps):
            piece = acc_s[b * padded_out + lo : b * padded_out + lo + 2 * ROWS, :]
            shift = (half - b) % points
            total = total + (pltpu.roll(piece, shift, 1) if shift else piece)
        row = lo + lax.broadcasted_iota(jnp.int32, (2 * ROWS, 1), 0)
        keep = inside & (row < out_chan)
        o_ref[rows, :] = jnp.where(keep, total, 0.0).astype(o_ref.dtype)


def traded_kernel(plan, *refs):
    members, main, rest = plan["members"], plan["main"], plan["rest"]
    pack, valid, extras = plan["pack"], plan["valid"], plan["extras"]
    out_ref = refs[-1]
    _, rows_in, slots, _ = out_ref.shape
    lon_dev = plan["lon_dev"]
    bulk = lon_dev // ROWS * ROWS
    group = rows_in // pack
    lane = lax.broadcasted_iota(jnp.int32, (1, LANES), 1)
    out_ref[:, :, bulk:, :] = jnp.zeros(
        (members, rows_in, slots - bulk, out_ref.shape[3]), out_ref.dtype
    )
    for d in range(members):
        ref = refs[d]
        for k in range(main):
            out_ref[d, :, :lon_dev, k * LANES : (k + 1) * LANES] = ref[
                k * rows_in : (k + 1) * rows_in
            ]
        slab = ref[main * rows_in + group].astype(jnp.float32)
        for g in range(pack):
            for i in range(group):
                value = ref[main * rows_in + i].astype(jnp.float32)
                if g:
                    value = pltpu.roll(value, LANES - g * valid, 1)
                r = g * group + i
                for e in range(extras):
                    shift = (valid + e - (e * rows_in + r)) % LANES
                    moved = pltpu.roll(slab, shift, 1) if shift else slab
                    value = jnp.where(lane == valid + e, moved, value)
                value = jnp.where(lane == valid + extras, 1.0, value)
                out_ref[d, r, :lon_dev, main * LANES :] = value.astype(out_ref.dtype)


def split_bias(tile, row_high):
    row = lax.broadcasted_iota(jnp.int32, tile.shape, 0)
    size = tile.shape[0]
    total = jnp.where(row == row_high, tile + pltpu.roll(tile, size - 1, 0), tile)
    left = total - total.astype(jnp.bfloat16).astype(jnp.float32)
    return jnp.where(row == row_high + 1, pltpu.roll(left, 1, 0), total)


def fix_rows(plan, ref, index, piece, value_of):
    @pl.when(piece == 2 * plan["pairs"] - 1)
    def _():
        lo = plan["special_row"]
        tile = value_of(lo, lo + SPECIAL)
        ref[index, lo : lo + SPECIAL, :] = split_bias(tile, plan["bias_row"]).astype(ref.dtype)


def gradient_kernel(plan, *refs):
    members, taps, half = plan["members"], plan["taps"], plan["half"]
    out_chan, padded_out, points = plan["out_chan"], plan["padded_out"], plan["points"]
    main, pairs, pack, valid = plan["main"], plan["pairs"], plan["pack"], plan["valid"]
    rows_out, size, extras = plan["rows_out"], plan["half_rows"], plan["extras"]
    per_half, special = plan["per_half"], plan["special"]
    place_ref = refs[0]
    y_refs = refs[1 : 1 + members]
    x_ref, obs_ref, wid_ref = refs[1 + members : 4 + members]
    g_ref, score_ref, send_ref, keep_ref = refs[4 + members : 8 + members]
    g_s, gs_s, wide_s, packed_s = refs[8 + members :]
    step = 2 * LANES
    width_all = column_of(wid_ref, 1.0)
    for left in range(0, points, step):
        tally = jnp.zeros((ROWS, step), jnp.float32)
        for lo in range(0, padded_out, 2 * ROWS):
            rows = slice(lo, lo + 2 * ROWS)
            cols = slice(left, left + step)
            shape = (2 * ROWS, step)
            width = width_all[rows]
            inverse = 1.0 / (width * width)
            values = [y[rows, cols].astype(jnp.float32) for y in y_refs]
            target = obs_ref[rows, cols]
            pair_sum = jnp.full(shape, float(members), jnp.float32)
            pull = [jnp.zeros(shape, jnp.float32) for _ in values]
            for x in range(members):
                for y in range(x + 1, members):
                    spread = values[x] - values[y]
                    kernel_pair = jnp.exp(-0.5 * spread * spread * inverse)
                    pair_sum = pair_sum + 2.0 * kernel_pair
                    weighted = kernel_pair * spread
                    pull[x] = pull[x] + weighted
                    pull[y] = pull[y] - weighted
            obs_sum = jnp.zeros(shape, jnp.float32)
            for x in range(members):
                misfit = values[x] - target
                kernel_obs = jnp.exp(-0.5 * misfit * misfit * inverse)
                obs_sum = obs_sum + kernel_obs
                grad = inverse * (misfit * kernel_obs - pull[x] / members)
                g_s[x, rows, cols] = grad.astype(jnp.bfloat16)
            terms = pair_sum / (2.0 * members * members) - obs_sum / members
            row = lo + lax.broadcasted_iota(jnp.int32, (2 * ROWS, 1), 0)
            terms = jnp.where(row < out_chan, terms, 0.0)
            tally = tally + terms[:ROWS] + terms[ROWS:]
        score_ref[:, left : left + step] = jnp.sum(tally, axis=0, keepdims=True) / out_chan
    g_ref[...] = g_s[0]
    for x in range(members):
        for lo in range(0, padded_out, 2 * ROWS):
            grad = g_s[x, lo : lo + 2 * ROWS, :].astype(jnp.float32)
            for b in range(taps):
                shift = (b - half - plan["offset"]) % points
                moved = pltpu.roll(grad, shift, 1) if shift else grad
                start = b * padded_out + lo
                gs_s[x, start : start + 2 * ROWS, :] = moved.astype(jnp.bfloat16)
    tiles = main + 1
    stack = taps * padded_out
    total_taps = taps * taps
    split = size - special - SPECIAL
    for h in range(2):
        wide_s[:, h * size + special : (h + 1) * size, :] = jnp.zeros(
            (tiles, size - special, LANES), jnp.float32
        )
    for a in range(taps):
        total = None
        for x in range(members):
            part = lax.dot_general(
                gs_s[x],
                x_ref[x, a : a + rows_out].reshape(points, tiles * LANES),
                NN,
                preferred_element_type=jnp.float32,
            )
            total = part if total is None else total + part
        for b in range(taps):
            tap = a * taps + b
            block = total[b * padded_out : (b + 1) * padded_out]
            across = jnp.transpose(block[:, main * LANES :])
            if tap < 2 * per_half:
                h, i = tap // per_half, tap % per_half
                spans = [(0, padded_out, h * size + i * padded_out)]
                line = h * size + special + i * extras
            else:
                first = size - split
                spans = [(0, split, first), (split, padded_out, size + first)]
                line = size + special + per_half * extras
            for k in range(tiles):
                for lo, hi, at in spans:
                    wide_s[k, at : at + hi - lo, :] = block[lo:hi, k * LANES : (k + 1) * LANES]
            for e in range(extras):
                wide_s[0, line + e : line + e + 1, :padded_out] = across[valid + e : valid + e + 1]
            if a == 0 and b == half:
                line = size + special + plan["bias_row"]
                ones = valid + extras
                wide_s[0, line : line + 1, :padded_out] = across[ones : ones + 1]
    short = size // pack
    lane = lax.broadcasted_iota(jnp.int32, (1, LANES), 1)
    for h in range(2):
        packed = wide_s[main, h * size : h * size + short, :]
        for g in range(1, pack):
            at = h * size + g * short
            moved = pltpu.roll(wide_s[main, at : at + short, :], g * valid, 1)
            packed = jnp.where(lane >= g * valid, moved, packed)
        packed_s[h * short : (h + 1) * short, :] = packed
    pair, core = place_ref[1], place_ref[2]
    main_rows = size // pairs
    rest_rows = main_rows // pack
    for s in range(pairs):
        for out, side in ((keep_ref, core), (send_ref, 1 - core)):
            piece = 2 * (pair ^ s) + side
            at = 0
            for k in range(main):
                source = pl.ds(pl.multiple_of(piece * main_rows, main_rows), main_rows)
                out[s, at : at + main_rows, :] = wide_s[k, source, :].astype(out.dtype)
                at += main_rows
            source = pl.ds(pl.multiple_of(piece * rest_rows, rest_rows), rest_rows)
            out[s, at : at + rest_rows, :] = packed_s[source, :].astype(out.dtype)
        spot = 2 * size - main_rows
        fix_rows(
            plan, send_ref, s, 2 * (pair ^ s) + 1 - core,
            lambda lo, hi: wide_s[0, spot + lo : spot + hi, :]
            if main
            else packed_s[spot + lo : spot + hi, :],
        )


def core_add_kernel(plan, place_ref, keep_ref, got_ref, mine_ref, *out_refs):
    mine_ref[...] = keep_ref[0] + got_ref[0].astype(jnp.float32)
    pair, core = place_ref[1], place_ref[2]
    for s in range(1, plan["pairs"]):
        out = out_refs[s - 1]
        out[0] = (keep_ref[s] + got_ref[s].astype(jnp.float32)).astype(out.dtype)
        fix_rows(
            plan, out, 0, 2 * (pair ^ s) + core,
            lambda lo, hi: keep_ref[s, lo:hi, :] + got_ref[s, lo:hi, :].astype(jnp.float32),
        )


def pair_add_kernel(plan, factor, place_ref, mine_ref, *refs):
    out = refs[-1]

    def value(lo, hi):
        total = mine_ref[lo:hi, :]
        for ref in refs[:-1]:
            total = total + ref[0, lo:hi, :].astype(jnp.float32)
        return total * factor

    out[0] = value(0, mine_ref.shape[0]).astype(out.dtype)
    fix_rows(plan, out, 0, 2 * place_ref[1] + place_ref[2], value)


def assemble_kernel(plan, second, layout, *refs):
    members, main, rest = plan["members"], plan["main"], plan["rest"]
    out_chan, padded_out, pairs = plan["out_chan"], plan["padded_out"], plan["pairs"]
    pack, valid, sub = plan["pack"], plan["valid"], plan["sub"]
    size, extras, half, taps = plan["half_rows"], plan["extras"], plan["half"], plan["taps"]
    per_half, special = plan["per_half"], plan["special"]
    place_ref = refs[0]
    piece_refs = refs[1 : 1 + len(layout)]
    at = 1 + len(layout)
    if second:
        carry_ref = refs[at + 1]
        out_ref, bias_ref = refs[at + 2 : at + 4]
        all_s, packed_s, stage_s, sems = refs[at + 4 :]
    else:
        out_ref, carry_ref = refs[at : at + 2]
        all_s, packed_s, stage_s, sems = refs[at + 2 :]
    member, pair, core = place_ref[0], place_ref[1], place_ref[2]
    own_half = lax.div(pair, pairs // 2)
    this_half = 1 - own_half if second else own_half
    blocks = main * members + rest
    main_rows = size // pairs
    rest_rows = main_rows // pack
    for ref, (d, s, other) in zip(piece_refs, layout):
        owner = member ^ d
        side = 1 - core if other else core
        piece = lax.rem(2 * (pair ^ s) + side, pairs)
        row = 0
        for k in range(main):
            spot = pl.ds(pl.multiple_of(piece * main_rows, ROWS), main_rows)
            all_s[k * members + owner, spot, :] = ref[0, row : row + main_rows, :].astype(
                jnp.float32
            )
            row += main_rows
        spot = pl.ds(pl.multiple_of(piece * rest_rows, ROWS), rest_rows)
        packed_s[owner, spot, :] = ref[0, row : row + rest_rows, :].astype(jnp.float32)
    short = size // pack
    lane = lax.broadcasted_iota(jnp.int32, (1, LANES), 1)
    for k in range(rest):
        for g in range(pack):
            tile = None
            for owner in range(members):
                shift = (owner * sub - g * valid - k * sub) % LANES
                value = packed_s[owner]
                if shift:
                    value = pltpu.roll(value, shift, 1)
                tile = value if tile is None else jnp.where(lane >= owner * sub, value, tile)
            all_s[main * members + k, g * short : (g + 1) * short, :] = tile
    source = all_s if main else packed_s
    lines = source[0, special : special + SPECIAL, :]
    lines = jnp.concatenate(
        [lines, jnp.zeros((LANES - SPECIAL, LANES), jnp.float32)], axis=0
    )
    columns = jnp.transpose(lines)
    copies = []
    for i in range(per_half):
        for k in range(blocks):
            stage_s[i, :, k * LANES : (k + 1) * LANES] = all_s[
                k, i * padded_out : i * padded_out + out_chan, :
            ]
        for e in range(extras):
            stage_s[i, :, blocks * LANES + e : blocks * LANES + e + 1] = columns[
                :out_chan, i * extras + e : i * extras + e + 1
            ]
        copy = pltpu.make_async_copy(
            stage_s.at[i], out_ref.at[this_half * per_half + i], sems.at[i]
        )
        copy.start()
        copies.append(copy)
    if not second:
        carry_ref[:, : size - special, :] = all_s[:, special:size, :]
        if not main:
            carry_ref[0, :SPECIAL, :] = lines[:SPECIAL]
    else:
        low = this_half == 0
        split = size - special - SPECIAL
        begin = special + SPECIAL
        for k in range(blocks):
            here = all_s[k, begin:size, :]
            there = carry_ref[k, SPECIAL : SPECIAL + split, :]
            top = jnp.where(low, here, there)
            bottom = jnp.where(low, there, here)
            lanes = slice(k * LANES, (k + 1) * LANES)
            stage_s[per_half, :split, lanes] = top
            stage_s[per_half, split:, lanes] = bottom[: out_chan - split]
        final = jnp.where(low, carry_ref[0, :SPECIAL, :], lines[:SPECIAL])
        final_columns = jnp.transpose(
            jnp.concatenate(
                [final, jnp.zeros((LANES - SPECIAL, LANES), jnp.float32)], axis=0
            )
        )
        for e in range(extras):
            line = per_half * extras + e
            stage_s[per_half, :, blocks * LANES + e : blocks * LANES + e + 1] = final_columns[
                :out_chan, line : line + 1
            ]
        copy = pltpu.make_async_copy(
            stage_s.at[per_half], out_ref.at[2 * per_half], sems.at[per_half]
        )
        copy.start()
        copies.append(copy)
        line = plan["bias_row"]
        bias_ref[...] = (final[line : line + 1] + final[line + 1 : line + 2])[:, :out_chan]
    for copy in copies:
        copy.wait()


def body(fields, weight, out_bias, observed, widths, owner_start):
    _, in_chan, rows_in, lon_dev = fields.shape
    taps, _, out_chan, _ = weight.shape
    half = taps // 2
    halo = 2 * half
    members = lax.axis_size("member")
    lon_count = lax.axis_size("lon")
    pairs = lon_count // 2
    rows_out = rows_in - taps + 1
    offset = round_up(halo, ROWS)
    slots = round_up(offset + lon_dev + halo, 2 * ROWS)
    points = rows_out * slots
    padded_out = round_up(out_chan, 2 * ROWS)
    full_blocks = in_chan // LANES
    main, rest = full_blocks // members, full_blocks % members
    sub = LANES // members
    valid = rest * sub
    pack = LANES // valid if rows_in % (LANES // valid) == 0 else 1
    extras = in_chan - full_blocks * LANES
    stack = taps * padded_out
    total_taps = taps * taps
    per_half = total_taps // 2
    special = per_half * padded_out
    half_rows = round_up(
        special + SPECIAL + round_up(-(-out_chan // 2), ROWS), ROWS * pack * pairs
    )
    bias_row = (per_half + 1) * extras
    assert rest and total_taps % 2 and bias_row + 2 <= SPECIAL
    wide = round_up(in_chan, LANES)
    plan = dict(
        members=members, taps=taps, half=half, offset=offset, lon_dev=lon_dev, out_chan=out_chan,
        padded_out=padded_out, rows_out=rows_out, points=points, main=main, rest=rest, pairs=pairs,
        pack=pack, valid=valid, sub=sub, extras=extras, half_rows=half_rows, per_half=per_half,
        special=special, bias_row=bias_row,
        special_row=special - (pairs - 1) * (half_rows // pairs),
    )
    own_member = lax.axis_index("member")
    own_lon = lax.axis_index("lon")
    place = jnp.stack([own_member, own_lon // 2, own_lon % 2]).astype(jnp.int32)
    factor = 1.0 / math.sqrt(members * rows_out * lon_dev * lon_count)
    even = own_lon % 2 == 0

    def swap_lon(value, d):
        return lax.ppermute(value, "lon", [(i, i ^ d) for i in range(lon_count)])

    def swap_far(value):
        step = [(i, (i + 1 if i % 2 else i - 1) % lon_count) for i in range(lon_count)]
        return lax.ppermute(value, "lon", step)

    def swap_member(value, d):
        return lax.ppermute(value, "member", [(i, i ^ d) for i in range(members)])

    field = jnp.transpose(fields[0], (1, 2, 0))
    start_edge = field[:, :halo, :]
    end_edge = field[:, lon_dev - halo :, :]
    far = swap_far(jnp.where(even, start_edge, end_edge))
    near = swap_lon(jnp.where(even, end_edge, start_edge), 1)

    packed_rows = main * rows_in + rows_in // pack + 1
    packed = pl.pallas_call(
        functools.partial(pack_kernel, plan),
        out_shape=[jax.ShapeDtypeStruct((packed_rows, lon_dev, LANES), jnp.bfloat16)] * members,
        in_specs=[smem(), vmem()],
        out_specs=[vmem()] * members,
        cost_estimate=cost(0, 3_000_000),
        compiler_params=limit(16),
        name="pack",
    )(place, field)
    traded = [packed[0]] + [swap_member(packed[d], d) for d in range(1, members)]

    own_outputs = pl.pallas_call(
        functools.partial(forward_kernel, plan),
        out_shape=jax.ShapeDtypeStruct((padded_out, points), jnp.bfloat16),
        in_specs=[smem()] + [vmem()] * 5,
        out_specs=vmem(),
        scratch_shapes=[
            pltpu.VMEM((rows_in, slots, wide), jnp.bfloat16),
            pltpu.VMEM((total_taps, padded_out, wide), jnp.bfloat16),
            pltpu.VMEM((stack, points), jnp.float32),
        ],
        cost_estimate=cost(2 * taps * stack * points * wide, 6_000_000),
        compiler_params=limit(24),
        name="forward",
    )(place, field, near, far, weight.reshape(total_taps, out_chan, in_chan), out_bias[None, :])
    outputs = [own_outputs] + [swap_member(own_outputs, d) for d in range(1, members)]

    traded, observed, widths, _ = lax.optimization_barrier(
        (traded, observed, widths, own_outputs)
    )
    start_edge = observed[:, :, :half]
    end_edge = observed[:, :, lon_dev - half :]
    far = swap_far(jnp.where(even, start_edge, end_edge))
    near = swap_lon(jnp.where(even, end_edge, start_edge), 1)
    truth = jnp.pad(
        jnp.concatenate(
            [jnp.where(even, far, near), observed, jnp.where(even, near, far)], axis=2
        ),
        (
            (0, padded_out - out_chan),
            (0, 0),
            (offset - half, slots - offset - lon_dev - half),
        ),
    ).reshape(padded_out, points)
    tiles = main + 1
    x_all = pl.pallas_call(
        functools.partial(traded_kernel, plan),
        out_shape=jax.ShapeDtypeStruct((members, rows_in, slots, tiles * LANES), jnp.bfloat16),
        in_specs=[vmem()] * members,
        out_specs=vmem(),
        cost_estimate=cost(0, 4_000_000),
        compiler_params=limit(24),
        name="traded",
    )(*traded)

    main_rows = half_rows // pairs
    piece_rows = main * main_rows + main_rows // pack
    piece = jax.ShapeDtypeStruct((1, piece_rows, LANES), jnp.bfloat16)
    grad_own, score, send, keep = pl.pallas_call(
        functools.partial(gradient_kernel, plan),
        out_shape=(
            jax.ShapeDtypeStruct((padded_out, points), jnp.bfloat16),
            jax.ShapeDtypeStruct((1, points), jnp.float32),
            jax.ShapeDtypeStruct((pairs, piece_rows, LANES), jnp.bfloat16),
            jax.ShapeDtypeStruct((pairs, piece_rows, LANES), jnp.float32),
        ),
        in_specs=[smem()] + [vmem()] * (members + 3),
        out_specs=[vmem()] * 4,
        scratch_shapes=[
            pltpu.VMEM((members, padded_out, points), jnp.bfloat16),
            pltpu.VMEM((members, stack, points), jnp.bfloat16),
            pltpu.VMEM((tiles, 2 * half_rows, LANES), jnp.float32),
            pltpu.VMEM((2 * half_rows // pack, LANES), jnp.float32),
        ],
        cost_estimate=cost(
            2 * taps * stack * points * members * tiles * LANES, 6_000_000, 1_000_000
        ),
        compiler_params=limit(32),
        name="gradient",
    )(place, *outputs, x_all, truth, widths[None, :])

    mine, *out_pieces = pl.pallas_call(
        functools.partial(core_add_kernel, plan),
        out_shape=[jax.ShapeDtypeStruct((piece_rows, LANES), jnp.float32)] + [piece] * (pairs - 1),
        in_specs=[smem(), vmem(), vmem()],
        out_specs=[vmem()] * pairs,
        cost_estimate=cost(0, 1_500_000),
        compiler_params=limit(16),
        name="core_add",
    )(place, keep, swap_lon(send, 1))
    got = [swap_lon(value, 2 * s) for s, value in enumerate(out_pieces, 1)]
    final = pl.pallas_call(
        functools.partial(pair_add_kernel, plan, factor),
        out_shape=piece,
        in_specs=[smem()] + [vmem()] * pairs,
        out_specs=vmem(),
        cost_estimate=cost(0, 600_000),
        compiler_params=limit(16),
        name="pair_add",
    )(place, mine, *got)

    gathered = [final] + [swap_lon(final, 2 * s) for s in range(1, pairs)]
    grad_shape = jax.ShapeDtypeStruct((total_taps, out_chan, in_chan), jnp.float32)
    blocks = full_blocks
    tail_rows = half_rows - special
    weight_grad = carry = None
    any_space = pl.BlockSpec(memory_space=pl.ANY)
    for second in range(2):
        group = range(second * pairs // 2, (second + 1) * pairs // 2)
        column = jnp.concatenate([gathered[s] for s in group])
        got = {0: column}
        for d in range(1, members):
            if members == 4 and d == 3:
                via = 1 + second
                got[d] = swap_member(got[via], 3 - via)
            else:
                got[d] = swap_member(column, d)
        held, layout = [], []
        for d in range(members):
            both = (got[d], swap_lon(got[d], 1))
            for other, value in enumerate(both):
                for at, s in enumerate(group):
                    held.append((value, at))
                    layout.append((d, s, bool(other)))
        arrays = [value for value, at in held if at == 0]
        inputs = [place] + arrays
        specs = [smem()] + [vmem()] * len(arrays)
        if second:
            aliases = {len(inputs): 0}
            inputs += [weight_grad, carry]
            specs += [any_space, vmem()]
            shapes = [grad_shape, jax.ShapeDtypeStruct((1, out_chan), jnp.float32)]
        else:
            aliases = {}
            shapes = [grad_shape, jax.ShapeDtypeStruct((blocks, tail_rows, LANES), jnp.float32)]
        slots_held = per_half + second

        def kernel(*refs, second=second, layout=tuple(layout), count=len(arrays), each=len(group)):
            pieces = [ref.at[pl.ds(at, 1)] for ref in refs[1 : 1 + count] for at in range(each)]
            assemble_kernel(plan, second, layout, refs[0], *pieces, *refs[1 + count :])

        weight_grad, other_out = pl.pallas_call(
            kernel,
            out_shape=shapes,
            in_specs=specs,
            out_specs=[any_space, vmem()],
            scratch_shapes=[
                pltpu.VMEM((blocks, half_rows, LANES), jnp.float32),
                pltpu.VMEM((members, half_rows // pack, LANES), jnp.float32),
                pltpu.VMEM((slots_held, out_chan, in_chan), jnp.float32),
                pltpu.SemaphoreType.DMA((slots_held,)),
            ],
            input_output_aliases=aliases,
            cost_estimate=cost(0, 5_000_000),
            compiler_params=limit(24),
            name="assemble",
        )(*inputs)
        carry = other_out
    bias_grad = carry[0]
    weight_grad = weight_grad.reshape(taps, taps, out_chan, in_chan)

    out_grad = grad_own[:out_chan].reshape(1, out_chan, rows_out, slots)[
        :, :, :, offset : offset + lon_dev
    ]
    point_blocks = score.reshape(rows_out, slots)[:, offset : offset + lon_dev].reshape(-1, BLOCK)
    count = point_blocks.shape[0]
    capacity = max(2, 3 * count // members)
    starts = owner_start[0]
    first = lax.dynamic_slice_in_dim(starts, own_member, 1)[0]
    owned = lax.dynamic_slice_in_dim(starts, own_member + 1, 1)[0] - first
    window = lax.dynamic_slice_in_dim(
        jnp.pad(point_blocks, ((0, capacity), (0, 0))), first, capacity, 0
    )
    slot_index = jnp.arange(capacity, dtype=jnp.int32)
    owned_score = jnp.where((slot_index < owned)[:, None], window, 0.0).reshape(1, 1, -1)
    return (out_grad, owned_score, weight_grad, bias_grad)


def solution(mesh):
    in_specs = (P("member", None, None, "lon"), P(), P(), P(None, None, "lon"), P(), P("lon", None))
    out_specs = (P("member", None, None, "lon"), P("lon", "member", None), P(), P())
    return jax.shard_map(body, mesh=mesh, in_specs=in_specs, out_specs=out_specs, check_vma=False)
```

```python
import functools
import math
import types

import jax
import jax.numpy as jnp
from jax import lax
from jax.experimental import pallas as pl
from jax.experimental.pallas import tpu as pltpu
from jax.sharding import PartitionSpec as P


BLOCK = 45
LANES = 128
ROWS = 8
SPECIAL = 16


NT = (((1,), (1,)), ((), ()))
NN = (((1,), (0,)), ((), ()))


def round_up(value, unit):
    return -(-value // unit) * unit


def vmem():
    return pl.BlockSpec(memory_space=pltpu.VMEM)


def smem():
    return pl.BlockSpec(memory_space=pltpu.SMEM)


def limit(mib):
    return pltpu.CompilerParams(vmem_limit_bytes=mib << 20)


def here():
    lon = lax.axis_index("lon")
    return lax.axis_index("member"), lax.div(lon, 2), lax.rem(lon, 2)


def cost(flops, moved, special=0):
    return pl.CostEstimate(flops=flops, bytes_accessed=moved, transcendentals=special)


def column_of(row_ref, fill):
    count = row_ref.shape[1]
    row = jnp.concatenate(
        [row_ref[...], jnp.full((1, LANES - count), fill, jnp.float32)], axis=1
    )
    return jnp.transpose(jnp.broadcast_to(row, (LANES, LANES)))[:, :1]


def pack_kernel(plan, f_ref, near_ref, far_ref, *out_refs):
    members, main, rest = plan.members, plan.main, plan.rest
    pack, valid, sub = plan.pack, plan.valid, plan.sub
    rows_in, lon_dev, in_chan = f_ref.shape
    place_ref = here()
    halo = 2 * plan.half
    even = place_ref[2] == 0
    start_edge = f_ref[:, :halo, :].astype(jnp.float32)
    final = (lon_dev - halo) // ROWS * ROWS
    end_edge = f_ref[:, final:, :].astype(jnp.float32)[:, lon_dev - halo - final :]
    far_ref[...] = jnp.where(even, start_edge, end_edge).astype(far_ref.dtype)
    near_ref[...] = jnp.where(even, end_edge, start_edge).astype(near_ref.dtype)
    group = rows_in // pack
    base = main * members
    lane = lax.broadcasted_iota(jnp.int32, (1, 1, LANES), 2)
    full = (base + rest) * LANES
    slab = jnp.zeros((1, lon_dev, LANES), jnp.float32)
    for e in range(in_chan - full):
        for r in range(rows_in):
            value = f_ref[r : r + 1, :, full + e : full + e + 1].astype(jnp.float32)
            slab = jnp.where(lane == e * rows_in + r, value, slab)
    for d in range(members):
        owner = place_ref[0] ^ d
        out = out_refs[d]
        for k in range(main):
            spot = pl.ds(pl.multiple_of((k * members + owner) * LANES, LANES), LANES)
            out[k * rows_in : (k + 1) * rows_in] = f_ref[:, :, spot]
        for i in range(group):
            row = None
            for g in range(pack):
                for k in range(rest):
                    tile = f_ref[
                        g * group + i, :, (base + k) * LANES : (base + k + 1) * LANES
                    ].astype(jnp.float32)
                    start = g * valid + k * sub
                    moved = pltpu.roll(tile, lax.rem(start - owner * sub + LANES, LANES), 1)
                    row = moved if row is None else jnp.where(lane[0] >= start, moved, row)
            out[main * rows_in + i] = row.astype(out.dtype)
        out[main * rows_in + group] = slab[0].astype(out.dtype)


def forward_kernel(
    plan, field_ref, near_ref, far_ref, weight_ref, b_ref, o_ref,
    f_s, raw_s, x_s, w_s, acc_s, sems,
):
    taps, half, offset = plan.taps, plan.half, plan.offset
    lon_dev, halo = plan.lon_dev, 2 * plan.half
    rows_in, slots, wide = x_s.shape
    out_chan, in_chan = plan.out_chan, near_ref.shape[2]
    padded_out = w_s.shape[1]
    rows_out = rows_in - taps + 1
    points = rows_out * slots
    bulk = lon_dev // ROWS * ROWS
    full = in_chan // LANES * LANES
    field_copies = []
    for part in range(2):
        span = pl.ds(part * (rows_in // 2), rows_in // 2)
        copy = pltpu.make_async_copy(field_ref.at[span], f_s.at[span], sems.at[taps + part])
        copy.start()
        field_copies.append(copy)
    weight_copies = []
    for a in range(taps):
        span = pl.ds(a * taps, taps)
        copy = pltpu.make_async_copy(weight_ref.at[span], raw_s.at[span], sems.at[a])
        weight_copies.append(copy)
    weight_copies[0].start()
    x_s[:, :, full:] = jnp.zeros((rows_in, slots, wide - full), x_s.dtype)
    w_s[:, :, full:] = jnp.zeros((taps * taps, padded_out, wide - full), w_s.dtype)
    for copy in field_copies:
        copy.wait()
    for copy in weight_copies[1:]:
        copy.start()
    x_s[:, offset : offset + bulk, :in_chan] = f_s[:, :bulk, :]
    near = near_ref[...].astype(jnp.float32)
    far = far_ref[...].astype(jnp.float32)
    even = here()[2] == 0
    first = jnp.concatenate(
        [
            jnp.zeros((rows_in, offset - halo, in_chan), jnp.float32),
            jnp.where(even, far, near),
        ],
        axis=1,
    )
    x_s[:, :offset, :in_chan] = first.astype(x_s.dtype)
    tail = slots - offset - bulk
    final = jnp.concatenate(
        [
            f_s[:, bulk:, :].astype(jnp.float32),
            jnp.where(even, near, far),
            jnp.zeros((rows_in, tail - (lon_dev - bulk) - halo, in_chan), jnp.float32),
        ],
        axis=1,
    )
    x_s[:, offset + bulk :, :in_chan] = final.astype(x_s.dtype)
    for a in range(taps):
        weight_copies[a].wait()
        mine = slice(a * taps, (a + 1) * taps)
        w_s[mine, :out_chan, :in_chan] = raw_s[mine]
        part = lax.dot_general(
            w_s[a * taps : (a + 1) * taps].reshape(taps * padded_out, wide),
            x_s[a : a + rows_out].reshape(points, wide),
            NT,
            preferred_element_type=jnp.float32,
        )
        if a == 0:
            acc_s[...] = part
        else:
            acc_s[...] += part
    slot = lax.broadcasted_iota(jnp.int32, (1, points), 1) % slots
    inside = (slot >= offset - half) & (slot < offset + lon_dev + half)
    bias = column_of(b_ref, 0.0)
    for lo in range(0, padded_out, 2 * ROWS):
        rows = slice(lo, lo + 2 * ROWS)
        total = jnp.zeros((2 * ROWS, points), jnp.float32) + bias[rows]
        for b in range(taps):
            piece = acc_s[b * padded_out + lo : b * padded_out + lo + 2 * ROWS, :]
            shift = (half - b) % points
            total = total + (pltpu.roll(piece, shift, 1) if shift else piece)
        row = lo + lax.broadcasted_iota(jnp.int32, (2 * ROWS, 1), 0)
        keep = inside & (row < out_chan)
        o_ref[rows, :] = jnp.where(keep, total, 0.0).astype(o_ref.dtype)


def prep_kernel(plan, obs_ref, near_ref, far_ref, *refs):
    truth_ref, row_s = refs[-2:]
    refs = refs[:-2]
    half, offset, padded_out = plan.half, plan.offset, plan.padded_out
    even = here()[2] == 0
    near, far = near_ref[...], far_ref[...]
    out_chan = obs_ref.shape[2]
    total_rows = obs_ref.shape[1]
    width = plan.points // total_rows
    per = LANES // width
    row_s[...] = jnp.zeros(row_s.shape, jnp.float32)
    for x in range(half):
        row_s[:, offset - half + x, :out_chan] = jnp.where(even, far[x], near[x])
        row_s[:, offset + plan.lon_dev + x, :out_chan] = jnp.where(even, near[x], far[x])
    for x in range(plan.lon_dev):
        row_s[:, offset + x, :out_chan] = obs_ref[x]
    for j in range(total_rows // per):
        tile = row_s[j * per : (j + 1) * per].reshape(LANES, LANES)
        truth_ref[:, j * LANES : (j + 1) * LANES] = jnp.transpose(tile)[:padded_out]
    members, main = plan.members, plan.main
    pack, valid, extras = plan.pack, plan.valid, plan.extras
    out_ref = refs[-1]
    _, rows_in, slots, _ = out_ref.shape
    lon_dev = plan.lon_dev
    bulk = lon_dev // ROWS * ROWS
    group = rows_in // pack
    lane = lax.broadcasted_iota(jnp.int32, (1, LANES), 1)
    out_ref[:, :, bulk:, :] = jnp.zeros(
        (members, rows_in, slots - bulk, out_ref.shape[3]), out_ref.dtype
    )
    for d in range(members):
        ref = refs[d]
        for k in range(main):
            out_ref[d, :, :lon_dev, k * LANES : (k + 1) * LANES] = ref[
                k * rows_in : (k + 1) * rows_in
            ]
        slab = ref[main * rows_in + group].astype(jnp.float32)
        for g in range(pack):
            for i in range(group):
                value = ref[main * rows_in + i].astype(jnp.float32)
                if g:
                    value = pltpu.roll(value, LANES - g * valid, 1)
                r = g * group + i
                for e in range(extras):
                    shift = (valid + e - (e * rows_in + r)) % LANES
                    moved = pltpu.roll(slab, shift, 1) if shift else slab
                    value = jnp.where(lane == valid + e, moved, value)
                value = jnp.where(lane == valid + extras, 1.0, value)
                out_ref[d, r, :lon_dev, main * LANES :] = value.astype(out_ref.dtype)


def split_bias(tile, row_high):
    row = lax.broadcasted_iota(jnp.int32, tile.shape, 0)
    size = tile.shape[0]
    total = jnp.where(row == row_high, tile + pltpu.roll(tile, size - 1, 0), tile)
    left = total - total.astype(jnp.bfloat16).astype(jnp.float32)
    return jnp.where(row == row_high + 1, pltpu.roll(left, 1, 0), total)


def fix_rows(plan, ref, index, piece, value_of):
    @pl.when(piece == 2 * plan.pairs - 1)
    def _():
        lo = plan.special_row
        tile = value_of(lo, lo + SPECIAL)
        ref[index, lo : lo + SPECIAL, :] = split_bias(tile, plan.bias_row).astype(ref.dtype)


def gradient_kernel(plan, *refs):
    members, taps, half = plan.members, plan.taps, plan.half
    out_chan, padded_out, points = plan.out_chan, plan.padded_out, plan.points
    main, pairs, pack, valid = plan.main, plan.pairs, plan.pack, plan.valid
    rows_out, size, extras = plan.rows_out, plan.half_rows, plan.extras
    per_half, special = plan.per_half, plan.special
    place_ref = here()
    y_refs = refs[:members]
    x_ref, obs_ref, wid_ref = refs[members : 3 + members]
    g_ref, score_ref, send_ref, keep_ref = refs[3 + members : 7 + members]
    g_s, gs_s, wide_s, packed_s = refs[7 + members :]
    step = 2 * LANES
    width_all = column_of(wid_ref, 1.0)
    for left in range(0, points, step):
        tally = jnp.zeros((ROWS, step), jnp.float32)
        for lo in range(0, padded_out, 2 * ROWS):
            rows = slice(lo, lo + 2 * ROWS)
            cols = slice(left, left + step)
            shape = (2 * ROWS, step)
            width = width_all[rows]
            inverse = 1.0 / (width * width)
            values = [y[rows, cols].astype(jnp.float32) for y in y_refs]
            target = obs_ref[rows, cols]
            pair_sum = jnp.full(shape, float(members), jnp.float32)
            pull = [jnp.zeros(shape, jnp.float32) for _ in values]
            for x in range(members):
                for y in range(x + 1, members):
                    spread = values[x] - values[y]
                    kernel_pair = jnp.exp(-0.5 * spread * spread * inverse)
                    pair_sum = pair_sum + 2.0 * kernel_pair
                    weighted = kernel_pair * spread
                    pull[x] = pull[x] + weighted
                    pull[y] = pull[y] - weighted
            obs_sum = jnp.zeros(shape, jnp.float32)
            for x in range(members):
                misfit = values[x] - target
                kernel_obs = jnp.exp(-0.5 * misfit * misfit * inverse)
                obs_sum = obs_sum + kernel_obs
                grad = inverse * (misfit * kernel_obs - pull[x] / members)
                g_s[x, rows, cols] = grad.astype(jnp.bfloat16)
            terms = pair_sum / (2.0 * members * members) - obs_sum / members
            row = lo + lax.broadcasted_iota(jnp.int32, (2 * ROWS, 1), 0)
            terms = jnp.where(row < out_chan, terms, 0.0)
            tally = tally + terms[:ROWS] + terms[ROWS:]
        score_ref[:, left : left + step] = jnp.sum(tally, axis=0, keepdims=True) / out_chan
    g_ref[...] = g_s[0]
    for x in range(members):
        for lo in range(0, padded_out, 2 * ROWS):
            grad = g_s[x, lo : lo + 2 * ROWS, :].astype(jnp.float32)
            for b in range(taps):
                shift = (b - half - plan.offset) % points
                moved = pltpu.roll(grad, shift, 1) if shift else grad
                start = b * padded_out + lo
                gs_s[x, start : start + 2 * ROWS, :] = moved.astype(jnp.bfloat16)
    tiles = main + 1
    split = size - special - SPECIAL
    for h in range(2):
        wide_s[:, h * size + special : (h + 1) * size, :] = jnp.zeros(
            (tiles, size - special, LANES), jnp.float32
        )
    for a in range(taps):
        total = None
        for x in range(members):
            part = lax.dot_general(
                gs_s[x],
                x_ref[x, a : a + rows_out].reshape(points, tiles * LANES),
                NN,
                preferred_element_type=jnp.float32,
            )
            total = part if total is None else total + part
        for b in range(taps):
            tap = a * taps + b
            block = total[b * padded_out : (b + 1) * padded_out]
            across = jnp.transpose(block[:, main * LANES :])
            if tap < 2 * per_half:
                h, i = tap // per_half, tap % per_half
                spans = [(0, padded_out, h * size + i * padded_out)]
                line = h * size + special + i * extras
            else:
                first = size - split
                spans = [(0, split, first), (split, padded_out, size + first)]
                line = size + special + per_half * extras
            for k in range(tiles):
                for lo, hi, at in spans:
                    wide_s[k, at : at + hi - lo, :] = block[lo:hi, k * LANES : (k + 1) * LANES]
            for e in range(extras):
                wide_s[0, line + e : line + e + 1, :padded_out] = across[valid + e : valid + e + 1]
            if a == 0 and b == half:
                line = size + special + plan.bias_row
                ones = valid + extras
                wide_s[0, line : line + 1, :padded_out] = across[ones : ones + 1]
    short = size // pack
    lane = lax.broadcasted_iota(jnp.int32, (1, LANES), 1)
    for h in range(2):
        packed = wide_s[main, h * size : h * size + short, :]
        for g in range(1, pack):
            at = h * size + g * short
            moved = pltpu.roll(wide_s[main, at : at + short, :], g * valid, 1)
            packed = jnp.where(lane >= g * valid, moved, packed)
        packed_s[h * short : (h + 1) * short, :] = packed
    pair, core = place_ref[1], place_ref[2]
    main_rows = size // pairs
    rest_rows = main_rows // pack
    for s in range(pairs):
        for out, side in ((keep_ref, core), (send_ref, 1 - core)):
            piece = 2 * (pair ^ s) + side
            at = 0
            for k in range(main):
                source = pl.ds(pl.multiple_of(piece * main_rows, main_rows), main_rows)
                out[s, at : at + main_rows, :] = wide_s[k, source, :].astype(out.dtype)
                at += main_rows
            source = pl.ds(pl.multiple_of(piece * rest_rows, rest_rows), rest_rows)
            out[s, at : at + rest_rows, :] = packed_s[source, :].astype(out.dtype)
        spot = 2 * size - main_rows
        fix_rows(
            plan, send_ref, s, 2 * (pair ^ s) + 1 - core,
            lambda lo, hi: wide_s[0, spot + lo : spot + hi, :]
            if main
            else packed_s[spot + lo : spot + hi, :],
        )


def core_add_kernel(plan, keep_ref, got_ref, mine_ref, *out_refs):
    place_ref = here()
    mine_ref[...] = keep_ref[0] + got_ref[0].astype(jnp.float32)
    pair, core = place_ref[1], place_ref[2]
    for s in range(1, plan.pairs):
        out = out_refs[s - 1]
        out[0] = (keep_ref[s] + got_ref[s].astype(jnp.float32)).astype(out.dtype)
        fix_rows(
            plan, out, 0, 2 * (pair ^ s) + core,
            lambda lo, hi: keep_ref[s, lo:hi, :] + got_ref[s, lo:hi, :].astype(jnp.float32),
        )


def pair_add_kernel(plan, factor, mine_ref, *refs):
    place_ref = here()
    out = refs[-1]

    def value(lo, hi):
        total = mine_ref[lo:hi, :]
        for ref in refs[:-1]:
            total = total + ref[0, lo:hi, :].astype(jnp.float32)
        return total * factor

    out[0] = value(0, mine_ref.shape[0]).astype(out.dtype)
    fix_rows(plan, out, 0, 2 * place_ref[1] + place_ref[2], value)


def out_grad_kernel(plan, g_ref, out_ref, row_s):
    lon_dev, offset = plan.lon_dev, plan.offset
    rows_out, out_chan = out_ref.shape[1:]
    width = plan.points // rows_out
    per = LANES // width
    padded_out = g_ref.shape[0]
    for j in range(rows_out // per):
        tile = g_ref[:, j * LANES : (j + 1) * LANES].astype(jnp.float32)
        tile = jnp.concatenate(
            [tile, jnp.zeros((LANES - padded_out, LANES), jnp.float32)], axis=0
        )
        row_s[j * per : (j + 1) * per] = jnp.transpose(tile).reshape(per, width, LANES)
    for x in range(lon_dev):
        out_ref[x] = row_s[:, offset + x, :out_chan].astype(out_ref.dtype)


def owned_kernel(plan, start_ref, score_ref, out_ref, row_s):
    lon_dev, offset, points = plan.lon_dev, plan.offset, plan.points
    rows_out = plan.rows_out
    width = points // rows_out
    capacity = out_ref.shape[1] // lon_dev
    member = here()[0]
    first = start_ref[0, member]
    count = start_ref[0, member + 1] - first
    lane = lax.broadcasted_iota(jnp.int32, (1, points), 1)
    row_s[...] = jnp.zeros(row_s.shape, jnp.float32)
    score = score_ref[...]
    for i in range(rows_out):
        moved = pltpu.roll(score, (points - i * width - offset) % points, 1)
        row_s[i : i + 1, :] = jnp.where(lane < lon_dev, moved, 0.0)[:, :LANES]
    reach = round_up(capacity * lon_dev, LANES)
    total = jnp.zeros((1, reach), jnp.float32)
    blank = jnp.zeros((1, reach - LANES), jnp.float32)
    for t in range(capacity):
        row = jnp.where(t < count, row_s[pl.ds(first + t, 1), :], 0.0)
        row = jnp.concatenate([row, blank], axis=1)
        total = total + (pltpu.roll(row, t * lon_dev, 1) if t else row)
    out_ref[...] = total[:, : capacity * lon_dev]


def assemble_kernel(plan, second, layout, final, *refs):
    members, main, rest = plan.members, plan.main, plan.rest
    out_chan, padded_out, pairs = plan.out_chan, plan.padded_out, plan.pairs
    pack, valid, sub = plan.pack, plan.valid, plan.sub
    size, extras, per_half = plan.half_rows, plan.extras, plan.per_half
    special = plan.special
    member, pair, core = here()
    piece_refs = refs[: len(layout)]
    refs = refs[len(layout) :]
    own_half = lax.div(pair, pairs // 2)
    this_half = 1 - own_half if second else own_half
    low = this_half == 0
    main_rows = size // pairs
    rest_rows = main_rows // pack
    split = size - special - SPECIAL
    begin = special + SPECIAL
    known_ref = carry_ref = None
    if second:
        carry_ref, _, *refs = refs
        if final == "late":
            known_ref, *refs = refs
    out_ref, other_ref, main_s, packed_s, main_stage, rest_stage, sems = refs
    if known_ref is not None:
        packed_s[...] = known_ref[:members]
    shown = []
    for d, _, _ in layout:
        if d not in shown:
            shown.append(d)
    for ref, (d, s, other) in zip(piece_refs, layout):
        side = 1 - core if other else core
        piece = lax.rem(2 * (pair ^ s) + side, pairs)
        row = 0
        for k in range(main):
            spot = pl.ds(pl.multiple_of(piece * main_rows, ROWS), main_rows)
            main_s[shown.index(d) * main + k, spot, :] = ref[0, row : row + main_rows, :].astype(
                jnp.float32
            )
            row += main_rows
        spot = pl.ds(pl.multiple_of(piece * rest_rows, ROWS), rest_rows)
        packed_s[member ^ d, spot, :] = ref[0, row : row + rest_rows, :].astype(jnp.float32)
    lines = packed_s[0, special:begin, :] if not main else None
    for at, d in enumerate(shown if main else ()):
        found = main_s[at * main, special:begin, :]
        if lines is None:
            lines = found if known_ref is None else known_ref[members, :SPECIAL, :]
        lines = jnp.where(member == d, found, lines)
    copies = []

    def emit(source, stage, lanes):
        spans = [(pl.ds(0, per_half), pl.ds(this_half * per_half, per_half))]
        if second:
            spans.append((pl.ds(per_half, 1), pl.ds(2 * per_half, 1)))
        for from_span, to_span in spans:
            copy = pltpu.make_async_copy(
                source.at[stage, from_span],
                out_ref.at[to_span, :, lanes],
                sems.at[len(copies)],
            )
            copy.start()
            copies.append(copy)

    def fill(stage_ref, stage, lanes, tile, block):
        for i in range(per_half):
            stage_ref[stage, i, :, lanes] = tile[i * padded_out : i * padded_out + out_chan]
        mine = tile[begin:size]
        if second:
            theirs = carry_ref[block, SPECIAL:, :]
            stage_ref[stage, per_half, :split, lanes] = jnp.where(low, mine, theirs)
            stage_ref[stage, per_half, split:, lanes] = jnp.where(low, theirs, mine)[
                : out_chan - split
            ]
        else:
            other_ref[block, SPECIAL:, :] = mine

    if not second:
        other_ref[:, :SPECIAL, :] = jnp.zeros(
            (other_ref.shape[0], SPECIAL, LANES), jnp.float32
        )
        other_ref[0, :SPECIAL, :] = lines
    for at, d in enumerate(shown if main else ()):
        for k in range(main):
            block = k * members + (member ^ d)
            fill(main_stage, at * main + k, slice(None), main_s[at * main + k], block)
            emit(
                main_stage,
                at * main + k,
                pl.ds(pl.multiple_of(block * LANES, LANES), LANES),
            )
    if final == "early":
        other_ref[:members] = packed_s[...]
        other_ref[members] = jnp.zeros(other_ref.shape[1:], jnp.float32)
        other_ref[members, :SPECIAL, :] = lines
    else:
        lane = lax.broadcasted_iota(jnp.int32, (1, LANES), 1)
        base = main * members
        for k in range(rest):
            tiles = []
            for g in range(pack):
                tile = None
                for owner in range(members):
                    shift = (owner * sub - g * valid - k * sub) % LANES
                    value = packed_s[owner]
                    if shift:
                        value = pltpu.roll(value, shift, 1)
                    tile = (
                        value if tile is None else jnp.where(lane >= owner * sub, value, tile)
                    )
                tiles.append(tile)
            tile = tiles[0] if pack == 1 else jnp.concatenate(tiles, axis=0)
            fill(rest_stage, 0, slice(k * LANES, (k + 1) * LANES), tile, base + k)
        blank = jnp.zeros((LANES - SPECIAL, LANES), jnp.float32)

        def put_columns(rows, first, count, tap):
            columns = jnp.transpose(jnp.concatenate([rows, blank], axis=0))
            for i in range(count):
                for e in range(extras):
                    at = first + i * extras + e
                    lanes = slice(rest * LANES + e, rest * LANES + e + 1)
                    rest_stage[0, tap + i, :, lanes] = columns[:out_chan, at : at + 1]

        put_columns(lines, 0, per_half, 0)
        if second:
            top = jnp.where(low, carry_ref[0, :SPECIAL, :], lines)
            put_columns(top, per_half * extras, 1, per_half)
            line = plan.bias_row
            other_ref[...] = (top[line : line + 1] + top[line + 1 : line + 2])[:, :out_chan]
        emit(rest_stage, 0, pl.ds(base * LANES, rest * LANES + extras))
    for copy in copies:
        copy.wait()


def body(fields, weight, out_bias, observed, widths, owner_start):
    _, in_chan, rows_in, lon_dev = fields.shape
    taps, _, out_chan, _ = weight.shape
    half = taps // 2
    halo = 2 * half
    members = lax.axis_size("member")
    lon_count = lax.axis_size("lon")
    pairs = lon_count // 2
    rows_out = rows_in - taps + 1
    offset = round_up(halo, ROWS)
    slots = round_up(offset + lon_dev + halo, 2 * ROWS)
    points = rows_out * slots
    padded_out = round_up(out_chan, 2 * ROWS)
    full_blocks = in_chan // LANES
    main, rest = full_blocks // members, full_blocks % members
    sub = LANES // members
    valid = rest * sub
    pack = LANES // valid if rows_in % (LANES // valid) == 0 else 1
    extras = in_chan - full_blocks * LANES
    stack = taps * padded_out
    total_taps = taps * taps
    per_half = total_taps // 2
    special = per_half * padded_out
    half_rows = round_up(
        special + SPECIAL + round_up(-(-out_chan // 2), ROWS), ROWS * pack * pairs
    )
    bias_row = (per_half + 1) * extras
    assert rest and total_taps % 2 and bias_row + 2 <= SPECIAL
    wide = round_up(in_chan, LANES)
    plan = types.SimpleNamespace(
        members=members, taps=taps, half=half, offset=offset, lon_dev=lon_dev, out_chan=out_chan,
        padded_out=padded_out, rows_out=rows_out, points=points, main=main, rest=rest, pairs=pairs,
        pack=pack, valid=valid, sub=sub, extras=extras, half_rows=half_rows, per_half=per_half,
        special=special, bias_row=bias_row,
        special_row=special - (pairs - 1) * (half_rows // pairs),
    )
    own_lon = lax.axis_index("lon")
    factor = 1.0 / math.sqrt(members * rows_out * lon_dev * lon_count)
    even = own_lon % 2 == 0

    def swap_lon(value, d):
        return lax.ppermute(value, "lon", [(i, i ^ d) for i in range(lon_count)])

    def swap_far(value):
        step = [(i, (i + 1 if i % 2 else i - 1) % lon_count) for i in range(lon_count)]
        return lax.ppermute(value, "lon", step)

    def swap_member(value, d):
        return lax.ppermute(value, "member", [(i, i ^ d) for i in range(members)])

    any_space = pl.BlockSpec(memory_space=pl.ANY)
    field = jnp.transpose(fields[0], (1, 2, 0))
    packed_rows = main * rows_in + rows_in // pack + 1
    edge = jax.ShapeDtypeStruct((rows_in, halo, in_chan), jnp.bfloat16)
    near, far, *packed = pl.pallas_call(
        functools.partial(pack_kernel, plan),
        out_shape=[edge, edge]
        + [jax.ShapeDtypeStruct((packed_rows, lon_dev, LANES), jnp.bfloat16)] * members,
        in_specs=[vmem()],
        out_specs=[vmem()] * (members + 2),
        cost_estimate=cost(0, 4_000_000),
        compiler_params=limit(16),
        name="pack",
    )(field)
    far = swap_far(far)
    near = swap_lon(near, 1)
    traded = [packed[0]]
    for d in range(1, members):
        traded.append(swap_member(packed[d], d))

    own_outputs = pl.pallas_call(
        functools.partial(forward_kernel, plan),
        out_shape=jax.ShapeDtypeStruct((padded_out, points), jnp.bfloat16),
        in_specs=[any_space, vmem(), vmem(), any_space, vmem()],
        out_specs=vmem(),
        scratch_shapes=[
            pltpu.VMEM((rows_in, lon_dev, in_chan), jnp.bfloat16),
            pltpu.VMEM((total_taps, out_chan, in_chan), jnp.bfloat16),
            pltpu.VMEM((rows_in, slots, wide), jnp.bfloat16),
            pltpu.VMEM((total_taps, padded_out, wide), jnp.bfloat16),
            pltpu.VMEM((stack, points), jnp.float32),
            pltpu.SemaphoreType.DMA((taps + 2,)),
        ],
        cost_estimate=cost(2 * taps * stack * points * wide, 6_000_000),
        compiler_params=limit(56),
        name="forward",
    )(field, near, far, weight.reshape(total_taps, out_chan, in_chan), out_bias[None, :])
    outputs = [own_outputs]
    for d in range(1, members):
        outputs.append(swap_member(own_outputs, d))

    seen = jnp.transpose(observed, (2, 1, 0))
    start_edge = seen[:half]
    end_edge = seen[lon_dev - half :]
    strips = (jnp.where(even, start_edge, end_edge), jnp.where(even, end_edge, start_edge))
    strips, _ = lax.optimization_barrier((strips, own_outputs))
    far = swap_far(strips[0])
    near = swap_lon(strips[1], 1)
    tiles = main + 1
    x_all, truth = pl.pallas_call(
        functools.partial(prep_kernel, plan),
        out_shape=(
            jax.ShapeDtypeStruct((members, rows_in, slots, tiles * LANES), jnp.bfloat16),
            jax.ShapeDtypeStruct((padded_out, points), jnp.float32),
        ),
        in_specs=[vmem()] * (members + 3),
        out_specs=[vmem()] * 2,
        scratch_shapes=[pltpu.VMEM((rows_out, slots, LANES), jnp.float32)],
        cost_estimate=cost(0, 4_000_000),
        compiler_params=limit(20),
        name="prep",
    )(seen, near, far, *traded)

    main_rows = half_rows // pairs
    piece_rows = main * main_rows + main_rows // pack
    piece = jax.ShapeDtypeStruct((1, piece_rows, LANES), jnp.bfloat16)
    grad_own, score, send, keep = pl.pallas_call(
        functools.partial(gradient_kernel, plan),
        out_shape=(
            jax.ShapeDtypeStruct((padded_out, points), jnp.bfloat16),
            jax.ShapeDtypeStruct((1, points), jnp.float32),
            jax.ShapeDtypeStruct((pairs, piece_rows, LANES), jnp.bfloat16),
            jax.ShapeDtypeStruct((pairs, piece_rows, LANES), jnp.float32),
        ),
        in_specs=[vmem()] * (members + 3),
        out_specs=[vmem()] * 4,
        scratch_shapes=[
            pltpu.VMEM((members, padded_out, points), jnp.bfloat16),
            pltpu.VMEM((members, stack, points), jnp.bfloat16),
            pltpu.VMEM((tiles, 2 * half_rows, LANES), jnp.float32),
            pltpu.VMEM((2 * half_rows // pack, LANES), jnp.float32),
        ],
        cost_estimate=cost(
            2 * taps * stack * points * members * tiles * LANES, 6_000_000, 1_000_000
        ),
        compiler_params=limit(32),
        name="gradient",
    )(*outputs, x_all, truth, widths[None, :])

    mine, *out_pieces = pl.pallas_call(
        functools.partial(core_add_kernel, plan),
        out_shape=[jax.ShapeDtypeStruct((piece_rows, LANES), jnp.float32)] + [piece] * (pairs - 1),
        in_specs=[vmem(), vmem()],
        out_specs=[vmem()] * pairs,
        cost_estimate=cost(0, 1_500_000),
        compiler_params=limit(16),
        name="core_add",
    )(keep, swap_lon(send, 1))
    got = []
    for at, value in enumerate(out_pieces, 1):
        got.append(swap_lon(value, 2 * at))
    final = pl.pallas_call(
        functools.partial(pair_add_kernel, plan, factor),
        out_shape=piece,
        in_specs=[vmem()] * pairs,
        out_specs=vmem(),
        cost_estimate=cost(0, 600_000),
        compiler_params=limit(16),
        name="pair_add",
    )(mine, *got)

    gathered = [final]
    for at in range(1, pairs):
        gathered.append(swap_lon(final, 2 * at))
    grad_shape = jax.ShapeDtypeStruct((total_taps, out_chan, in_chan), jnp.float32)
    blocks = full_blocks
    tail_rows = half_rows - special
    halves = []
    for second in range(2):
        group = range(second * pairs // 2, (second + 1) * pairs // 2)
        column = jnp.concatenate([gathered[s] for s in group])
        held = []
        for d in range(members):
            value = column
            if d:
                value = swap_member(column, d)
            held.append((d, (value, swap_lon(value, 1))))
        halves.append((group, held))
    rest_lanes = rest * LANES + extras
    short = half_rows // pack

    def assemble(second, final, held, extra_inputs, other_shape):
        group = halves[second][0]
        arrays, layout = [], []
        for d, both in held:
            for other, value in enumerate(both):
                arrays.append(value)
                layout += [(d, s, bool(other)) for s in group]
        count, each = len(arrays), len(group)
        stages = max(len(held) * main, 1)
        taps_held = per_half + second

        def kernel(*refs):
            pieces = [ref.at[pl.ds(at, 1)] for ref in refs[:count] for at in range(each)]
            assemble_kernel(plan, second, tuple(layout), final, *pieces, *refs[count:])

        specs = [vmem()] * count
        if second:
            specs += [vmem(), any_space] + [vmem()] * (len(extra_inputs) - 2)
        return pl.pallas_call(
            kernel,
            out_shape=[grad_shape, jax.ShapeDtypeStruct(other_shape, jnp.float32)],
            in_specs=specs,
            out_specs=[any_space, vmem()],
            scratch_shapes=[
                pltpu.VMEM((stages, half_rows, LANES), jnp.float32),
                pltpu.VMEM((members, short, LANES), jnp.float32),
                pltpu.VMEM((stages, taps_held, out_chan, LANES), jnp.float32),
                pltpu.VMEM((1, taps_held, out_chan, rest_lanes), jnp.float32),
                pltpu.SemaphoreType.DMA((2 * stages + 2,)),
            ],
            input_output_aliases={count + 1: 0} if second else {},
            cost_estimate=cost(0, 5_000_000),
            compiler_params=limit(24),
            name="assemble",
        )(*arrays, *extra_inputs)

    weight_grad, carry = assemble(0, "all", halves[0][1], (), (blocks, tail_rows, LANES))
    held = halves[1][1]
    if main:
        weight_grad, known = assemble(
            1, "early", held[:-1], (carry, weight_grad), (members + 1, short, LANES)
        )
        weight_grad, bias_out = assemble(
            1, "late", held[-1:], (carry, weight_grad, known), (1, out_chan)
        )
    else:
        weight_grad, bias_out = assemble(1, "all", held, (carry, weight_grad), (1, out_chan))
    bias_grad = bias_out[0]
    weight_grad = weight_grad.reshape(taps, taps, out_chan, in_chan)

    assert BLOCK == lon_dev
    out_grad = pl.pallas_call(
        functools.partial(out_grad_kernel, plan),
        out_shape=jax.ShapeDtypeStruct((lon_dev, rows_out, out_chan), jnp.bfloat16),
        in_specs=[vmem()],
        out_specs=vmem(),
        scratch_shapes=[pltpu.VMEM((rows_out, slots, LANES), jnp.float32)],
        cost_estimate=cost(0, 400_000),
        compiler_params=limit(8),
        name="out_grad",
    )(grad_own)
    out_grad = jnp.transpose(out_grad, (2, 1, 0))[None]
    capacity = max(2, 3 * rows_out // members)
    owned_score = pl.pallas_call(
        functools.partial(owned_kernel, plan),
        out_shape=jax.ShapeDtypeStruct((1, capacity * lon_dev), jnp.float32),
        in_specs=[smem(), vmem()],
        out_specs=vmem(),
        scratch_shapes=[pltpu.VMEM((round_up(rows_out + capacity, ROWS), LANES), jnp.float32)],
        cost_estimate=cost(0, 100_000),
        compiler_params=limit(8),
        name="owned",
    )(owner_start, score)
    owned_score = owned_score[None]
    return (out_grad, owned_score, weight_grad, bias_grad)


def solution(mesh):
    in_specs = (P("member", None, None, "lon"), P(), P(), P(None, None, "lon"), P(), P("lon", None))
    out_specs = (P("member", None, None, "lon"), P("lon", "member", None), P(), P())
    return jax.shard_map(body, mesh=mesh, in_specs=in_specs, out_specs=out_specs, check_vma=False)
```

```python
import functools
import math
import types

import jax
import jax.numpy as jnp
from jax import lax
from jax.experimental import pallas as pl
from jax.experimental.pallas import tpu as pltpu
from jax.sharding import PartitionSpec as P


BLOCK = 45
LANES = 128
ROWS = 8
SPECIAL = 16


NT = (((1,), (1,)), ((), ()))
NN = (((1,), (0,)), ((), ()))


def round_up(value, unit):
    return -(-value // unit) * unit


def vmem():
    return pl.BlockSpec(memory_space=pltpu.VMEM)


def smem():
    return pl.BlockSpec(memory_space=pltpu.SMEM)


def limit(mib):
    return pltpu.CompilerParams(vmem_limit_bytes=mib << 20)


def here():
    lon = lax.axis_index("lon")
    return lax.axis_index("member"), lax.div(lon, 2), lax.rem(lon, 2)


def cost(flops, moved, special=0):
    return pl.CostEstimate(flops=flops, bytes_accessed=moved, transcendentals=special)


def column_of(row_ref, fill):
    count = row_ref.shape[1]
    row = jnp.concatenate(
        [row_ref[...], jnp.full((1, LANES - count), fill, jnp.float32)], axis=1
    )
    return jnp.transpose(jnp.broadcast_to(row, (LANES, LANES)))[:, :1]


def pack_kernel(plan, f_ref, near_ref, far_ref, *out_refs):
    members, main, rest = plan.members, plan.main, plan.rest
    pack, valid, sub = plan.pack, plan.valid, plan.sub
    rows_in, lon_dev, in_chan = f_ref.shape
    place_ref = here()
    halo = 2 * plan.half
    even = place_ref[2] == 0
    start_edge = f_ref[:, :halo, :].astype(jnp.float32)
    final = (lon_dev - halo) // ROWS * ROWS
    end_edge = f_ref[:, final:, :].astype(jnp.float32)[:, lon_dev - halo - final :]
    far_ref[...] = jnp.where(even, start_edge, end_edge).astype(far_ref.dtype)
    near_ref[...] = jnp.where(even, end_edge, start_edge).astype(near_ref.dtype)
    group = rows_in // pack
    base = main * members
    lane = lax.broadcasted_iota(jnp.int32, (1, 1, LANES), 2)
    full = (base + rest) * LANES
    slab = jnp.zeros((1, lon_dev, LANES), jnp.float32)
    for e in range(in_chan - full):
        for r in range(rows_in):
            value = f_ref[r : r + 1, :, full + e : full + e + 1].astype(jnp.float32)
            slab = jnp.where(lane == e * rows_in + r, value, slab)
    for d in range(members):
        owner = place_ref[0] ^ d
        out = out_refs[d]
        for k in range(main):
            spot = pl.ds(pl.multiple_of((k * members + owner) * LANES, LANES), LANES)
            out[k * rows_in : (k + 1) * rows_in] = f_ref[:, :, spot]
        for i in range(group):
            row = None
            for g in range(pack):
                for k in range(rest):
                    tile = f_ref[
                        g * group + i, :, (base + k) * LANES : (base + k + 1) * LANES
                    ].astype(jnp.float32)
                    start = g * valid + k * sub
                    moved = pltpu.roll(tile, lax.rem(start - owner * sub + LANES, LANES), 1)
                    row = moved if row is None else jnp.where(lane[0] >= start, moved, row)
            out[main * rows_in + i] = row.astype(out.dtype)
        out[main * rows_in + group] = slab[0].astype(out.dtype)


def forward_kernel(
    plan, field_ref, near_ref, far_ref, weight_ref, b_ref, o_ref,
    f_s, raw_s, x_s, w_s, acc_s, sems,
):
    taps, half, offset = plan.taps, plan.half, plan.offset
    lon_dev, halo = plan.lon_dev, 2 * plan.half
    rows_in, slots, wide = x_s.shape
    out_chan, in_chan = plan.out_chan, near_ref.shape[2]
    padded_out = w_s.shape[1]
    rows_out = rows_in - taps + 1
    points = rows_out * slots
    bulk = lon_dev // ROWS * ROWS
    full = in_chan // LANES * LANES
    field_copies = []
    for part in range(2):
        span = pl.ds(part * (rows_in // 2), rows_in // 2)
        copy = pltpu.make_async_copy(field_ref.at[span], f_s.at[span], sems.at[taps + part])
        copy.start()
        field_copies.append(copy)
    weight_copies = []
    for a in range(taps):
        span = pl.ds(a * taps, taps)
        copy = pltpu.make_async_copy(weight_ref.at[span], raw_s.at[span], sems.at[a])
        weight_copies.append(copy)
    weight_copies[0].start()
    x_s[:, :, full:] = jnp.zeros((rows_in, slots, wide - full), x_s.dtype)
    w_s[:, :, full:] = jnp.zeros((taps * taps, padded_out, wide - full), w_s.dtype)
    for copy in field_copies:
        copy.wait()
    for copy in weight_copies[1:]:
        copy.start()
    x_s[:, offset : offset + bulk, :in_chan] = f_s[:, :bulk, :]
    near = near_ref[...].astype(jnp.float32)
    far = far_ref[...].astype(jnp.float32)
    even = here()[2] == 0
    first = jnp.concatenate(
        [
            jnp.zeros((rows_in, offset - halo, in_chan), jnp.float32),
            jnp.where(even, far, near),
        ],
        axis=1,
    )
    x_s[:, :offset, :in_chan] = first.astype(x_s.dtype)
    tail = slots - offset - bulk
    final = jnp.concatenate(
        [
            f_s[:, bulk:, :].astype(jnp.float32),
            jnp.where(even, near, far),
            jnp.zeros((rows_in, tail - (lon_dev - bulk) - halo, in_chan), jnp.float32),
        ],
        axis=1,
    )
    x_s[:, offset + bulk :, :in_chan] = final.astype(x_s.dtype)
    for a in range(taps):
        weight_copies[a].wait()
        mine = slice(a * taps, (a + 1) * taps)
        w_s[mine, :out_chan, :in_chan] = raw_s[mine]
        part = lax.dot_general(
            w_s[a * taps : (a + 1) * taps].reshape(taps * padded_out, wide),
            x_s[a : a + rows_out].reshape(points, wide),
            NT,
            preferred_element_type=jnp.float32,
        )
        if a == 0:
            acc_s[...] = part
        else:
            acc_s[...] += part
    slot = lax.broadcasted_iota(jnp.int32, (1, points), 1) % slots
    inside = (slot >= offset - half) & (slot < offset + lon_dev + half)
    bias = column_of(b_ref, 0.0)
    for lo in range(0, padded_out, 2 * ROWS):
        rows = slice(lo, lo + 2 * ROWS)
        total = jnp.zeros((2 * ROWS, points), jnp.float32) + bias[rows]
        for b in range(taps):
            piece = acc_s[b * padded_out + lo : b * padded_out + lo + 2 * ROWS, :]
            shift = (half - b) % points
            total = total + (pltpu.roll(piece, shift, 1) if shift else piece)
        row = lo + lax.broadcasted_iota(jnp.int32, (2 * ROWS, 1), 0)
        keep = inside & (row < out_chan)
        o_ref[rows, :] = jnp.where(keep, total, 0.0).astype(o_ref.dtype)


def prep_kernel(plan, obs_ref, near_ref, far_ref, own_ref, *refs):
    truth_ref, own_out_ref, row_s = refs[-3:]
    refs = refs[:-3]
    own_out_ref[...] = own_ref[...]
    half, offset, padded_out = plan.half, plan.offset, plan.padded_out
    even = here()[2] == 0
    near, far = near_ref[...], far_ref[...]
    out_chan = obs_ref.shape[2]
    total_rows = obs_ref.shape[1]
    width = plan.points // total_rows
    per = LANES // width
    row_s[...] = jnp.zeros(row_s.shape, jnp.float32)
    for x in range(half):
        row_s[:, offset - half + x, :out_chan] = jnp.where(even, far[x], near[x])
        row_s[:, offset + plan.lon_dev + x, :out_chan] = jnp.where(even, near[x], far[x])
    for x in range(plan.lon_dev):
        row_s[:, offset + x, :out_chan] = obs_ref[x]
    for j in range(total_rows // per):
        tile = row_s[j * per : (j + 1) * per].reshape(LANES, LANES)
        truth_ref[:, j * LANES : (j + 1) * LANES] = jnp.transpose(tile)[:padded_out]
    members, main = plan.members, plan.main
    pack, valid, extras = plan.pack, plan.valid, plan.extras
    out_ref = refs[-1]
    _, rows_in, slots, _ = out_ref.shape
    lon_dev = plan.lon_dev
    bulk = lon_dev // ROWS * ROWS
    group = rows_in // pack
    lane = lax.broadcasted_iota(jnp.int32, (1, LANES), 1)
    out_ref[:, :, bulk:, :] = jnp.zeros(
        (members, rows_in, slots - bulk, out_ref.shape[3]), out_ref.dtype
    )
    for d in range(members):
        ref = refs[d]
        for k in range(main):
            out_ref[d, :, :lon_dev, k * LANES : (k + 1) * LANES] = ref[
                k * rows_in : (k + 1) * rows_in
            ]
        slab = ref[main * rows_in + group].astype(jnp.float32)
        for g in range(pack):
            for i in range(group):
                value = ref[main * rows_in + i].astype(jnp.float32)
                if g:
                    value = pltpu.roll(value, LANES - g * valid, 1)
                r = g * group + i
                for e in range(extras):
                    shift = (valid + e - (e * rows_in + r)) % LANES
                    moved = pltpu.roll(slab, shift, 1) if shift else slab
                    value = jnp.where(lane == valid + e, moved, value)
                value = jnp.where(lane == valid + extras, 1.0, value)
                out_ref[d, r, :lon_dev, main * LANES :] = value.astype(out_ref.dtype)


def split_bias(tile, row_high):
    row = lax.broadcasted_iota(jnp.int32, tile.shape, 0)
    size = tile.shape[0]
    total = jnp.where(row == row_high, tile + pltpu.roll(tile, size - 1, 0), tile)
    left = total - total.astype(jnp.bfloat16).astype(jnp.float32)
    return jnp.where(row == row_high + 1, pltpu.roll(left, 1, 0), total)


def fix_rows(plan, ref, index, piece, value_of):
    @pl.when(piece == 2 * plan.pairs - 1)
    def _():
        lo = plan.special_row
        tile = value_of(lo, lo + SPECIAL)
        ref[index, lo : lo + SPECIAL, :] = split_bias(tile, plan.bias_row).astype(ref.dtype)


def gradient_kernel(plan, *refs):
    members, taps, half = plan.members, plan.taps, plan.half
    out_chan, padded_out, points = plan.out_chan, plan.padded_out, plan.points
    main, pairs, pack, valid = plan.main, plan.pairs, plan.pack, plan.valid
    rows_out, size, extras = plan.rows_out, plan.half_rows, plan.extras
    per_half, special = plan.per_half, plan.special
    place_ref = here()
    y_refs = refs[:members]
    x_ref, obs_ref, wid_ref = refs[members : 3 + members]
    g_ref, score_ref, send_ref, keep_ref = refs[3 + members : 7 + members]
    g_s, gs_s, wide_s, packed_s = refs[7 + members :]
    step = 2 * LANES
    width_all = column_of(wid_ref, 1.0)
    for left in range(0, points, step):
        tally = jnp.zeros((ROWS, step), jnp.float32)
        for lo in range(0, padded_out, 2 * ROWS):
            rows = slice(lo, lo + 2 * ROWS)
            cols = slice(left, left + step)
            shape = (2 * ROWS, step)
            width = width_all[rows]
            inverse = 1.0 / (width * width)
            values = [y[rows, cols].astype(jnp.float32) for y in y_refs]
            target = obs_ref[rows, cols]
            pair_sum = jnp.full(shape, float(members), jnp.float32)
            pull = [jnp.zeros(shape, jnp.float32) for _ in values]
            for x in range(members):
                for y in range(x + 1, members):
                    spread = values[x] - values[y]
                    kernel_pair = jnp.exp(-0.5 * spread * spread * inverse)
                    pair_sum = pair_sum + 2.0 * kernel_pair
                    weighted = kernel_pair * spread
                    pull[x] = pull[x] + weighted
                    pull[y] = pull[y] - weighted
            obs_sum = jnp.zeros(shape, jnp.float32)
            for x in range(members):
                misfit = values[x] - target
                kernel_obs = jnp.exp(-0.5 * misfit * misfit * inverse)
                obs_sum = obs_sum + kernel_obs
                grad = inverse * (misfit * kernel_obs - pull[x] / members)
                g_s[x, rows, cols] = grad.astype(jnp.bfloat16)
            terms = pair_sum / (2.0 * members * members) - obs_sum / members
            row = lo + lax.broadcasted_iota(jnp.int32, (2 * ROWS, 1), 0)
            terms = jnp.where(row < out_chan, terms, 0.0)
            tally = tally + terms[:ROWS] + terms[ROWS:]
        score_ref[:, left : left + step] = jnp.sum(tally, axis=0, keepdims=True) / out_chan
    g_ref[...] = g_s[0]
    for x in range(members):
        for lo in range(0, padded_out, 2 * ROWS):
            grad = g_s[x, lo : lo + 2 * ROWS, :].astype(jnp.float32)
            for b in range(taps):
                shift = (b - half - plan.offset) % points
                moved = pltpu.roll(grad, shift, 1) if shift else grad
                start = b * padded_out + lo
                gs_s[x, start : start + 2 * ROWS, :] = moved.astype(jnp.bfloat16)
    tiles = main + 1
    split = size - special - SPECIAL
    for h in range(2):
        wide_s[:, h * size + special : (h + 1) * size, :] = jnp.zeros(
            (tiles, size - special, LANES), jnp.float32
        )
    for a in range(taps):
        total = None
        for x in range(members):
            part = lax.dot_general(
                gs_s[x],
                x_ref[x, a : a + rows_out].reshape(points, tiles * LANES),
                NN,
                preferred_element_type=jnp.float32,
            )
            total = part if total is None else total + part
        for b in range(taps):
            tap = a * taps + b
            block = total[b * padded_out : (b + 1) * padded_out]
            across = jnp.transpose(block[:, main * LANES :])
            if tap < 2 * per_half:
                h, i = tap // per_half, tap % per_half
                spans = [(0, padded_out, h * size + i * padded_out)]
                line = h * size + special + i * extras
            else:
                first = size - split
                spans = [(0, split, first), (split, padded_out, size + first)]
                line = size + special + per_half * extras
            for k in range(tiles):
                for lo, hi, at in spans:
                    wide_s[k, at : at + hi - lo, :] = block[lo:hi, k * LANES : (k + 1) * LANES]
            for e in range(extras):
                wide_s[0, line + e : line + e + 1, :padded_out] = across[valid + e : valid + e + 1]
            if a == 0 and b == half:
                line = size + special + plan.bias_row
                ones = valid + extras
                wide_s[0, line : line + 1, :padded_out] = across[ones : ones + 1]
    short = size // pack
    lane = lax.broadcasted_iota(jnp.int32, (1, LANES), 1)
    for h in range(2):
        packed = wide_s[main, h * size : h * size + short, :]
        for g in range(1, pack):
            at = h * size + g * short
            moved = pltpu.roll(wide_s[main, at : at + short, :], g * valid, 1)
            packed = jnp.where(lane >= g * valid, moved, packed)
        packed_s[h * short : (h + 1) * short, :] = packed
    pair, core = place_ref[1], place_ref[2]
    main_rows = size // pairs
    rest_rows = main_rows // pack
    for s in range(pairs):
        for out, side in ((keep_ref, core), (send_ref, 1 - core)):
            piece = 2 * (pair ^ s) + side
            at = 0
            for k in range(main):
                source = pl.ds(pl.multiple_of(piece * main_rows, main_rows), main_rows)
                out[s, at : at + main_rows, :] = wide_s[k, source, :].astype(out.dtype)
                at += main_rows
            source = pl.ds(pl.multiple_of(piece * rest_rows, rest_rows), rest_rows)
            out[s, at : at + rest_rows, :] = packed_s[source, :].astype(out.dtype)
        spot = 2 * size - main_rows
        fix_rows(
            plan, send_ref, s, 2 * (pair ^ s) + 1 - core,
            lambda lo, hi: wide_s[0, spot + lo : spot + hi, :]
            if main
            else packed_s[spot + lo : spot + hi, :],
        )


def core_add_kernel(plan, keep_ref, got_ref, mine_ref, *out_refs):
    place_ref = here()
    mine_ref[...] = keep_ref[0] + got_ref[0].astype(jnp.float32)
    pair, core = place_ref[1], place_ref[2]
    for s in range(1, plan.pairs):
        out = out_refs[s - 1]
        out[0] = (keep_ref[s] + got_ref[s].astype(jnp.float32)).astype(out.dtype)
        fix_rows(
            plan, out, 0, 2 * (pair ^ s) + core,
            lambda lo, hi: keep_ref[s, lo:hi, :] + got_ref[s, lo:hi, :].astype(jnp.float32),
        )


def pair_add_kernel(plan, factor, mine_ref, *refs):
    place_ref = here()
    out = refs[-1]

    def value(lo, hi):
        total = mine_ref[lo:hi, :]
        for ref in refs[:-1]:
            total = total + ref[0, lo:hi, :].astype(jnp.float32)
        return total * factor

    out[0] = value(0, mine_ref.shape[0]).astype(out.dtype)
    fix_rows(plan, out, 0, 2 * place_ref[1] + place_ref[2], value)


def out_grad_kernel(plan, g_ref, out_ref, row_s):
    lon_dev, offset = plan.lon_dev, plan.offset
    rows_out, out_chan = out_ref.shape[1:]
    width = plan.points // rows_out
    per = LANES // width
    padded_out = g_ref.shape[0]
    for j in range(rows_out // per):
        tile = g_ref[:, j * LANES : (j + 1) * LANES].astype(jnp.float32)
        tile = jnp.concatenate(
            [tile, jnp.zeros((LANES - padded_out, LANES), jnp.float32)], axis=0
        )
        row_s[j * per : (j + 1) * per] = jnp.transpose(tile).reshape(per, width, LANES)
    for x in range(lon_dev):
        out_ref[x] = row_s[:, offset + x, :out_chan].astype(out_ref.dtype)


def owned_kernel(plan, start_ref, score_ref, out_ref, row_s):
    lon_dev, offset, points = plan.lon_dev, plan.offset, plan.points
    rows_out = plan.rows_out
    width = points // rows_out
    capacity = out_ref.shape[1] // lon_dev
    member = here()[0]
    first = start_ref[0, member]
    count = start_ref[0, member + 1] - first
    lane = lax.broadcasted_iota(jnp.int32, (1, points), 1)
    row_s[...] = jnp.zeros(row_s.shape, jnp.float32)
    score = score_ref[...]
    for i in range(rows_out):
        moved = pltpu.roll(score, (points - i * width - offset) % points, 1)
        row_s[i : i + 1, :] = jnp.where(lane < lon_dev, moved, 0.0)[:, :LANES]
    reach = round_up(capacity * lon_dev, LANES)
    total = jnp.zeros((1, reach), jnp.float32)
    blank = jnp.zeros((1, reach - LANES), jnp.float32)
    for t in range(capacity):
        row = jnp.where(t < count, row_s[pl.ds(first + t, 1), :], 0.0)
        row = jnp.concatenate([row, blank], axis=1)
        total = total + (pltpu.roll(row, t * lon_dev, 1) if t else row)
    out_ref[...] = total[:, : capacity * lon_dev]


def assemble_kernel(plan, second, layout, final, *refs):
    members, main, rest = plan.members, plan.main, plan.rest
    out_chan, padded_out, pairs = plan.out_chan, plan.padded_out, plan.pairs
    pack, valid, sub = plan.pack, plan.valid, plan.sub
    size, extras, per_half = plan.half_rows, plan.extras, plan.per_half
    special = plan.special
    member, pair, core = here()
    piece_refs = refs[: len(layout)]
    refs = refs[len(layout) :]
    own_half = lax.div(pair, pairs // 2)
    this_half = 1 - own_half if second else own_half
    low = this_half == 0
    main_rows = size // pairs
    rest_rows = main_rows // pack
    split = size - special - SPECIAL
    begin = special + SPECIAL
    known_ref = carry_ref = None
    if second:
        carry_ref, _, *refs = refs
        if final == "late":
            known_ref, *refs = refs
    out_ref, other_ref, main_s, packed_s, main_stage, rest_stage, sems = refs
    if known_ref is not None:
        packed_s[...] = known_ref[:members]
    shown = []
    for d, _, _ in layout:
        if d not in shown:
            shown.append(d)
    for ref, (d, s, other) in zip(piece_refs, layout):
        side = 1 - core if other else core
        piece = lax.rem(2 * (pair ^ s) + side, pairs)
        row = 0
        for k in range(main):
            spot = pl.ds(pl.multiple_of(piece * main_rows, ROWS), main_rows)
            main_s[shown.index(d) * main + k, spot, :] = ref[0, row : row + main_rows, :].astype(
                jnp.float32
            )
            row += main_rows
        spot = pl.ds(pl.multiple_of(piece * rest_rows, ROWS), rest_rows)
        packed_s[member ^ d, spot, :] = ref[0, row : row + rest_rows, :].astype(jnp.float32)
    lines = packed_s[0, special:begin, :] if not main else None
    for at, d in enumerate(shown if main else ()):
        found = main_s[at * main, special:begin, :]
        if lines is None:
            lines = found if known_ref is None else known_ref[members, :SPECIAL, :]
        lines = jnp.where(member == d, found, lines)
    copies = []

    def emit(source, stage, lanes):
        spans = [(pl.ds(0, per_half), pl.ds(this_half * per_half, per_half))]
        if second:
            spans.append((pl.ds(per_half, 1), pl.ds(2 * per_half, 1)))
        for from_span, to_span in spans:
            copy = pltpu.make_async_copy(
                source.at[stage, from_span],
                out_ref.at[to_span, :, lanes],
                sems.at[len(copies)],
            )
            copy.start()
            copies.append(copy)

    def fill(stage_ref, stage, lanes, tile, block):
        for i in range(per_half):
            stage_ref[stage, i, :, lanes] = tile[i * padded_out : i * padded_out + out_chan]
        mine = tile[begin:size]
        if second:
            theirs = carry_ref[block, SPECIAL:, :]
            stage_ref[stage, per_half, :split, lanes] = jnp.where(low, mine, theirs)
            stage_ref[stage, per_half, split:, lanes] = jnp.where(low, theirs, mine)[
                : out_chan - split
            ]
        else:
            other_ref[block, SPECIAL:, :] = mine

    if not second:
        other_ref[:, :SPECIAL, :] = jnp.zeros(
            (other_ref.shape[0], SPECIAL, LANES), jnp.float32
        )
        other_ref[0, :SPECIAL, :] = lines
    for at, d in enumerate(shown if main else ()):
        for k in range(main):
            block = k * members + (member ^ d)
            fill(main_stage, at * main + k, slice(None), main_s[at * main + k], block)
            emit(
                main_stage,
                at * main + k,
                pl.ds(pl.multiple_of(block * LANES, LANES), LANES),
            )
    if final == "early":
        other_ref[:members] = packed_s[...]
        other_ref[members] = jnp.zeros(other_ref.shape[1:], jnp.float32)
        other_ref[members, :SPECIAL, :] = lines
    else:
        lane = lax.broadcasted_iota(jnp.int32, (1, LANES), 1)
        base = main * members
        for k in range(rest):
            tiles = []
            for g in range(pack):
                tile = None
                for owner in range(members):
                    shift = (owner * sub - g * valid - k * sub) % LANES
                    value = packed_s[owner]
                    if shift:
                        value = pltpu.roll(value, shift, 1)
                    tile = (
                        value if tile is None else jnp.where(lane >= owner * sub, value, tile)
                    )
                tiles.append(tile)
            tile = tiles[0] if pack == 1 else jnp.concatenate(tiles, axis=0)
            fill(rest_stage, 0, slice(k * LANES, (k + 1) * LANES), tile, base + k)
        blank = jnp.zeros((LANES - SPECIAL, LANES), jnp.float32)

        def put_columns(rows, first, count, tap):
            columns = jnp.transpose(jnp.concatenate([rows, blank], axis=0))
            for i in range(count):
                for e in range(extras):
                    at = first + i * extras + e
                    lanes = slice(rest * LANES + e, rest * LANES + e + 1)
                    rest_stage[0, tap + i, :, lanes] = columns[:out_chan, at : at + 1]

        put_columns(lines, 0, per_half, 0)
        if second:
            top = jnp.where(low, carry_ref[0, :SPECIAL, :], lines)
            put_columns(top, per_half * extras, 1, per_half)
            line = plan.bias_row
            other_ref[...] = (top[line : line + 1] + top[line + 1 : line + 2])[:, :out_chan]
        emit(rest_stage, 0, pl.ds(base * LANES, rest * LANES + extras))
    for copy in copies:
        copy.wait()


def body(fields, weight, out_bias, observed, widths, owner_start):
    _, in_chan, rows_in, lon_dev = fields.shape
    taps, _, out_chan, _ = weight.shape
    half = taps // 2
    halo = 2 * half
    members = lax.axis_size("member")
    lon_count = lax.axis_size("lon")
    pairs = lon_count // 2
    rows_out = rows_in - taps + 1
    offset = round_up(halo, ROWS)
    slots = round_up(offset + lon_dev + halo, 2 * ROWS)
    points = rows_out * slots
    padded_out = round_up(out_chan, 2 * ROWS)
    full_blocks = in_chan // LANES
    main, rest = full_blocks // members, full_blocks % members
    sub = LANES // members
    valid = rest * sub
    pack = LANES // valid if rows_in % (LANES // valid) == 0 else 1
    extras = in_chan - full_blocks * LANES
    stack = taps * padded_out
    total_taps = taps * taps
    per_half = total_taps // 2
    special = per_half * padded_out
    half_rows = round_up(
        special + SPECIAL + round_up(-(-out_chan // 2), ROWS), ROWS * pack * pairs
    )
    bias_row = (per_half + 1) * extras
    assert rest and total_taps % 2 and bias_row + 2 <= SPECIAL
    wide = round_up(in_chan, LANES)
    plan = types.SimpleNamespace(
        members=members, taps=taps, half=half, offset=offset, lon_dev=lon_dev, out_chan=out_chan,
        padded_out=padded_out, rows_out=rows_out, points=points, main=main, rest=rest, pairs=pairs,
        pack=pack, valid=valid, sub=sub, extras=extras, half_rows=half_rows, per_half=per_half,
        special=special, bias_row=bias_row,
        special_row=special - (pairs - 1) * (half_rows // pairs),
    )
    own_lon = lax.axis_index("lon")
    factor = 1.0 / math.sqrt(members * rows_out * lon_dev * lon_count)
    even = own_lon % 2 == 0

    def swap_lon(value, d):
        return lax.ppermute(value, "lon", [(i, i ^ d) for i in range(lon_count)])

    def swap_far(value):
        step = [(i, (i + 1 if i % 2 else i - 1) % lon_count) for i in range(lon_count)]
        return lax.ppermute(value, "lon", step)

    def swap_member(value, d):
        return lax.ppermute(value, "member", [(i, i ^ d) for i in range(members)])

    any_space = pl.BlockSpec(memory_space=pl.ANY)
    field = jnp.transpose(fields[0], (1, 2, 0))
    packed_rows = main * rows_in + rows_in // pack + 1
    edge = jax.ShapeDtypeStruct((rows_in, halo, in_chan), jnp.bfloat16)
    near, far, *packed = pl.pallas_call(
        functools.partial(pack_kernel, plan),
        out_shape=[edge, edge]
        + [jax.ShapeDtypeStruct((packed_rows, lon_dev, LANES), jnp.bfloat16)] * members,
        in_specs=[vmem()],
        out_specs=[vmem()] * (members + 2),
        cost_estimate=cost(0, 4_000_000),
        compiler_params=limit(16),
        name="pack",
    )(field)
    far = swap_far(far)
    near = swap_lon(near, 1)
    traded = [packed[0]]
    for d in range(1, members):
        traded.append(swap_member(packed[d], d))

    own_outputs = pl.pallas_call(
        functools.partial(forward_kernel, plan),
        out_shape=jax.ShapeDtypeStruct((padded_out, points), jnp.bfloat16),
        in_specs=[any_space, vmem(), vmem(), any_space, vmem()],
        out_specs=vmem(),
        scratch_shapes=[
            pltpu.VMEM((rows_in, lon_dev, in_chan), jnp.bfloat16),
            pltpu.VMEM((total_taps, out_chan, in_chan), jnp.bfloat16),
            pltpu.VMEM((rows_in, slots, wide), jnp.bfloat16),
            pltpu.VMEM((total_taps, padded_out, wide), jnp.bfloat16),
            pltpu.VMEM((stack, points), jnp.float32),
            pltpu.SemaphoreType.DMA((taps + 2,)),
        ],
        cost_estimate=cost(2 * taps * stack * points * wide, 6_000_000),
        compiler_params=limit(56),
        name="forward",
    )(field, near, far, weight.reshape(total_taps, out_chan, in_chan), out_bias[None, :])
    outputs = [own_outputs]
    for d in range(1, members):
        outputs.append(swap_member(own_outputs, d))

    seen = jnp.transpose(observed, (2, 1, 0))
    start_edge = seen[:half]
    end_edge = seen[lon_dev - half :]
    strips = (jnp.where(even, start_edge, end_edge), jnp.where(even, end_edge, start_edge))
    strips, _ = lax.optimization_barrier((strips, own_outputs))
    far = swap_far(strips[0])
    near = swap_lon(strips[1], 1)
    tiles = main + 1
    x_all, truth, own_copy = pl.pallas_call(
        functools.partial(prep_kernel, plan),
        out_shape=(
            jax.ShapeDtypeStruct((members, rows_in, slots, tiles * LANES), jnp.bfloat16),
            jax.ShapeDtypeStruct((padded_out, points), jnp.float32),
            jax.ShapeDtypeStruct((padded_out, points), jnp.bfloat16),
        ),
        in_specs=[vmem()] * (members + 4),
        out_specs=[vmem()] * 3,
        scratch_shapes=[pltpu.VMEM((rows_out, slots, LANES), jnp.float32)],
        cost_estimate=cost(0, 4_000_000),
        compiler_params=limit(20),
        name="prep",
    )(seen, near, far, own_outputs, *traded)
    outputs[0] = own_copy

    main_rows = half_rows // pairs
    piece_rows = main * main_rows + main_rows // pack
    piece = jax.ShapeDtypeStruct((1, piece_rows, LANES), jnp.bfloat16)
    grad_own, score, send, keep = pl.pallas_call(
        functools.partial(gradient_kernel, plan),
        out_shape=(
            jax.ShapeDtypeStruct((padded_out, points), jnp.bfloat16),
            jax.ShapeDtypeStruct((1, points), jnp.float32),
            jax.ShapeDtypeStruct((pairs, piece_rows, LANES), jnp.bfloat16),
            jax.ShapeDtypeStruct((pairs, piece_rows, LANES), jnp.float32),
        ),
        in_specs=[vmem()] * (members + 3),
        out_specs=[vmem()] * 4,
        scratch_shapes=[
            pltpu.VMEM((members, padded_out, points), jnp.bfloat16),
            pltpu.VMEM((members, stack, points), jnp.bfloat16),
            pltpu.VMEM((tiles, 2 * half_rows, LANES), jnp.float32),
            pltpu.VMEM((2 * half_rows // pack, LANES), jnp.float32),
        ],
        cost_estimate=cost(
            2 * taps * stack * points * members * tiles * LANES, 6_000_000, 1_000_000
        ),
        compiler_params=limit(32),
        name="gradient",
    )(*outputs, x_all, truth, widths[None, :])

    mine, *out_pieces = pl.pallas_call(
        functools.partial(core_add_kernel, plan),
        out_shape=[jax.ShapeDtypeStruct((piece_rows, LANES), jnp.float32)] + [piece] * (pairs - 1),
        in_specs=[vmem(), vmem()],
        out_specs=[vmem()] * pairs,
        cost_estimate=cost(0, 1_500_000),
        compiler_params=limit(16),
        name="core_add",
    )(keep, swap_lon(send, 1))
    got = []
    for at, value in enumerate(out_pieces, 1):
        got.append(swap_lon(value, 2 * at))
    final = pl.pallas_call(
        functools.partial(pair_add_kernel, plan, factor),
        out_shape=piece,
        in_specs=[vmem()] * pairs,
        out_specs=vmem(),
        cost_estimate=cost(0, 600_000),
        compiler_params=limit(16),
        name="pair_add",
    )(mine, *got)

    gathered = [final]
    for at in range(1, pairs):
        gathered.append(swap_lon(final, 2 * at))
    grad_shape = jax.ShapeDtypeStruct((total_taps, out_chan, in_chan), jnp.float32)
    blocks = full_blocks
    tail_rows = half_rows - special
    halves = []
    for second in range(2):
        group = range(second * pairs // 2, (second + 1) * pairs // 2)
        column = jnp.concatenate([gathered[s] for s in group])
        held = []
        for d in range(members):
            value = column
            if d:
                value = swap_member(column, d)
            held.append((d, (value, swap_lon(value, 1))))
        halves.append((group, held))
    rest_lanes = rest * LANES + extras
    short = half_rows // pack

    def assemble(second, final, held, extra_inputs, other_shape):
        group = halves[second][0]
        arrays, layout = [], []
        for d, both in held:
            for other, value in enumerate(both):
                arrays.append(value)
                layout += [(d, s, bool(other)) for s in group]
        count, each = len(arrays), len(group)
        stages = max(len(held) * main, 1)
        taps_held = per_half + second

        def kernel(*refs):
            pieces = [ref.at[pl.ds(at, 1)] for ref in refs[:count] for at in range(each)]
            assemble_kernel(plan, second, tuple(layout), final, *pieces, *refs[count:])

        specs = [vmem()] * count
        if second:
            specs += [vmem(), any_space] + [vmem()] * (len(extra_inputs) - 2)
        return pl.pallas_call(
            kernel,
            out_shape=[grad_shape, jax.ShapeDtypeStruct(other_shape, jnp.float32)],
            in_specs=specs,
            out_specs=[any_space, vmem()],
            scratch_shapes=[
                pltpu.VMEM((stages, half_rows, LANES), jnp.float32),
                pltpu.VMEM((members, short, LANES), jnp.float32),
                pltpu.VMEM((stages, taps_held, out_chan, LANES), jnp.float32),
                pltpu.VMEM((1, taps_held, out_chan, rest_lanes), jnp.float32),
                pltpu.SemaphoreType.DMA((2 * stages + 2,)),
            ],
            input_output_aliases={count + 1: 0} if second else {},
            cost_estimate=cost(0, 5_000_000),
            compiler_params=limit(24),
            name="assemble",
        )(*arrays, *extra_inputs)

    weight_grad, carry = assemble(0, "all", halves[0][1], (), (blocks, tail_rows, LANES))
    held = halves[1][1]
    if main:
        weight_grad, known = assemble(
            1, "early", held[:-1], (carry, weight_grad), (members + 1, short, LANES)
        )
        weight_grad, bias_out = assemble(
            1, "late", held[-1:], (carry, weight_grad, known), (1, out_chan)
        )
    else:
        weight_grad, bias_out = assemble(1, "all", held, (carry, weight_grad), (1, out_chan))
    bias_grad = bias_out[0]
    weight_grad = weight_grad.reshape(taps, taps, out_chan, in_chan)

    assert BLOCK == lon_dev
    out_grad = pl.pallas_call(
        functools.partial(out_grad_kernel, plan),
        out_shape=jax.ShapeDtypeStruct((lon_dev, rows_out, out_chan), jnp.bfloat16),
        in_specs=[vmem()],
        out_specs=vmem(),
        scratch_shapes=[pltpu.VMEM((rows_out, slots, LANES), jnp.float32)],
        cost_estimate=cost(0, 400_000),
        compiler_params=limit(8),
        name="out_grad",
    )(grad_own)
    out_grad = jnp.transpose(out_grad, (2, 1, 0))[None]
    capacity = max(2, 3 * rows_out // members)
    owned_score = pl.pallas_call(
        functools.partial(owned_kernel, plan),
        out_shape=jax.ShapeDtypeStruct((1, capacity * lon_dev), jnp.float32),
        in_specs=[smem(), vmem()],
        out_specs=vmem(),
        scratch_shapes=[pltpu.VMEM((round_up(rows_out + capacity, ROWS), LANES), jnp.float32)],
        cost_estimate=cost(0, 100_000),
        compiler_params=limit(8),
        name="owned",
    )(owner_start, score)
    owned_score = owned_score[None]
    return (out_grad, owned_score, weight_grad, bias_grad)


def solution(mesh):
    in_specs = (P("member", None, None, "lon"), P(), P(), P(None, None, "lon"), P(), P("lon", None))
    out_specs = (P("member", None, None, "lon"), P("lon", "member", None), P(), P())
    return jax.shard_map(body, mesh=mesh, in_specs=in_specs, out_specs=out_specs, check_vma=False)
```

```python
import functools
import math
import types

import jax
import jax.numpy as jnp
from jax import lax
from jax.experimental import pallas as pl
from jax.experimental.pallas import tpu as pltpu
from jax.sharding import PartitionSpec as P


BLOCK = 45
LANES = 128
ROWS = 8
SPECIAL = 16


NT = (((1,), (1,)), ((), ()))
NN = (((1,), (0,)), ((), ()))


def round_up(value, unit):
    return -(-value // unit) * unit


def vmem():
    return pl.BlockSpec(memory_space=pltpu.VMEM)


def smem():
    return pl.BlockSpec(memory_space=pltpu.SMEM)


def limit(mib):
    return pltpu.CompilerParams(vmem_limit_bytes=mib << 20)


def here():
    lon = lax.axis_index("lon")
    return lax.axis_index("member"), lax.div(lon, 2), lax.rem(lon, 2)


def cost(flops, moved, special=0):
    return pl.CostEstimate(flops=flops, bytes_accessed=moved, transcendentals=special)


def column_of(row_ref, fill):
    count = row_ref.shape[1]
    row = jnp.concatenate(
        [row_ref[...], jnp.full((1, LANES - count), fill, jnp.float32)], axis=1
    )
    return jnp.transpose(jnp.broadcast_to(row, (LANES, LANES)))[:, :1]


def pack_kernel(plan, f_ref, seen_ref, near_ref, far_ref, seen_near_ref, seen_far_ref, *out_refs):
    members, main, rest = plan.members, plan.main, plan.rest
    pack, valid, sub = plan.pack, plan.valid, plan.sub
    rows_in, lon_dev, in_chan = f_ref.shape
    place_ref = here()
    halo = 2 * plan.half
    even = place_ref[2] == 0
    start_edge = f_ref[:, :halo, :].astype(jnp.float32)
    final = (lon_dev - halo) // ROWS * ROWS
    end_edge = f_ref[:, final:, :].astype(jnp.float32)[:, lon_dev - halo - final :]
    far_ref[...] = jnp.where(even, start_edge, end_edge).astype(far_ref.dtype)
    near_ref[...] = jnp.where(even, end_edge, start_edge).astype(near_ref.dtype)
    start_seen = seen_ref[: plan.half]
    end_seen = seen_ref[lon_dev - plan.half :]
    seen_far_ref[...] = jnp.where(even, start_seen, end_seen)
    seen_near_ref[...] = jnp.where(even, end_seen, start_seen)
    group = rows_in // pack
    base = main * members
    lane = lax.broadcasted_iota(jnp.int32, (1, 1, LANES), 2)
    full = (base + rest) * LANES
    slab = jnp.zeros((1, lon_dev, LANES), jnp.float32)
    for e in range(in_chan - full):
        for r in range(rows_in):
            value = f_ref[r : r + 1, :, full + e : full + e + 1].astype(jnp.float32)
            slab = jnp.where(lane == e * rows_in + r, value, slab)
    for d in range(members):
        owner = place_ref[0] ^ d
        out = out_refs[d]
        for k in range(main):
            spot = pl.ds(pl.multiple_of((k * members + owner) * LANES, LANES), LANES)
            out[k * rows_in : (k + 1) * rows_in] = f_ref[:, :, spot]
        for i in range(group):
            row = None
            for g in range(pack):
                for k in range(rest):
                    tile = f_ref[
                        g * group + i, :, (base + k) * LANES : (base + k + 1) * LANES
                    ].astype(jnp.float32)
                    start = g * valid + k * sub
                    moved = pltpu.roll(tile, lax.rem(start - owner * sub + LANES, LANES), 1)
                    row = moved if row is None else jnp.where(lane[0] >= start, moved, row)
            out[main * rows_in + i] = row.astype(out.dtype)
        out[main * rows_in + group] = slab[0].astype(out.dtype)


def stage_kernel(w_ref, w_out):
    _, out_chan, in_chan = w_ref.shape
    full = in_chan // LANES * LANES
    w_out[:, :, full:] = jnp.zeros(
        (w_out.shape[0], w_out.shape[1], w_out.shape[2] - full), w_out.dtype
    )
    w_out[:, :out_chan, :in_chan] = w_ref[...]


def forward_kernel(
    plan, f_s, near_ref, far_ref, w_s, b_ref, o_ref, x_s, acc_s,
):
    taps, half, offset = plan.taps, plan.half, plan.offset
    lon_dev, halo = plan.lon_dev, 2 * plan.half
    rows_in, slots, wide = x_s.shape
    out_chan, in_chan = plan.out_chan, near_ref.shape[2]
    padded_out = w_s.shape[1]
    rows_out = rows_in - taps + 1
    points = rows_out * slots
    bulk = lon_dev // ROWS * ROWS
    full = in_chan // LANES * LANES
    x_s[:, :, full:] = jnp.zeros((rows_in, slots, wide - full), x_s.dtype)
    x_s[:, offset : offset + bulk, :in_chan] = f_s[:, :bulk, :]
    near = near_ref[...].astype(jnp.float32)
    far = far_ref[...].astype(jnp.float32)
    even = here()[2] == 0
    first = jnp.concatenate(
        [
            jnp.zeros((rows_in, offset - halo, in_chan), jnp.float32),
            jnp.where(even, far, near),
        ],
        axis=1,
    )
    x_s[:, :offset, :in_chan] = first.astype(x_s.dtype)
    tail = slots - offset - bulk
    final = jnp.concatenate(
        [
            f_s[:, bulk:, :].astype(jnp.float32),
            jnp.where(even, near, far),
            jnp.zeros((rows_in, tail - (lon_dev - bulk) - halo, in_chan), jnp.float32),
        ],
        axis=1,
    )
    x_s[:, offset + bulk :, :in_chan] = final.astype(x_s.dtype)
    for a in range(taps):
        part = lax.dot_general(
            w_s[a * taps : (a + 1) * taps].reshape(taps * padded_out, wide),
            x_s[a : a + rows_out].reshape(points, wide),
            NT,
            preferred_element_type=jnp.float32,
        )
        if a == 0:
            acc_s[...] = part
        else:
            acc_s[...] += part
    slot = lax.broadcasted_iota(jnp.int32, (1, points), 1) % slots
    inside = (slot >= offset - half) & (slot < offset + lon_dev + half)
    bias = column_of(b_ref, 0.0)
    for lo in range(0, padded_out, 2 * ROWS):
        rows = slice(lo, lo + 2 * ROWS)
        total = jnp.zeros((2 * ROWS, points), jnp.float32) + bias[rows]
        for b in range(taps):
            piece = acc_s[b * padded_out + lo : b * padded_out + lo + 2 * ROWS, :]
            shift = (half - b) % points
            total = total + (pltpu.roll(piece, shift, 1) if shift else piece)
        row = lo + lax.broadcasted_iota(jnp.int32, (2 * ROWS, 1), 0)
        keep = inside & (row < out_chan)
        o_ref[rows, :] = jnp.where(keep, total, 0.0).astype(o_ref.dtype)


def prep_kernel(plan, obs_ref, near_ref, far_ref, own_ref, *refs):
    truth_ref, own_out_ref, row_s = refs[-3:]
    refs = refs[:-3]
    own_out_ref[...] = own_ref[...]
    half, offset, padded_out = plan.half, plan.offset, plan.padded_out
    even = here()[2] == 0
    near, far = near_ref[...], far_ref[...]
    out_chan = obs_ref.shape[2]
    total_rows = obs_ref.shape[1]
    width = plan.points // total_rows
    per = LANES // width
    row_s[...] = jnp.zeros(row_s.shape, jnp.float32)
    for x in range(half):
        row_s[:, offset - half + x, :out_chan] = jnp.where(even, far[x], near[x])
        row_s[:, offset + plan.lon_dev + x, :out_chan] = jnp.where(even, near[x], far[x])
    for x in range(plan.lon_dev):
        row_s[:, offset + x, :out_chan] = obs_ref[x]
    for j in range(total_rows // per):
        tile = row_s[j * per : (j + 1) * per].reshape(LANES, LANES)
        truth_ref[:, j * LANES : (j + 1) * LANES] = jnp.transpose(tile)[:padded_out]
    members, main = plan.members, plan.main
    pack, valid, extras = plan.pack, plan.valid, plan.extras
    out_ref = refs[-1]
    _, rows_in, slots, _ = out_ref.shape
    lon_dev = plan.lon_dev
    bulk = lon_dev // ROWS * ROWS
    group = rows_in // pack
    lane = lax.broadcasted_iota(jnp.int32, (1, LANES), 1)
    out_ref[:, :, bulk:, :] = jnp.zeros(
        (members, rows_in, slots - bulk, out_ref.shape[3]), out_ref.dtype
    )
    for d in range(members):
        ref = refs[d]
        for k in range(main):
            out_ref[d, :, :lon_dev, k * LANES : (k + 1) * LANES] = ref[
                k * rows_in : (k + 1) * rows_in
            ]
        slab = ref[main * rows_in + group].astype(jnp.float32)
        for g in range(pack):
            for i in range(group):
                value = ref[main * rows_in + i].astype(jnp.float32)
                if g:
                    value = pltpu.roll(value, LANES - g * valid, 1)
                r = g * group + i
                for e in range(extras):
                    shift = (valid + e - (e * rows_in + r)) % LANES
                    moved = pltpu.roll(slab, shift, 1) if shift else slab
                    value = jnp.where(lane == valid + e, moved, value)
                value = jnp.where(lane == valid + extras, 1.0, value)
                out_ref[d, r, :lon_dev, main * LANES :] = value.astype(out_ref.dtype)


def split_bias(tile, row_high):
    row = lax.broadcasted_iota(jnp.int32, tile.shape, 0)
    size = tile.shape[0]
    total = jnp.where(row == row_high, tile + pltpu.roll(tile, size - 1, 0), tile)
    left = total - total.astype(jnp.bfloat16).astype(jnp.float32)
    return jnp.where(row == row_high + 1, pltpu.roll(left, 1, 0), total)


def fix_rows(plan, ref, index, piece, value_of):
    @pl.when(piece == 2 * plan.pairs - 1)
    def _():
        lo = plan.special_row
        tile = value_of(lo, lo + SPECIAL)
        ref[index, lo : lo + SPECIAL, :] = split_bias(tile, plan.bias_row).astype(ref.dtype)


def gradient_kernel(plan, *refs):
    members, taps, half = plan.members, plan.taps, plan.half
    out_chan, padded_out, points = plan.out_chan, plan.padded_out, plan.points
    main, pairs, pack, valid = plan.main, plan.pairs, plan.pack, plan.valid
    rows_out, size, extras = plan.rows_out, plan.half_rows, plan.extras
    per_half, special = plan.per_half, plan.special
    place_ref = here()
    y_refs = refs[:members]
    x_ref, obs_ref, wid_ref = refs[members : 3 + members]
    g_ref, score_ref, send_ref, keep_ref = refs[3 + members : 7 + members]
    g_s, gs_s, wide_s, packed_s = refs[7 + members :]
    step = 2 * LANES
    width_all = column_of(wid_ref, 1.0)
    for left in range(0, points, step):
        tally = jnp.zeros((ROWS, step), jnp.float32)
        for lo in range(0, padded_out, 2 * ROWS):
            rows = slice(lo, lo + 2 * ROWS)
            cols = slice(left, left + step)
            shape = (2 * ROWS, step)
            width = width_all[rows]
            inverse = 1.0 / (width * width)
            values = [y[rows, cols].astype(jnp.float32) for y in y_refs]
            target = obs_ref[rows, cols]
            pair_sum = jnp.full(shape, float(members), jnp.float32)
            pull = [jnp.zeros(shape, jnp.float32) for _ in values]
            for x in range(members):
                for y in range(x + 1, members):
                    spread = values[x] - values[y]
                    kernel_pair = jnp.exp(-0.5 * spread * spread * inverse)
                    pair_sum = pair_sum + 2.0 * kernel_pair
                    weighted = kernel_pair * spread
                    pull[x] = pull[x] + weighted
                    pull[y] = pull[y] - weighted
            obs_sum = jnp.zeros(shape, jnp.float32)
            for x in range(members):
                misfit = values[x] - target
                kernel_obs = jnp.exp(-0.5 * misfit * misfit * inverse)
                obs_sum = obs_sum + kernel_obs
                grad = inverse * (misfit * kernel_obs - pull[x] / members)
                g_s[x, rows, cols] = grad.astype(jnp.bfloat16)
            terms = pair_sum / (2.0 * members * members) - obs_sum / members
            row = lo + lax.broadcasted_iota(jnp.int32, (2 * ROWS, 1), 0)
            terms = jnp.where(row < out_chan, terms, 0.0)
            tally = tally + terms[:ROWS] + terms[ROWS:]
        score_ref[:, left : left + step] = jnp.sum(tally, axis=0, keepdims=True) / out_chan
    g_ref[...] = g_s[0]
    for x in range(members):
        for lo in range(0, padded_out, 2 * ROWS):
            grad = g_s[x, lo : lo + 2 * ROWS, :].astype(jnp.float32)
            for b in range(taps):
                shift = (b - half - plan.offset) % points
                moved = pltpu.roll(grad, shift, 1) if shift else grad
                start = b * padded_out + lo
                gs_s[x, start : start + 2 * ROWS, :] = moved.astype(jnp.bfloat16)
    tiles = main + 1
    split = size - special - SPECIAL
    for h in range(2):
        wide_s[:, h * size + special : (h + 1) * size, :] = jnp.zeros(
            (tiles, size - special, LANES), jnp.float32
        )
    for a in range(taps):
        total = None
        for x in range(members):
            part = lax.dot_general(
                gs_s[x],
                x_ref[x, a : a + rows_out].reshape(points, tiles * LANES),
                NN,
                preferred_element_type=jnp.float32,
            )
            total = part if total is None else total + part
        for b in range(taps):
            tap = a * taps + b
            block = total[b * padded_out : (b + 1) * padded_out]
            across = jnp.transpose(block[:, main * LANES :])
            if tap < 2 * per_half:
                h, i = tap // per_half, tap % per_half
                spans = [(0, padded_out, h * size + i * padded_out)]
                line = h * size + special + i * extras
            else:
                first = size - split
                spans = [(0, split, first), (split, padded_out, size + first)]
                line = size + special + per_half * extras
            for k in range(tiles):
                for lo, hi, at in spans:
                    wide_s[k, at : at + hi - lo, :] = block[lo:hi, k * LANES : (k + 1) * LANES]
            for e in range(extras):
                wide_s[0, line + e : line + e + 1, :padded_out] = across[valid + e : valid + e + 1]
            if a == 0 and b == half:
                line = size + special + plan.bias_row
                ones = valid + extras
                wide_s[0, line : line + 1, :padded_out] = across[ones : ones + 1]
    short = size // pack
    lane = lax.broadcasted_iota(jnp.int32, (1, LANES), 1)
    for h in range(2):
        packed = wide_s[main, h * size : h * size + short, :]
        for g in range(1, pack):
            at = h * size + g * short
            moved = pltpu.roll(wide_s[main, at : at + short, :], g * valid, 1)
            packed = jnp.where(lane >= g * valid, moved, packed)
        packed_s[h * short : (h + 1) * short, :] = packed
    pair, core = place_ref[1], place_ref[2]
    main_rows = size // pairs
    rest_rows = main_rows // pack
    for s in range(pairs):
        for out, side in ((keep_ref, core), (send_ref, 1 - core)):
            piece = 2 * (pair ^ s) + side
            at = 0
            for k in range(main):
                source = pl.ds(pl.multiple_of(piece * main_rows, main_rows), main_rows)
                out[s, at : at + main_rows, :] = wide_s[k, source, :].astype(out.dtype)
                at += main_rows
            source = pl.ds(pl.multiple_of(piece * rest_rows, rest_rows), rest_rows)
            out[s, at : at + rest_rows, :] = packed_s[source, :].astype(out.dtype)
        spot = 2 * size - main_rows
        fix_rows(
            plan, send_ref, s, 2 * (pair ^ s) + 1 - core,
            lambda lo, hi: wide_s[0, spot + lo : spot + hi, :]
            if main
            else packed_s[spot + lo : spot + hi, :],
        )


def core_add_kernel(plan, keep_ref, got_ref, mine_ref, *out_refs):
    place_ref = here()
    mine_ref[...] = keep_ref[0] + got_ref[0].astype(jnp.float32)
    pair, core = place_ref[1], place_ref[2]
    for s in range(1, plan.pairs):
        out = out_refs[s - 1]
        out[0] = (keep_ref[s] + got_ref[s].astype(jnp.float32)).astype(out.dtype)
        fix_rows(
            plan, out, 0, 2 * (pair ^ s) + core,
            lambda lo, hi: keep_ref[s, lo:hi, :] + got_ref[s, lo:hi, :].astype(jnp.float32),
        )


def pair_add_kernel(plan, factor, mine_ref, *refs):
    place_ref = here()
    out = refs[-1]

    def value(lo, hi):
        total = mine_ref[lo:hi, :]
        for ref in refs[:-1]:
            total = total + ref[0, lo:hi, :].astype(jnp.float32)
        return total * factor

    out[0] = value(0, mine_ref.shape[0]).astype(out.dtype)
    fix_rows(plan, out, 0, 2 * place_ref[1] + place_ref[2], value)


def out_grad_kernel(plan, g_ref, out_ref, row_s):
    lon_dev, offset = plan.lon_dev, plan.offset
    rows_out, out_chan = out_ref.shape[1:]
    width = plan.points // rows_out
    per = LANES // width
    padded_out = g_ref.shape[0]
    for j in range(rows_out // per):
        tile = g_ref[:, j * LANES : (j + 1) * LANES].astype(jnp.float32)
        tile = jnp.concatenate(
            [tile, jnp.zeros((LANES - padded_out, LANES), jnp.float32)], axis=0
        )
        row_s[j * per : (j + 1) * per] = jnp.transpose(tile).reshape(per, width, LANES)
    for x in range(lon_dev):
        out_ref[x] = row_s[:, offset + x, :out_chan].astype(out_ref.dtype)


def owned_kernel(plan, start_ref, score_ref, out_ref, row_s):
    lon_dev, offset, points = plan.lon_dev, plan.offset, plan.points
    rows_out = plan.rows_out
    width = points // rows_out
    capacity = out_ref.shape[1] // lon_dev
    member = here()[0]
    first = start_ref[0, member]
    count = start_ref[0, member + 1] - first
    lane = lax.broadcasted_iota(jnp.int32, (1, points), 1)
    row_s[...] = jnp.zeros(row_s.shape, jnp.float32)
    score = score_ref[...]
    for i in range(rows_out):
        moved = pltpu.roll(score, (points - i * width - offset) % points, 1)
        row_s[i : i + 1, :] = jnp.where(lane < lon_dev, moved, 0.0)[:, :LANES]
    reach = round_up(capacity * lon_dev, LANES)
    total = jnp.zeros((1, reach), jnp.float32)
    blank = jnp.zeros((1, reach - LANES), jnp.float32)
    for t in range(capacity):
        row = jnp.where(t < count, row_s[pl.ds(first + t, 1), :], 0.0)
        row = jnp.concatenate([row, blank], axis=1)
        total = total + (pltpu.roll(row, t * lon_dev, 1) if t else row)
    out_ref[...] = total[:, : capacity * lon_dev]


def assemble_kernel(plan, second, layout, final, *refs):
    members, main, rest = plan.members, plan.main, plan.rest
    out_chan, padded_out, pairs = plan.out_chan, plan.padded_out, plan.pairs
    pack, valid, sub = plan.pack, plan.valid, plan.sub
    size, extras, per_half = plan.half_rows, plan.extras, plan.per_half
    special = plan.special
    member, pair, core = here()
    piece_refs = refs[: len(layout)]
    refs = refs[len(layout) :]
    own_half = lax.div(pair, pairs // 2)
    this_half = 1 - own_half if second else own_half
    low = this_half == 0
    main_rows = size // pairs
    rest_rows = main_rows // pack
    split = size - special - SPECIAL
    begin = special + SPECIAL
    known_ref = carry_ref = None
    if second:
        carry_ref, _, *refs = refs
        if final == "late":
            known_ref, *refs = refs
    out_ref, other_ref, main_s, packed_s, main_stage, rest_stage, sems = refs
    if known_ref is not None:
        packed_s[...] = known_ref[:members]
    shown = []
    for d, _, _ in layout:
        if d not in shown:
            shown.append(d)
    for ref, (d, s, other) in zip(piece_refs, layout):
        side = 1 - core if other else core
        piece = lax.rem(2 * (pair ^ s) + side, pairs)
        row = 0
        for k in range(main):
            spot = pl.ds(pl.multiple_of(piece * main_rows, ROWS), main_rows)
            main_s[shown.index(d) * main + k, spot, :] = ref[0, row : row + main_rows, :].astype(
                jnp.float32
            )
            row += main_rows
        spot = pl.ds(pl.multiple_of(piece * rest_rows, ROWS), rest_rows)
        packed_s[member ^ d, spot, :] = ref[0, row : row + rest_rows, :].astype(jnp.float32)
    lines = packed_s[0, special:begin, :] if not main else None
    for at, d in enumerate(shown if main else ()):
        found = main_s[at * main, special:begin, :]
        if lines is None:
            lines = found if known_ref is None else known_ref[members, :SPECIAL, :]
        lines = jnp.where(member == d, found, lines)
    copies = []

    def emit(source, stage, lanes):
        spans = [(pl.ds(0, per_half), pl.ds(this_half * per_half, per_half))]
        if second:
            spans.append((pl.ds(per_half, 1), pl.ds(2 * per_half, 1)))
        for from_span, to_span in spans:
            copy = pltpu.make_async_copy(
                source.at[stage, from_span],
                out_ref.at[to_span, :, lanes],
                sems.at[len(copies)],
            )
            copy.start()
            copies.append(copy)

    def fill(stage_ref, stage, lanes, tile, block):
        for i in range(per_half):
            stage_ref[stage, i, :, lanes] = tile[i * padded_out : i * padded_out + out_chan]
        mine = tile[begin:size]
        if second:
            theirs = carry_ref[block, SPECIAL:, :]
            stage_ref[stage, per_half, :split, lanes] = jnp.where(low, mine, theirs)
            stage_ref[stage, per_half, split:, lanes] = jnp.where(low, theirs, mine)[
                : out_chan - split
            ]
        else:
            other_ref[block, SPECIAL:, :] = mine

    if not second:
        other_ref[:, :SPECIAL, :] = jnp.zeros(
            (other_ref.shape[0], SPECIAL, LANES), jnp.float32
        )
        other_ref[0, :SPECIAL, :] = lines
    for at, d in enumerate(shown if main else ()):
        for k in range(main):
            block = k * members + (member ^ d)
            fill(main_stage, at * main + k, slice(None), main_s[at * main + k], block)
            emit(
                main_stage,
                at * main + k,
                pl.ds(pl.multiple_of(block * LANES, LANES), LANES),
            )
    if final == "early":
        other_ref[:members] = packed_s[...]
        other_ref[members] = jnp.zeros(other_ref.shape[1:], jnp.float32)
        other_ref[members, :SPECIAL, :] = lines
    else:
        lane = lax.broadcasted_iota(jnp.int32, (1, LANES), 1)
        base = main * members
        for k in range(rest):
            tiles = []
            for g in range(pack):
                tile = None
                for owner in range(members):
                    shift = (owner * sub - g * valid - k * sub) % LANES
                    value = packed_s[owner]
                    if shift:
                        value = pltpu.roll(value, shift, 1)
                    tile = (
                        value if tile is None else jnp.where(lane >= owner * sub, value, tile)
                    )
                tiles.append(tile)
            tile = tiles[0] if pack == 1 else jnp.concatenate(tiles, axis=0)
            fill(rest_stage, 0, slice(k * LANES, (k + 1) * LANES), tile, base + k)
        blank = jnp.zeros((LANES - SPECIAL, LANES), jnp.float32)

        def put_columns(rows, first, count, tap):
            columns = jnp.transpose(jnp.concatenate([rows, blank], axis=0))
            for i in range(count):
                for e in range(extras):
                    at = first + i * extras + e
                    lanes = slice(rest * LANES + e, rest * LANES + e + 1)
                    rest_stage[0, tap + i, :, lanes] = columns[:out_chan, at : at + 1]

        put_columns(lines, 0, per_half, 0)
        if second:
            top = jnp.where(low, carry_ref[0, :SPECIAL, :], lines)
            put_columns(top, per_half * extras, 1, per_half)
            line = plan.bias_row
            other_ref[...] = (top[line : line + 1] + top[line + 1 : line + 2])[:, :out_chan]
        emit(rest_stage, 0, pl.ds(base * LANES, rest * LANES + extras))
    for copy in copies:
        copy.wait()


def body(fields, weight, out_bias, observed, widths, owner_start):
    _, in_chan, rows_in, lon_dev = fields.shape
    taps, _, out_chan, _ = weight.shape
    half = taps // 2
    halo = 2 * half
    members = lax.axis_size("member")
    lon_count = lax.axis_size("lon")
    pairs = lon_count // 2
    rows_out = rows_in - taps + 1
    offset = round_up(halo, ROWS)
    slots = round_up(offset + lon_dev + halo, 2 * ROWS)
    points = rows_out * slots
    padded_out = round_up(out_chan, 2 * ROWS)
    full_blocks = in_chan // LANES
    main, rest = full_blocks // members, full_blocks % members
    sub = LANES // members
    valid = rest * sub
    pack = LANES // valid if rows_in % (LANES // valid) == 0 else 1
    extras = in_chan - full_blocks * LANES
    stack = taps * padded_out
    total_taps = taps * taps
    per_half = total_taps // 2
    special = per_half * padded_out
    half_rows = round_up(
        special + SPECIAL + round_up(-(-out_chan // 2), ROWS), ROWS * pack * pairs
    )
    bias_row = (per_half + 1) * extras
    assert rest and total_taps % 2 and bias_row + 2 <= SPECIAL
    wide = round_up(in_chan, LANES)
    plan = types.SimpleNamespace(
        members=members, taps=taps, half=half, offset=offset, lon_dev=lon_dev, out_chan=out_chan,
        padded_out=padded_out, rows_out=rows_out, points=points, main=main, rest=rest, pairs=pairs,
        pack=pack, valid=valid, sub=sub, extras=extras, half_rows=half_rows, per_half=per_half,
        special=special, bias_row=bias_row,
        special_row=special - (pairs - 1) * (half_rows // pairs),
    )
    factor = 1.0 / math.sqrt(members * rows_out * lon_dev * lon_count)

    def swap_lon(value, d):
        return lax.ppermute(value, "lon", [(i, i ^ d) for i in range(lon_count)])

    def swap_far(value):
        step = [(i, (i + 1 if i % 2 else i - 1) % lon_count) for i in range(lon_count)]
        return lax.ppermute(value, "lon", step)

    def swap_member(value, d):
        return lax.ppermute(value, "member", [(i, i ^ d) for i in range(members)])

    any_space = pl.BlockSpec(memory_space=pl.ANY)
    field = jnp.transpose(fields[0], (1, 2, 0))
    packed_rows = main * rows_in + rows_in // pack + 1
    edge = jax.ShapeDtypeStruct((rows_in, halo, in_chan), jnp.bfloat16)
    seen = jnp.transpose(observed, (2, 1, 0))
    strip = jax.ShapeDtypeStruct((half, rows_out, out_chan), jnp.float32)
    near, far, seen_near, seen_far, *packed = pl.pallas_call(
        functools.partial(pack_kernel, plan),
        out_shape=[edge, edge, strip, strip]
        + [jax.ShapeDtypeStruct((packed_rows, lon_dev, LANES), jnp.bfloat16)] * members,
        in_specs=[vmem()] * 2,
        out_specs=[vmem()] * (members + 4),
        cost_estimate=cost(0, 4_000_000),
        compiler_params=limit(16),
        name="pack",
    )(field, seen)
    far = swap_far(far)
    near = swap_lon(near, 1)
    traded = [packed[0]]
    for d in range(1, members):
        traded.append(swap_member(packed[d], d))

    seen_far = swap_far(seen_far)
    seen_near = swap_lon(seen_near, 1)
    weight_flat = weight.reshape(total_taps, out_chan, in_chan)
    w_all = pl.pallas_call(
        stage_kernel,
        out_shape=jax.ShapeDtypeStruct((total_taps, padded_out, wide), jnp.bfloat16),
        in_specs=[vmem()],
        out_specs=vmem(),
        cost_estimate=cost(0, 5_000_000),
        compiler_params=limit(8),
        name="stage",
    )(weight_flat)
    own_outputs = pl.pallas_call(
        functools.partial(forward_kernel, plan),
        out_shape=jax.ShapeDtypeStruct((padded_out, points), jnp.bfloat16),
        in_specs=[vmem()] * 5,
        out_specs=vmem(),
        scratch_shapes=[
            pltpu.VMEM((rows_in, slots, wide), jnp.bfloat16),
            pltpu.VMEM((stack, points), jnp.float32),
        ],
        cost_estimate=cost(2 * taps * stack * points * wide, 6_000_000),
        compiler_params=limit(20),
        name="forward",
    )(field, near, far, w_all, out_bias[None, :])
    outputs = [own_outputs]
    for d in range(1, members):
        outputs.append(swap_member(own_outputs, d))

    tiles = main + 1
    x_all, truth, own_copy = pl.pallas_call(
        functools.partial(prep_kernel, plan),
        out_shape=(
            jax.ShapeDtypeStruct((members, rows_in, slots, tiles * LANES), jnp.bfloat16),
            jax.ShapeDtypeStruct((padded_out, points), jnp.float32),
            jax.ShapeDtypeStruct((padded_out, points), jnp.bfloat16),
        ),
        in_specs=[vmem()] * (members + 4),
        out_specs=[vmem()] * 3,
        scratch_shapes=[pltpu.VMEM((rows_out, slots, LANES), jnp.float32)],
        cost_estimate=cost(0, 4_000_000),
        compiler_params=limit(20),
        name="prep",
    )(seen, seen_near, seen_far, own_outputs, *traded)
    outputs[0] = own_copy

    main_rows = half_rows // pairs
    piece_rows = main * main_rows + main_rows // pack
    piece = jax.ShapeDtypeStruct((1, piece_rows, LANES), jnp.bfloat16)
    grad_own, score, send, keep = pl.pallas_call(
        functools.partial(gradient_kernel, plan),
        out_shape=(
            jax.ShapeDtypeStruct((padded_out, points), jnp.bfloat16),
            jax.ShapeDtypeStruct((1, points), jnp.float32),
            jax.ShapeDtypeStruct((pairs, piece_rows, LANES), jnp.bfloat16),
            jax.ShapeDtypeStruct((pairs, piece_rows, LANES), jnp.float32),
        ),
        in_specs=[vmem()] * (members + 3),
        out_specs=[vmem()] * 4,
        scratch_shapes=[
            pltpu.VMEM((members, padded_out, points), jnp.bfloat16),
            pltpu.VMEM((members, stack, points), jnp.bfloat16),
            pltpu.VMEM((tiles, 2 * half_rows, LANES), jnp.float32),
            pltpu.VMEM((2 * half_rows // pack, LANES), jnp.float32),
        ],
        cost_estimate=cost(
            2 * taps * stack * points * members * tiles * LANES, 6_000_000, 1_000_000
        ),
        compiler_params=limit(32),
        name="gradient",
    )(*outputs, x_all, truth, widths[None, :])

    mine, *out_pieces = pl.pallas_call(
        functools.partial(core_add_kernel, plan),
        out_shape=[jax.ShapeDtypeStruct((piece_rows, LANES), jnp.float32)] + [piece] * (pairs - 1),
        in_specs=[vmem(), vmem()],
        out_specs=[vmem()] * pairs,
        cost_estimate=cost(0, 1_500_000),
        compiler_params=limit(16),
        name="core_add",
    )(keep, swap_lon(send, 1))
    got = []
    for at, value in enumerate(out_pieces, 1):
        got.append(swap_lon(value, 2 * at))
    final = pl.pallas_call(
        functools.partial(pair_add_kernel, plan, factor),
        out_shape=piece,
        in_specs=[vmem()] * pairs,
        out_specs=vmem(),
        cost_estimate=cost(0, 600_000),
        compiler_params=limit(16),
        name="pair_add",
    )(mine, *got)

    gathered = [final]
    for at in range(1, pairs):
        gathered.append(swap_lon(final, 2 * at))
    grad_shape = jax.ShapeDtypeStruct((total_taps, out_chan, in_chan), jnp.float32)
    blocks = full_blocks
    tail_rows = half_rows - special
    halves = []
    for second in range(2):
        group = range(second * pairs // 2, (second + 1) * pairs // 2)
        column = jnp.concatenate([gathered[s] for s in group])
        held = []
        for d in range(members):
            value = column
            if d:
                value = swap_member(column, d)
            held.append((d, (value, swap_lon(value, 1))))
        halves.append((group, held))
    rest_lanes = rest * LANES + extras
    short = half_rows // pack

    def assemble(second, final, held, extra_inputs, other_shape):
        group = halves[second][0]
        arrays, layout = [], []
        for d, both in held:
            for other, value in enumerate(both):
                arrays.append(value)
                layout += [(d, s, bool(other)) for s in group]
        count, each = len(arrays), len(group)
        stages = max(len(held) * main, 1)
        taps_held = per_half + second

        def kernel(*refs):
            pieces = [ref.at[pl.ds(at, 1)] for ref in refs[:count] for at in range(each)]
            assemble_kernel(plan, second, tuple(layout), final, *pieces, *refs[count:])

        specs = [vmem()] * count
        if second:
            specs += [vmem(), any_space] + [vmem()] * (len(extra_inputs) - 2)
        return pl.pallas_call(
            kernel,
            out_shape=[grad_shape, jax.ShapeDtypeStruct(other_shape, jnp.float32)],
            in_specs=specs,
            out_specs=[any_space, vmem()],
            scratch_shapes=[
                pltpu.VMEM((stages, half_rows, LANES), jnp.float32),
                pltpu.VMEM((members, short, LANES), jnp.float32),
                pltpu.VMEM((stages, taps_held, out_chan, LANES), jnp.float32),
                pltpu.VMEM((1, taps_held, out_chan, rest_lanes), jnp.float32),
                pltpu.SemaphoreType.DMA((2 * stages + 2,)),
            ],
            input_output_aliases={count + 1: 0} if second else {},
            cost_estimate=cost(0, 5_000_000),
            compiler_params=limit(24),
            name="assemble",
        )(*arrays, *extra_inputs)

    weight_grad, carry = assemble(0, "all", halves[0][1], (), (blocks, tail_rows, LANES))
    held = halves[1][1]
    if main:
        weight_grad, known = assemble(
            1, "early", held[:-1], (carry, weight_grad), (members + 1, short, LANES)
        )
        weight_grad, bias_out = assemble(
            1, "late", held[-1:], (carry, weight_grad, known), (1, out_chan)
        )
    else:
        weight_grad, bias_out = assemble(1, "all", held, (carry, weight_grad), (1, out_chan))
    bias_grad = bias_out[0]
    weight_grad = weight_grad.reshape(taps, taps, out_chan, in_chan)

    assert BLOCK == lon_dev
    out_grad = pl.pallas_call(
        functools.partial(out_grad_kernel, plan),
        out_shape=jax.ShapeDtypeStruct((lon_dev, rows_out, out_chan), jnp.bfloat16),
        in_specs=[vmem()],
        out_specs=vmem(),
        scratch_shapes=[pltpu.VMEM((rows_out, slots, LANES), jnp.float32)],
        cost_estimate=cost(0, 400_000),
        compiler_params=limit(8),
        name="out_grad",
    )(grad_own)
    out_grad = jnp.transpose(out_grad, (2, 1, 0))[None]
    capacity = max(2, 3 * rows_out // members)
    owned_score = pl.pallas_call(
        functools.partial(owned_kernel, plan),
        out_shape=jax.ShapeDtypeStruct((1, capacity * lon_dev), jnp.float32),
        in_specs=[smem(), vmem()],
        out_specs=vmem(),
        scratch_shapes=[pltpu.VMEM((round_up(rows_out + capacity, ROWS), LANES), jnp.float32)],
        cost_estimate=cost(0, 100_000),
        compiler_params=limit(8),
        name="owned",
    )(owner_start, score)
    owned_score = owned_score[None]
    return (out_grad, owned_score, weight_grad, bias_grad)


def solution(mesh):
    in_specs = (P("member", None, None, "lon"), P(), P(), P(None, None, "lon"), P(), P("lon", None))
    out_specs = (P("member", None, None, "lon"), P("lon", "member", None), P(), P())
    return jax.shard_map(body, mesh=mesh, in_specs=in_specs, out_specs=out_specs, check_vma=False)
```

```python
import functools
import math
import types

import jax
import jax.numpy as jnp
from jax import lax
from jax.experimental import pallas as pl
from jax.experimental.pallas import tpu as pltpu
from jax.sharding import PartitionSpec as P


BLOCK = 45
LANES = 128
ROWS = 8
SPECIAL = 16


NT = (((1,), (1,)), ((), ()))
NN = (((1,), (0,)), ((), ()))


def round_up(value, unit):
    return -(-value // unit) * unit


def vmem():
    return pl.BlockSpec(memory_space=pltpu.VMEM)


def smem():
    return pl.BlockSpec(memory_space=pltpu.SMEM)


def limit(mib):
    return pltpu.CompilerParams(vmem_limit_bytes=mib << 20)


def here():
    lon = lax.axis_index("lon")
    return lax.axis_index("member"), lax.div(lon, 2), lax.rem(lon, 2)


def cost(flops, moved, special=0):
    return pl.CostEstimate(flops=flops, bytes_accessed=moved, transcendentals=special)


def column_of(row_ref, fill):
    count = row_ref.shape[1]
    row = jnp.concatenate(
        [row_ref[...], jnp.full((1, LANES - count), fill, jnp.float32)], axis=1
    )
    return jnp.transpose(jnp.broadcast_to(row, (LANES, LANES)))[:, :1]


def strips_kernel(seen_ref, near_ref, far_ref):
    even = here()[2] == 0
    width = near_ref.shape[0]
    start = seen_ref[:width]
    end = seen_ref[seen_ref.shape[0] - width :]
    far_ref[...] = jnp.where(even, start, end)
    near_ref[...] = jnp.where(even, end, start)


def pack_kernel(plan, f_ref, near_ref, far_ref, *out_refs):
    members, main, rest = plan.members, plan.main, plan.rest
    pack, valid, sub = plan.pack, plan.valid, plan.sub
    rows_in, lon_dev, in_chan = f_ref.shape
    place_ref = here()
    halo = 2 * plan.half
    even = place_ref[2] == 0
    start_edge = f_ref[:, :halo, :].astype(jnp.float32)
    final = (lon_dev - halo) // ROWS * ROWS
    end_edge = f_ref[:, final:, :].astype(jnp.float32)[:, lon_dev - halo - final :]
    far_ref[...] = jnp.where(even, start_edge, end_edge).astype(far_ref.dtype)
    near_ref[...] = jnp.where(even, end_edge, start_edge).astype(near_ref.dtype)
    group = rows_in // pack
    base = main * members
    lane = lax.broadcasted_iota(jnp.int32, (1, 1, LANES), 2)
    full = (base + rest) * LANES
    slab = jnp.zeros((1, lon_dev, LANES), jnp.float32)
    for e in range(in_chan - full):
        for r in range(rows_in):
            value = f_ref[r : r + 1, :, full + e : full + e + 1].astype(jnp.float32)
            slab = jnp.where(lane == e * rows_in + r, value, slab)
    for d in range(members):
        owner = place_ref[0] ^ d
        out = out_refs[d]
        for k in range(main):
            spot = pl.ds(pl.multiple_of((k * members + owner) * LANES, LANES), LANES)
            out[k * rows_in : (k + 1) * rows_in] = f_ref[:, :, spot]
        for i in range(group):
            row = None
            for g in range(pack):
                for k in range(rest):
                    tile = f_ref[
                        g * group + i, :, (base + k) * LANES : (base + k + 1) * LANES
                    ].astype(jnp.float32)
                    start = g * valid + k * sub
                    moved = pltpu.roll(tile, lax.rem(start - owner * sub + LANES, LANES), 1)
                    row = moved if row is None else jnp.where(lane[0] >= start, moved, row)
            out[main * rows_in + i] = row.astype(out.dtype)
        out[main * rows_in + group] = slab[0].astype(out.dtype)


def stage_kernel(w_ref, w_out):
    _, out_chan, in_chan = w_ref.shape
    full = in_chan // LANES * LANES
    w_out[:, :, full:] = jnp.zeros(
        (w_out.shape[0], w_out.shape[1], w_out.shape[2] - full), w_out.dtype
    )
    w_out[:, :out_chan, :in_chan] = w_ref[...]


def forward_kernel(
    plan, f_s, near_ref, far_ref, w_s, b_ref, o_ref, x_s, acc_s,
):
    taps, half, offset = plan.taps, plan.half, plan.offset
    lon_dev, halo = plan.lon_dev, 2 * plan.half
    rows_in, slots, wide = x_s.shape
    out_chan, in_chan = plan.out_chan, near_ref.shape[2]
    padded_out = w_s.shape[1]
    rows_out = rows_in - taps + 1
    points = rows_out * slots
    bulk = lon_dev // ROWS * ROWS
    full = in_chan // LANES * LANES
    x_s[:, :, full:] = jnp.zeros((rows_in, slots, wide - full), x_s.dtype)
    x_s[:, offset : offset + bulk, :in_chan] = f_s[:, :bulk, :]
    near = near_ref[...].astype(jnp.float32)
    far = far_ref[...].astype(jnp.float32)
    even = here()[2] == 0
    first = jnp.concatenate(
        [
            jnp.zeros((rows_in, offset - halo, in_chan), jnp.float32),
            jnp.where(even, far, near),
        ],
        axis=1,
    )
    x_s[:, :offset, :in_chan] = first.astype(x_s.dtype)
    tail = slots - offset - bulk
    final = jnp.concatenate(
        [
            f_s[:, bulk:, :].astype(jnp.float32),
            jnp.where(even, near, far),
            jnp.zeros((rows_in, tail - (lon_dev - bulk) - halo, in_chan), jnp.float32),
        ],
        axis=1,
    )
    x_s[:, offset + bulk :, :in_chan] = final.astype(x_s.dtype)
    for a in range(taps):
        part = lax.dot_general(
            w_s[a * taps : (a + 1) * taps].reshape(taps * padded_out, wide),
            x_s[a : a + rows_out].reshape(points, wide),
            NT,
            preferred_element_type=jnp.float32,
        )
        if a == 0:
            acc_s[...] = part
        else:
            acc_s[...] += part
    slot = lax.broadcasted_iota(jnp.int32, (1, points), 1) % slots
    inside = (slot >= offset - half) & (slot < offset + lon_dev + half)
    bias = column_of(b_ref, 0.0)
    for lo in range(0, padded_out, 2 * ROWS):
        rows = slice(lo, lo + 2 * ROWS)
        total = jnp.zeros((2 * ROWS, points), jnp.float32) + bias[rows]
        for b in range(taps):
            piece = acc_s[b * padded_out + lo : b * padded_out + lo + 2 * ROWS, :]
            shift = (half - b) % points
            total = total + (pltpu.roll(piece, shift, 1) if shift else piece)
        row = lo + lax.broadcasted_iota(jnp.int32, (2 * ROWS, 1), 0)
        keep = inside & (row < out_chan)
        o_ref[rows, :] = jnp.where(keep, total, 0.0).astype(o_ref.dtype)


def prep_kernel(plan, obs_ref, near_ref, far_ref, own_ref, *refs):
    truth_ref, own_out_ref, row_s = refs[-3:]
    refs = refs[:-3]
    own_out_ref[...] = own_ref[...]
    half, offset, padded_out = plan.half, plan.offset, plan.padded_out
    even = here()[2] == 0
    near, far = near_ref[...], far_ref[...]
    out_chan = obs_ref.shape[2]
    total_rows = obs_ref.shape[1]
    width = plan.points // total_rows
    per = LANES // width
    row_s[...] = jnp.zeros(row_s.shape, jnp.float32)
    for x in range(half):
        row_s[:, offset - half + x, :out_chan] = jnp.where(even, far[x], near[x])
        row_s[:, offset + plan.lon_dev + x, :out_chan] = jnp.where(even, near[x], far[x])
    for x in range(plan.lon_dev):
        row_s[:, offset + x, :out_chan] = obs_ref[x]
    for j in range(total_rows // per):
        tile = row_s[j * per : (j + 1) * per].reshape(LANES, LANES)
        truth_ref[:, j * LANES : (j + 1) * LANES] = jnp.transpose(tile)[:padded_out]
    members, main = plan.members, plan.main
    pack, valid, extras = plan.pack, plan.valid, plan.extras
    out_ref = refs[-1]
    _, rows_in, slots, _ = out_ref.shape
    lon_dev = plan.lon_dev
    bulk = lon_dev // ROWS * ROWS
    group = rows_in // pack
    lane = lax.broadcasted_iota(jnp.int32, (1, LANES), 1)
    out_ref[:, :, bulk:, :] = jnp.zeros(
        (members, rows_in, slots - bulk, out_ref.shape[3]), out_ref.dtype
    )
    for d in range(members):
        ref = refs[d]
        for k in range(main):
            out_ref[d, :, :lon_dev, k * LANES : (k + 1) * LANES] = ref[
                k * rows_in : (k + 1) * rows_in
            ]
        slab = ref[main * rows_in + group].astype(jnp.float32)
        for g in range(pack):
            for i in range(group):
                value = ref[main * rows_in + i].astype(jnp.float32)
                if g:
                    value = pltpu.roll(value, LANES - g * valid, 1)
                r = g * group + i
                for e in range(extras):
                    shift = (valid + e - (e * rows_in + r)) % LANES
                    moved = pltpu.roll(slab, shift, 1) if shift else slab
                    value = jnp.where(lane == valid + e, moved, value)
                value = jnp.where(lane == valid + extras, 1.0, value)
                out_ref[d, r, :lon_dev, main * LANES :] = value.astype(out_ref.dtype)


def split_bias(tile, row_high):
    row = lax.broadcasted_iota(jnp.int32, tile.shape, 0)
    size = tile.shape[0]
    total = jnp.where(row == row_high, tile + pltpu.roll(tile, size - 1, 0), tile)
    left = total - total.astype(jnp.bfloat16).astype(jnp.float32)
    return jnp.where(row == row_high + 1, pltpu.roll(left, 1, 0), total)


def fix_rows(plan, ref, index, piece, value_of):
    @pl.when(piece == 2 * plan.pairs - 1)
    def _():
        lo = plan.special_row
        tile = value_of(lo, lo + SPECIAL)
        ref[index, lo : lo + SPECIAL, :] = split_bias(tile, plan.bias_row).astype(ref.dtype)


def gradient_kernel(plan, *refs):
    members, taps, half = plan.members, plan.taps, plan.half
    out_chan, padded_out, points = plan.out_chan, plan.padded_out, plan.points
    main, pairs, pack, valid = plan.main, plan.pairs, plan.pack, plan.valid
    rows_out, size, extras = plan.rows_out, plan.half_rows, plan.extras
    per_half, special = plan.per_half, plan.special
    place_ref = here()
    y_refs = refs[:members]
    x_ref, obs_ref, wid_ref = refs[members : 3 + members]
    g_ref, score_ref, send_ref, keep_ref = refs[3 + members : 7 + members]
    g_s, gs_s, wide_s, packed_s = refs[7 + members :]
    step = 2 * LANES
    width_all = column_of(wid_ref, 1.0)
    for left in range(0, points, step):
        tally = jnp.zeros((ROWS, step), jnp.float32)
        for lo in range(0, padded_out, 2 * ROWS):
            rows = slice(lo, lo + 2 * ROWS)
            cols = slice(left, left + step)
            shape = (2 * ROWS, step)
            width = width_all[rows]
            inverse = 1.0 / (width * width)
            values = [y[rows, cols].astype(jnp.float32) for y in y_refs]
            target = obs_ref[rows, cols]
            pair_sum = jnp.full(shape, float(members), jnp.float32)
            pull = [jnp.zeros(shape, jnp.float32) for _ in values]
            for x in range(members):
                for y in range(x + 1, members):
                    spread = values[x] - values[y]
                    kernel_pair = jnp.exp(-0.5 * spread * spread * inverse)
                    pair_sum = pair_sum + 2.0 * kernel_pair
                    weighted = kernel_pair * spread
                    pull[x] = pull[x] + weighted
                    pull[y] = pull[y] - weighted
            obs_sum = jnp.zeros(shape, jnp.float32)
            for x in range(members):
                misfit = values[x] - target
                kernel_obs = jnp.exp(-0.5 * misfit * misfit * inverse)
                obs_sum = obs_sum + kernel_obs
                grad = inverse * (misfit * kernel_obs - pull[x] / members)
                g_s[x, rows, cols] = grad.astype(jnp.bfloat16)
            terms = pair_sum / (2.0 * members * members) - obs_sum / members
            row = lo + lax.broadcasted_iota(jnp.int32, (2 * ROWS, 1), 0)
            terms = jnp.where(row < out_chan, terms, 0.0)
            tally = tally + terms[:ROWS] + terms[ROWS:]
        score_ref[:, left : left + step] = jnp.sum(tally, axis=0, keepdims=True) / out_chan
    g_ref[...] = g_s[0]
    for x in range(members):
        for lo in range(0, padded_out, 2 * ROWS):
            grad = g_s[x, lo : lo + 2 * ROWS, :].astype(jnp.float32)
            for b in range(taps):
                shift = (b - half - plan.offset) % points
                moved = pltpu.roll(grad, shift, 1) if shift else grad
                start = b * padded_out + lo
                gs_s[x, start : start + 2 * ROWS, :] = moved.astype(jnp.bfloat16)
    tiles = main + 1
    split = size - special - SPECIAL
    for h in range(2):
        wide_s[:, h * size + special : (h + 1) * size, :] = jnp.zeros(
            (tiles, size - special, LANES), jnp.float32
        )
    for a in range(taps):
        total = None
        for x in range(members):
            part = lax.dot_general(
                gs_s[x],
                x_ref[x, a : a + rows_out].reshape(points, tiles * LANES),
                NN,
                preferred_element_type=jnp.float32,
            )
            total = part if total is None else total + part
        for b in range(taps):
            tap = a * taps + b
            block = total[b * padded_out : (b + 1) * padded_out]
            across = jnp.transpose(block[:, main * LANES :])
            if tap < 2 * per_half:
                h, i = tap // per_half, tap % per_half
                spans = [(0, padded_out, h * size + i * padded_out)]
                line = h * size + special + i * extras
            else:
                first = size - split
                spans = [(0, split, first), (split, padded_out, size + first)]
                line = size + special + per_half * extras
            for k in range(tiles):
                for lo, hi, at in spans:
                    wide_s[k, at : at + hi - lo, :] = block[lo:hi, k * LANES : (k + 1) * LANES]
            for e in range(extras):
                wide_s[0, line + e : line + e + 1, :padded_out] = across[valid + e : valid + e + 1]
            if a == 0 and b == half:
                line = size + special + plan.bias_row
                ones = valid + extras
                wide_s[0, line : line + 1, :padded_out] = across[ones : ones + 1]
    short = size // pack
    lane = lax.broadcasted_iota(jnp.int32, (1, LANES), 1)
    for h in range(2):
        packed = wide_s[main, h * size : h * size + short, :]
        for g in range(1, pack):
            at = h * size + g * short
            moved = pltpu.roll(wide_s[main, at : at + short, :], g * valid, 1)
            packed = jnp.where(lane >= g * valid, moved, packed)
        packed_s[h * short : (h + 1) * short, :] = packed
    pair, core = place_ref[1], place_ref[2]
    main_rows = size // pairs
    rest_rows = main_rows // pack
    for s in range(pairs):
        for out, side in ((keep_ref, core), (send_ref, 1 - core)):
            piece = 2 * (pair ^ s) + side
            at = 0
            for k in range(main):
                source = pl.ds(pl.multiple_of(piece * main_rows, main_rows), main_rows)
                out[s, at : at + main_rows, :] = wide_s[k, source, :].astype(out.dtype)
                at += main_rows
            source = pl.ds(pl.multiple_of(piece * rest_rows, rest_rows), rest_rows)
            out[s, at : at + rest_rows, :] = packed_s[source, :].astype(out.dtype)
        spot = 2 * size - main_rows
        fix_rows(
            plan, send_ref, s, 2 * (pair ^ s) + 1 - core,
            lambda lo, hi: wide_s[0, spot + lo : spot + hi, :]
            if main
            else packed_s[spot + lo : spot + hi, :],
        )


def core_add_kernel(plan, keep_ref, got_ref, mine_ref, *out_refs):
    place_ref = here()
    mine_ref[...] = keep_ref[0] + got_ref[0].astype(jnp.float32)
    pair, core = place_ref[1], place_ref[2]
    for s in range(1, plan.pairs):
        out = out_refs[s - 1]
        out[0] = (keep_ref[s] + got_ref[s].astype(jnp.float32)).astype(out.dtype)
        fix_rows(
            plan, out, 0, 2 * (pair ^ s) + core,
            lambda lo, hi: keep_ref[s, lo:hi, :] + got_ref[s, lo:hi, :].astype(jnp.float32),
        )


def pair_add_kernel(plan, factor, mine_ref, *refs):
    place_ref = here()
    out = refs[-1]

    def value(lo, hi):
        total = mine_ref[lo:hi, :]
        for ref in refs[:-1]:
            total = total + ref[0, lo:hi, :].astype(jnp.float32)
        return total * factor

    out[0] = value(0, mine_ref.shape[0]).astype(out.dtype)
    fix_rows(plan, out, 0, 2 * place_ref[1] + place_ref[2], value)


def out_grad_kernel(plan, g_ref, out_ref, row_s):
    lon_dev, offset = plan.lon_dev, plan.offset
    rows_out, out_chan = out_ref.shape[1:]
    width = plan.points // rows_out
    per = LANES // width
    padded_out = g_ref.shape[0]
    for j in range(rows_out // per):
        tile = g_ref[:, j * LANES : (j + 1) * LANES].astype(jnp.float32)
        tile = jnp.concatenate(
            [tile, jnp.zeros((LANES - padded_out, LANES), jnp.float32)], axis=0
        )
        row_s[j * per : (j + 1) * per] = jnp.transpose(tile).reshape(per, width, LANES)
    for x in range(lon_dev):
        out_ref[x] = row_s[:, offset + x, :out_chan].astype(out_ref.dtype)


def owned_kernel(plan, start_ref, score_ref, out_ref, row_s):
    lon_dev, offset, points = plan.lon_dev, plan.offset, plan.points
    rows_out = plan.rows_out
    width = points // rows_out
    capacity = out_ref.shape[1] // lon_dev
    member = here()[0]
    first = start_ref[0, member]
    count = start_ref[0, member + 1] - first
    lane = lax.broadcasted_iota(jnp.int32, (1, points), 1)
    row_s[...] = jnp.zeros(row_s.shape, jnp.float32)
    score = score_ref[...]
    for i in range(rows_out):
        moved = pltpu.roll(score, (points - i * width - offset) % points, 1)
        row_s[i : i + 1, :] = jnp.where(lane < lon_dev, moved, 0.0)[:, :LANES]
    reach = round_up(capacity * lon_dev, LANES)
    total = jnp.zeros((1, reach), jnp.float32)
    blank = jnp.zeros((1, reach - LANES), jnp.float32)
    for t in range(capacity):
        row = jnp.where(t < count, row_s[pl.ds(first + t, 1), :], 0.0)
        row = jnp.concatenate([row, blank], axis=1)
        total = total + (pltpu.roll(row, t * lon_dev, 1) if t else row)
    out_ref[...] = total[:, : capacity * lon_dev]


def assemble_kernel(plan, second, layout, final, *refs):
    members, main, rest = plan.members, plan.main, plan.rest
    out_chan, padded_out, pairs = plan.out_chan, plan.padded_out, plan.pairs
    pack, valid, sub = plan.pack, plan.valid, plan.sub
    size, extras, per_half = plan.half_rows, plan.extras, plan.per_half
    special = plan.special
    member, pair, core = here()
    piece_refs = refs[: len(layout)]
    refs = refs[len(layout) :]
    own_half = lax.div(pair, pairs // 2)
    this_half = 1 - own_half if second else own_half
    low = this_half == 0
    main_rows = size // pairs
    rest_rows = main_rows // pack
    split = size - special - SPECIAL
    begin = special + SPECIAL
    known_ref = carry_ref = None
    if second:
        carry_ref, _, *refs = refs
        if final == "late":
            known_ref, *refs = refs
    out_ref, other_ref, main_s, packed_s, main_stage, rest_stage, sems = refs
    if known_ref is not None:
        packed_s[...] = known_ref[:members]
    shown = []
    for d, _, _ in layout:
        if d not in shown:
            shown.append(d)
    for ref, (d, s, other) in zip(piece_refs, layout):
        side = 1 - core if other else core
        piece = lax.rem(2 * (pair ^ s) + side, pairs)
        row = 0
        for k in range(main):
            spot = pl.ds(pl.multiple_of(piece * main_rows, ROWS), main_rows)
            main_s[shown.index(d) * main + k, spot, :] = ref[0, row : row + main_rows, :].astype(
                jnp.float32
            )
            row += main_rows
        spot = pl.ds(pl.multiple_of(piece * rest_rows, ROWS), rest_rows)
        packed_s[member ^ d, spot, :] = ref[0, row : row + rest_rows, :].astype(jnp.float32)
    lines = packed_s[0, special:begin, :] if not main else None
    for at, d in enumerate(shown if main else ()):
        found = main_s[at * main, special:begin, :]
        if lines is None:
            lines = found if known_ref is None else known_ref[members, :SPECIAL, :]
        lines = jnp.where(member == d, found, lines)
    copies = []

    def emit(source, stage, lanes):
        spans = [(pl.ds(0, per_half), pl.ds(this_half * per_half, per_half))]
        if second:
            spans.append((pl.ds(per_half, 1), pl.ds(2 * per_half, 1)))
        for from_span, to_span in spans:
            copy = pltpu.make_async_copy(
                source.at[stage, from_span],
                out_ref.at[to_span, :, lanes],
                sems.at[len(copies)],
            )
            copy.start()
            copies.append(copy)

    def fill(stage_ref, stage, lanes, tile, block):
        for i in range(per_half):
            stage_ref[stage, i, :, lanes] = tile[i * padded_out : i * padded_out + out_chan]
        mine = tile[begin:size]
        if second:
            theirs = carry_ref[block, SPECIAL:, :]
            stage_ref[stage, per_half, :split, lanes] = jnp.where(low, mine, theirs)
            stage_ref[stage, per_half, split:, lanes] = jnp.where(low, theirs, mine)[
                : out_chan - split
            ]
        else:
            other_ref[block, SPECIAL:, :] = mine

    if not second:
        other_ref[:, :SPECIAL, :] = jnp.zeros(
            (other_ref.shape[0], SPECIAL, LANES), jnp.float32
        )
        other_ref[0, :SPECIAL, :] = lines
    for at, d in enumerate(shown if main else ()):
        for k in range(main):
            block = k * members + (member ^ d)
            fill(main_stage, at * main + k, slice(None), main_s[at * main + k], block)
            emit(
                main_stage,
                at * main + k,
                pl.ds(pl.multiple_of(block * LANES, LANES), LANES),
            )
    if final == "early":
        other_ref[:members] = packed_s[...]
        other_ref[members] = jnp.zeros(other_ref.shape[1:], jnp.float32)
        other_ref[members, :SPECIAL, :] = lines
    else:
        lane = lax.broadcasted_iota(jnp.int32, (1, LANES), 1)
        base = main * members
        for k in range(rest):
            tiles = []
            for g in range(pack):
                tile = None
                for owner in range(members):
                    shift = (owner * sub - g * valid - k * sub) % LANES
                    value = packed_s[owner]
                    if shift:
                        value = pltpu.roll(value, shift, 1)
                    tile = (
                        value if tile is None else jnp.where(lane >= owner * sub, value, tile)
                    )
                tiles.append(tile)
            tile = tiles[0] if pack == 1 else jnp.concatenate(tiles, axis=0)
            fill(rest_stage, 0, slice(k * LANES, (k + 1) * LANES), tile, base + k)
        blank = jnp.zeros((LANES - SPECIAL, LANES), jnp.float32)

        def put_columns(rows, first, count, tap):
            columns = jnp.transpose(jnp.concatenate([rows, blank], axis=0))
            for i in range(count):
                for e in range(extras):
                    at = first + i * extras + e
                    lanes = slice(rest * LANES + e, rest * LANES + e + 1)
                    rest_stage[0, tap + i, :, lanes] = columns[:out_chan, at : at + 1]

        put_columns(lines, 0, per_half, 0)
        if second:
            top = jnp.where(low, carry_ref[0, :SPECIAL, :], lines)
            put_columns(top, per_half * extras, 1, per_half)
            line = plan.bias_row
            other_ref[...] = (top[line : line + 1] + top[line + 1 : line + 2])[:, :out_chan]
        emit(rest_stage, 0, pl.ds(base * LANES, rest * LANES + extras))
    for copy in copies:
        copy.wait()


def body(fields, weight, out_bias, observed, widths, owner_start):
    _, in_chan, rows_in, lon_dev = fields.shape
    taps, _, out_chan, _ = weight.shape
    half = taps // 2
    halo = 2 * half
    members = lax.axis_size("member")
    lon_count = lax.axis_size("lon")
    pairs = lon_count // 2
    rows_out = rows_in - taps + 1
    offset = round_up(halo, ROWS)
    slots = round_up(offset + lon_dev + halo, 2 * ROWS)
    points = rows_out * slots
    padded_out = round_up(out_chan, 2 * ROWS)
    full_blocks = in_chan // LANES
    main, rest = full_blocks // members, full_blocks % members
    sub = LANES // members
    valid = rest * sub
    pack = LANES // valid if rows_in % (LANES // valid) == 0 else 1
    extras = in_chan - full_blocks * LANES
    stack = taps * padded_out
    total_taps = taps * taps
    per_half = total_taps // 2
    special = per_half * padded_out
    half_rows = round_up(
        special + SPECIAL + round_up(-(-out_chan // 2), ROWS), ROWS * pack * pairs
    )
    bias_row = (per_half + 1) * extras
    assert rest and total_taps % 2 and bias_row + 2 <= SPECIAL
    wide = round_up(in_chan, LANES)
    plan = types.SimpleNamespace(
        members=members, taps=taps, half=half, offset=offset, lon_dev=lon_dev, out_chan=out_chan,
        padded_out=padded_out, rows_out=rows_out, points=points, main=main, rest=rest, pairs=pairs,
        pack=pack, valid=valid, sub=sub, extras=extras, half_rows=half_rows, per_half=per_half,
        special=special, bias_row=bias_row,
        special_row=special - (pairs - 1) * (half_rows // pairs),
    )
    factor = 1.0 / math.sqrt(members * rows_out * lon_dev * lon_count)

    def swap_lon(value, d):
        return lax.ppermute(value, "lon", [(i, i ^ d) for i in range(lon_count)])

    def swap_far(value):
        step = [(i, (i + 1 if i % 2 else i - 1) % lon_count) for i in range(lon_count)]
        return lax.ppermute(value, "lon", step)

    def swap_member(value, d):
        return lax.ppermute(value, "member", [(i, i ^ d) for i in range(members)])

    any_space = pl.BlockSpec(memory_space=pl.ANY)
    field = jnp.transpose(fields[0], (1, 2, 0))
    packed_rows = main * rows_in + rows_in // pack + 1
    edge = jax.ShapeDtypeStruct((rows_in, halo, in_chan), jnp.bfloat16)
    seen = jnp.transpose(observed, (2, 1, 0))
    strip = jax.ShapeDtypeStruct((half, rows_out, out_chan), jnp.float32)
    near, far, *packed = pl.pallas_call(
        functools.partial(pack_kernel, plan),
        out_shape=[edge, edge]
        + [jax.ShapeDtypeStruct((packed_rows, lon_dev, LANES), jnp.bfloat16)] * members,
        in_specs=[vmem()],
        out_specs=[vmem()] * (members + 2),
        cost_estimate=cost(0, 4_000_000),
        compiler_params=limit(16),
        name="pack",
    )(field)
    far = swap_far(far)
    near = swap_lon(near, 1)
    traded = [packed[0]]
    for d in range(1, members):
        traded.append(swap_member(packed[d], d))

    seen_near, seen_far = pl.pallas_call(
        strips_kernel,
        out_shape=[strip, strip],
        in_specs=[vmem()],
        out_specs=[vmem()] * 2,
        cost_estimate=cost(0, 400_000),
        compiler_params=limit(4),
        name="strips",
    )(seen)
    seen_far = swap_far(seen_far)
    seen_near = swap_lon(seen_near, 1)
    weight_flat = weight.reshape(total_taps, out_chan, in_chan)
    w_all = pl.pallas_call(
        stage_kernel,
        out_shape=jax.ShapeDtypeStruct((total_taps, padded_out, wide), jnp.bfloat16),
        in_specs=[vmem()],
        out_specs=vmem(),
        cost_estimate=cost(0, 5_000_000),
        compiler_params=limit(8),
        name="stage",
    )(weight_flat)
    own_outputs = pl.pallas_call(
        functools.partial(forward_kernel, plan),
        out_shape=jax.ShapeDtypeStruct((padded_out, points), jnp.bfloat16),
        in_specs=[vmem()] * 5,
        out_specs=vmem(),
        scratch_shapes=[
            pltpu.VMEM((rows_in, slots, wide), jnp.bfloat16),
            pltpu.VMEM((stack, points), jnp.float32),
        ],
        cost_estimate=cost(2 * taps * stack * points * wide, 6_000_000),
        compiler_params=limit(20),
        name="forward",
    )(field, near, far, w_all, out_bias[None, :])
    outputs = [own_outputs]
    for d in range(1, members):
        outputs.append(swap_member(own_outputs, d))

    tiles = main + 1
    x_all, truth, own_copy = pl.pallas_call(
        functools.partial(prep_kernel, plan),
        out_shape=(
            jax.ShapeDtypeStruct((members, rows_in, slots, tiles * LANES), jnp.bfloat16),
            jax.ShapeDtypeStruct((padded_out, points), jnp.float32),
            jax.ShapeDtypeStruct((padded_out, points), jnp.bfloat16),
        ),
        in_specs=[vmem()] * (members + 4),
        out_specs=[vmem()] * 3,
        scratch_shapes=[pltpu.VMEM((rows_out, slots, LANES), jnp.float32)],
        cost_estimate=cost(0, 4_000_000),
        compiler_params=limit(20),
        name="prep",
    )(seen, seen_near, seen_far, own_outputs, *traded)
    outputs[0] = own_copy

    main_rows = half_rows // pairs
    piece_rows = main * main_rows + main_rows // pack
    piece = jax.ShapeDtypeStruct((1, piece_rows, LANES), jnp.bfloat16)
    grad_own, score, send, keep = pl.pallas_call(
        functools.partial(gradient_kernel, plan),
        out_shape=(
            jax.ShapeDtypeStruct((padded_out, points), jnp.bfloat16),
            jax.ShapeDtypeStruct((1, points), jnp.float32),
            jax.ShapeDtypeStruct((pairs, piece_rows, LANES), jnp.bfloat16),
            jax.ShapeDtypeStruct((pairs, piece_rows, LANES), jnp.float32),
        ),
        in_specs=[vmem()] * (members + 3),
        out_specs=[vmem()] * 4,
        scratch_shapes=[
            pltpu.VMEM((members, padded_out, points), jnp.bfloat16),
            pltpu.VMEM((members, stack, points), jnp.bfloat16),
            pltpu.VMEM((tiles, 2 * half_rows, LANES), jnp.float32),
            pltpu.VMEM((2 * half_rows // pack, LANES), jnp.float32),
        ],
        cost_estimate=cost(
            2 * taps * stack * points * members * tiles * LANES, 6_000_000, 1_000_000
        ),
        compiler_params=limit(32),
        name="gradient",
    )(*outputs, x_all, truth, widths[None, :])

    mine, *out_pieces = pl.pallas_call(
        functools.partial(core_add_kernel, plan),
        out_shape=[jax.ShapeDtypeStruct((piece_rows, LANES), jnp.float32)] + [piece] * (pairs - 1),
        in_specs=[vmem(), vmem()],
        out_specs=[vmem()] * pairs,
        cost_estimate=cost(0, 1_500_000),
        compiler_params=limit(16),
        name="core_add",
    )(keep, swap_lon(send, 1))
    got = []
    for at, value in enumerate(out_pieces, 1):
        got.append(swap_lon(value, 2 * at))
    final = pl.pallas_call(
        functools.partial(pair_add_kernel, plan, factor),
        out_shape=piece,
        in_specs=[vmem()] * pairs,
        out_specs=vmem(),
        cost_estimate=cost(0, 600_000),
        compiler_params=limit(16),
        name="pair_add",
    )(mine, *got)

    gathered = [final]
    for at in range(1, pairs):
        gathered.append(swap_lon(final, 2 * at))
    grad_shape = jax.ShapeDtypeStruct((total_taps, out_chan, in_chan), jnp.float32)
    blocks = full_blocks
    tail_rows = half_rows - special
    halves = []
    for second in range(2):
        group = range(second * pairs // 2, (second + 1) * pairs // 2)
        column = jnp.concatenate([gathered[s] for s in group])
        held = []
        for d in range(members):
            value = column
            if d:
                value = swap_member(column, d)
            held.append((d, (value, swap_lon(value, 1))))
        halves.append((group, held))
    rest_lanes = rest * LANES + extras
    short = half_rows // pack

    def assemble(second, final, held, extra_inputs, other_shape):
        group = halves[second][0]
        arrays, layout = [], []
        for d, both in held:
            for other, value in enumerate(both):
                arrays.append(value)
                layout += [(d, s, bool(other)) for s in group]
        count, each = len(arrays), len(group)
        stages = max(len(held) * main, 1)
        taps_held = per_half + second

        def kernel(*refs):
            pieces = [ref.at[pl.ds(at, 1)] for ref in refs[:count] for at in range(each)]
            assemble_kernel(plan, second, tuple(layout), final, *pieces, *refs[count:])

        specs = [vmem()] * count
        if second:
            specs += [vmem(), any_space] + [vmem()] * (len(extra_inputs) - 2)
        return pl.pallas_call(
            kernel,
            out_shape=[grad_shape, jax.ShapeDtypeStruct(other_shape, jnp.float32)],
            in_specs=specs,
            out_specs=[any_space, vmem()],
            scratch_shapes=[
                pltpu.VMEM((stages, half_rows, LANES), jnp.float32),
                pltpu.VMEM((members, short, LANES), jnp.float32),
                pltpu.VMEM((stages, taps_held, out_chan, LANES), jnp.float32),
                pltpu.VMEM((1, taps_held, out_chan, rest_lanes), jnp.float32),
                pltpu.SemaphoreType.DMA((2 * stages + 2,)),
            ],
            input_output_aliases={count + 1: 0} if second else {},
            cost_estimate=cost(0, 5_000_000),
            compiler_params=limit(24),
            name="assemble",
        )(*arrays, *extra_inputs)

    weight_grad, carry = assemble(0, "all", halves[0][1], (), (blocks, tail_rows, LANES))
    held = halves[1][1]
    if main:
        weight_grad, known = assemble(
            1, "early", held[:-1], (carry, weight_grad), (members + 1, short, LANES)
        )
        weight_grad, bias_out = assemble(
            1, "late", held[-1:], (carry, weight_grad, known), (1, out_chan)
        )
    else:
        weight_grad, bias_out = assemble(1, "all", held, (carry, weight_grad), (1, out_chan))
    bias_grad = bias_out[0]
    weight_grad = weight_grad.reshape(taps, taps, out_chan, in_chan)

    assert BLOCK == lon_dev
    out_grad = pl.pallas_call(
        functools.partial(out_grad_kernel, plan),
        out_shape=jax.ShapeDtypeStruct((lon_dev, rows_out, out_chan), jnp.bfloat16),
        in_specs=[vmem()],
        out_specs=vmem(),
        scratch_shapes=[pltpu.VMEM((rows_out, slots, LANES), jnp.float32)],
        cost_estimate=cost(0, 400_000),
        compiler_params=limit(8),
        name="out_grad",
    )(grad_own)
    out_grad = jnp.transpose(out_grad, (2, 1, 0))[None]
    capacity = max(2, 3 * rows_out // members)
    owned_score = pl.pallas_call(
        functools.partial(owned_kernel, plan),
        out_shape=jax.ShapeDtypeStruct((1, capacity * lon_dev), jnp.float32),
        in_specs=[smem(), vmem()],
        out_specs=vmem(),
        scratch_shapes=[pltpu.VMEM((round_up(rows_out + capacity, ROWS), LANES), jnp.float32)],
        cost_estimate=cost(0, 100_000),
        compiler_params=limit(8),
        name="owned",
    )(owner_start, score)
    owned_score = owned_score[None]
    return (out_grad, owned_score, weight_grad, bias_grad)


def solution(mesh):
    in_specs = (P("member", None, None, "lon"), P(), P(), P(None, None, "lon"), P(), P("lon", None))
    out_specs = (P("member", None, None, "lon"), P("lon", "member", None), P(), P())
    return jax.shard_map(body, mesh=mesh, in_specs=in_specs, out_specs=out_specs, check_vma=False)
```

```python
import functools
import math
import types

import jax
import jax.numpy as jnp
from jax import lax
from jax.experimental import pallas as pl
from jax.experimental.pallas import tpu as pltpu
from jax.sharding import PartitionSpec as P


BLOCK = 45
LANES = 128
ROWS = 8
SPECIAL = 16


NT = (((1,), (1,)), ((), ()))
NN = (((1,), (0,)), ((), ()))


def round_up(value, unit):
    return -(-value // unit) * unit


def vmem():
    return pl.BlockSpec(memory_space=pltpu.VMEM)


def smem():
    return pl.BlockSpec(memory_space=pltpu.SMEM)


def limit(mib):
    return pltpu.CompilerParams(vmem_limit_bytes=mib << 20)


def here():
    lon = lax.axis_index("lon")
    return lax.axis_index("member"), lax.div(lon, 2), lax.rem(lon, 2)


def cost(flops, moved, special=0):
    return pl.CostEstimate(flops=flops, bytes_accessed=moved, transcendentals=special)


def column_of(row_ref, fill):
    count = row_ref.shape[1]
    row = jnp.concatenate(
        [row_ref[...], jnp.full((1, LANES - count), fill, jnp.float32)], axis=1
    )
    return jnp.transpose(jnp.broadcast_to(row, (LANES, LANES)))[:, :1]


def strips_kernel(seen_ref, near_ref, far_ref):
    even = here()[2] == 0
    width = near_ref.shape[0]
    start = seen_ref[:width]
    end = seen_ref[seen_ref.shape[0] - width :]
    far_ref[...] = jnp.where(even, start, end)
    near_ref[...] = jnp.where(even, end, start)


def pack_kernel(plan, f_ref, near_ref, far_ref, *out_refs):
    members, main, rest = plan.members, plan.main, plan.rest
    pack, valid, sub = plan.pack, plan.valid, plan.sub
    rows_in, lon_dev, in_chan = f_ref.shape
    place_ref = here()
    halo = 2 * plan.half
    even = place_ref[2] == 0
    start_edge = f_ref[:, :halo, :].astype(jnp.float32)
    final = (lon_dev - halo) // ROWS * ROWS
    end_edge = f_ref[:, final:, :].astype(jnp.float32)[:, lon_dev - halo - final :]
    far_ref[...] = jnp.where(even, start_edge, end_edge).astype(far_ref.dtype)
    near_ref[...] = jnp.where(even, end_edge, start_edge).astype(near_ref.dtype)
    group = rows_in // pack
    base = main * members
    lane = lax.broadcasted_iota(jnp.int32, (1, 1, LANES), 2)
    full = (base + rest) * LANES
    slab = jnp.zeros((1, lon_dev, LANES), jnp.float32)
    for e in range(in_chan - full):
        for r in range(rows_in):
            value = f_ref[r : r + 1, :, full + e : full + e + 1].astype(jnp.float32)
            slab = jnp.where(lane == e * rows_in + r, value, slab)
    for d in range(members):
        owner = place_ref[0] ^ d
        out = out_refs[d]
        for k in range(main):
            spot = pl.ds(pl.multiple_of((k * members + owner) * LANES, LANES), LANES)
            out[k * rows_in : (k + 1) * rows_in] = f_ref[:, :, spot]
        for i in range(group):
            row = None
            for g in range(pack):
                for k in range(rest):
                    tile = f_ref[
                        g * group + i, :, (base + k) * LANES : (base + k + 1) * LANES
                    ].astype(jnp.float32)
                    start = g * valid + k * sub
                    moved = pltpu.roll(tile, lax.rem(start - owner * sub + LANES, LANES), 1)
                    row = moved if row is None else jnp.where(lane[0] >= start, moved, row)
            out[main * rows_in + i] = row.astype(out.dtype)
        out[main * rows_in + group] = slab[0].astype(out.dtype)


def stage_kernel(w_ref, w_out):
    _, out_chan, in_chan = w_ref.shape
    full = in_chan // LANES * LANES
    w_out[:, :, full:] = jnp.zeros(
        (w_out.shape[0], w_out.shape[1], w_out.shape[2] - full), w_out.dtype
    )
    w_out[:, :out_chan, :in_chan] = w_ref[...]


def forward_kernel(
    plan, f_s, near_ref, far_ref, w_s, b_ref, o_ref, x_s, acc_s,
):
    taps, half, offset = plan.taps, plan.half, plan.offset
    lon_dev, halo = plan.lon_dev, 2 * plan.half
    rows_in, slots, wide = x_s.shape
    out_chan, in_chan = plan.out_chan, near_ref.shape[2]
    padded_out = w_s.shape[1]
    rows_out = rows_in - taps + 1
    points = rows_out * slots
    bulk = lon_dev // ROWS * ROWS
    full = in_chan // LANES * LANES
    x_s[:, :, full:] = jnp.zeros((rows_in, slots, wide - full), x_s.dtype)
    x_s[:, offset : offset + bulk, :in_chan] = f_s[:, :bulk, :]
    near = near_ref[...].astype(jnp.float32)
    far = far_ref[...].astype(jnp.float32)
    even = here()[2] == 0
    first = jnp.concatenate(
        [
            jnp.zeros((rows_in, offset - halo, in_chan), jnp.float32),
            jnp.where(even, far, near),
        ],
        axis=1,
    )
    x_s[:, :offset, :in_chan] = first.astype(x_s.dtype)
    tail = slots - offset - bulk
    final = jnp.concatenate(
        [
            f_s[:, bulk:, :].astype(jnp.float32),
            jnp.where(even, near, far),
            jnp.zeros((rows_in, tail - (lon_dev - bulk) - halo, in_chan), jnp.float32),
        ],
        axis=1,
    )
    x_s[:, offset + bulk :, :in_chan] = final.astype(x_s.dtype)
    for a in range(taps):
        part = lax.dot_general(
            w_s[a * taps : (a + 1) * taps].reshape(taps * padded_out, wide),
            x_s[a : a + rows_out].reshape(points, wide),
            NT,
            preferred_element_type=jnp.float32,
        )
        if a == 0:
            acc_s[...] = part
        else:
            acc_s[...] += part
    slot = lax.broadcasted_iota(jnp.int32, (1, points), 1) % slots
    inside = (slot >= offset - half) & (slot < offset + lon_dev + half)
    bias = column_of(b_ref, 0.0)
    for lo in range(0, padded_out, 2 * ROWS):
        rows = slice(lo, lo + 2 * ROWS)
        total = jnp.zeros((2 * ROWS, points), jnp.float32) + bias[rows]
        for b in range(taps):
            piece = acc_s[b * padded_out + lo : b * padded_out + lo + 2 * ROWS, :]
            shift = (half - b) % points
            total = total + (pltpu.roll(piece, shift, 1) if shift else piece)
        row = lo + lax.broadcasted_iota(jnp.int32, (2 * ROWS, 1), 0)
        keep = inside & (row < out_chan)
        o_ref[rows, :] = jnp.where(keep, total, 0.0).astype(o_ref.dtype)


def prep_kernel(plan, obs_ref, near_ref, far_ref, own_ref, *refs):
    even_out, odd_out, truth_ref, own_out_ref, row_s = refs[-5:]
    refs = refs[:-5]
    own_out_ref[...] = own_ref[...]
    half, offset, padded_out = plan.half, plan.offset, plan.padded_out
    even = here()[2] == 0
    near, far = near_ref[...], far_ref[...]
    out_chan = obs_ref.shape[2]
    total_rows = obs_ref.shape[1]
    width = plan.points // total_rows
    per = LANES // width
    row_s[...] = jnp.zeros(row_s.shape, jnp.float32)
    for x in range(half):
        row_s[:, offset - half + x, :out_chan] = jnp.where(even, far[x], near[x])
        row_s[:, offset + plan.lon_dev + x, :out_chan] = jnp.where(even, near[x], far[x])
    for x in range(plan.lon_dev):
        row_s[:, offset + x, :out_chan] = obs_ref[x]
    for j in range(total_rows // per):
        tile = row_s[j * per : (j + 1) * per].reshape(LANES, LANES)
        truth_ref[:, j * LANES : (j + 1) * LANES] = jnp.transpose(tile)[:padded_out]
    members, main = plan.members, plan.main
    pack, valid, extras = plan.pack, plan.valid, plan.extras
    rows_in, slots, lon_dev = plan.rows_in, plan.slots, plan.lon_dev
    bulk = lon_dev // ROWS * ROWS
    group = rows_in // pack
    lane = lax.broadcasted_iota(jnp.int32, (1, LANES), 1)
    for out in (even_out, odd_out):
        for first in range(0, LANES, slots):
            out[:, :, first + bulk : first + slots, :] = jnp.zeros(
                out.shape[:2] + (slots - bulk, out.shape[3]), out.dtype
            )

    def put(d, r, lanes, value):
        even_out[r // per, d, r % per * slots : r % per * slots + lon_dev, lanes] = value
        if 0 < r <= per * odd_out.shape[0]:
            at = (r - 1) % per * slots
            odd_out[(r - 1) // per, d, at : at + lon_dev, lanes] = value

    for d in range(members):
        ref = refs[d]
        for k in range(main):
            for r in range(rows_in):
                put(d, r, slice(k * LANES, (k + 1) * LANES), ref[k * rows_in + r])
        slab = ref[main * rows_in + group].astype(jnp.float32)
        for g in range(pack):
            for i in range(group):
                value = ref[main * rows_in + i].astype(jnp.float32)
                if g:
                    value = pltpu.roll(value, LANES - g * valid, 1)
                r = g * group + i
                for e in range(extras):
                    shift = (valid + e - (e * rows_in + r)) % LANES
                    moved = pltpu.roll(slab, shift, 1) if shift else slab
                    value = jnp.where(lane == valid + e, moved, value)
                value = jnp.where(lane == valid + extras, 1.0, value)
                put(
                    d, r, slice(main * LANES, (main + 1) * LANES), value.astype(even_out.dtype)
                )


def split_bias(tile, row_high):
    row = lax.broadcasted_iota(jnp.int32, tile.shape, 0)
    size = tile.shape[0]
    total = jnp.where(row == row_high, tile + pltpu.roll(tile, size - 1, 0), tile)
    left = total - total.astype(jnp.bfloat16).astype(jnp.float32)
    return jnp.where(row == row_high + 1, pltpu.roll(left, 1, 0), total)


def fix_rows(plan, ref, index, piece, value_of):
    @pl.when(piece == 2 * plan.pairs - 1)
    def _():
        lo = plan.special_row
        tile = value_of(lo, lo + SPECIAL)
        ref[index, lo : lo + SPECIAL, :] = split_bias(tile, plan.bias_row).astype(ref.dtype)


def gradient_kernel(plan, *refs):
    members, taps, half = plan.members, plan.taps, plan.half
    out_chan, padded_out, points = plan.out_chan, plan.padded_out, plan.points
    main, pairs, pack, valid = plan.main, plan.pairs, plan.pack, plan.valid
    rows_out, size, extras = plan.rows_out, plan.half_rows, plan.extras
    per_half, special = plan.per_half, plan.special
    place_ref = here()
    y_refs = refs[:members]
    even_ref, odd_ref, obs_ref, wid_ref = refs[members : 4 + members]
    g_ref, score_ref, send_ref, keep_ref = refs[4 + members : 8 + members]
    g_s, gs_s, wide_s, packed_s = refs[8 + members :]
    step = 2 * LANES
    width_all = column_of(wid_ref, 1.0)
    for left in range(0, points, step):
        tally = jnp.zeros((ROWS, step), jnp.float32)
        for lo in range(0, padded_out, 2 * ROWS):
            rows = slice(lo, lo + 2 * ROWS)
            cols = slice(left, left + step)
            shape = (2 * ROWS, step)
            width = width_all[rows]
            inverse = 1.0 / (width * width)
            scale = (-0.5 * math.log2(math.e)) * inverse
            values = [y[rows, cols].astype(jnp.float32) for y in y_refs]
            target = obs_ref[rows, cols]
            pair_sum = jnp.full(shape, 0.5 * members, jnp.float32)
            pull = [jnp.zeros(shape, jnp.float32) for _ in values]
            for x in range(members):
                for y in range(x + 1, members):
                    spread = values[x] - values[y]
                    kernel_pair = jnp.exp2(spread * spread * scale)
                    pair_sum = pair_sum + kernel_pair
                    weighted = kernel_pair * spread
                    pull[x] = pull[x] + weighted
                    pull[y] = pull[y] - weighted
            obs_sum = jnp.zeros(shape, jnp.float32)
            for x in range(members):
                misfit = values[x] - target
                kernel_obs = jnp.exp2(misfit * misfit * scale)
                obs_sum = obs_sum + kernel_obs
                grad = inverse * (misfit * kernel_obs - pull[x] * (1.0 / members))
                g_s[x, rows, cols] = grad.astype(jnp.bfloat16)
            terms = pair_sum * (1.0 / (members * members)) - obs_sum * (1.0 / members)
            row = lo + lax.broadcasted_iota(jnp.int32, (2 * ROWS, 1), 0)
            terms = jnp.where(row < out_chan, terms, 0.0)
            tally = tally + terms[:ROWS] + terms[ROWS:]
        score_ref[:, left : left + step] = jnp.sum(tally, axis=0, keepdims=True) / out_chan
    g_ref[...] = g_s[0]
    for x in range(members):
        for lo in range(0, padded_out, 2 * ROWS):
            grad = g_s[x, lo : lo + 2 * ROWS, :].astype(jnp.float32)
            for b in range(taps):
                shift = (b - half - plan.offset) % points
                moved = pltpu.roll(grad, shift, 1) if shift else grad
                start = b * padded_out + lo
                moved = moved.astype(jnp.bfloat16)
                for t in range(points // LANES):
                    lanes = slice((t * members + x) * LANES, (t * members + x + 1) * LANES)
                    gs_s[start : start + 2 * ROWS, lanes] = moved[:, t * LANES : (t + 1) * LANES]
    tiles = main + 1
    split = size - special - SPECIAL
    for h in range(2):
        wide_s[:, h * size + special : (h + 1) * size, :] = jnp.zeros(
            (tiles, size - special, LANES), jnp.float32
        )
    for a in range(taps):
        x_ref = odd_ref if a % 2 else even_ref
        total = lax.dot_general(
            gs_s[...],
            x_ref[a // 2 : (a + rows_out) // 2].reshape(points * members, tiles * LANES),
            NN,
            preferred_element_type=jnp.float32,
        )
        for b in range(taps):
            tap = a * taps + b
            block = total[b * padded_out : (b + 1) * padded_out]
            across = jnp.transpose(block[:, main * LANES :])
            if tap < 2 * per_half:
                h, i = tap // per_half, tap % per_half
                spans = [(0, padded_out, h * size + i * padded_out)]
                line = h * size + special + i * extras
            else:
                first = size - split
                spans = [(0, split, first), (split, padded_out, size + first)]
                line = size + special + per_half * extras
            for k in range(tiles):
                for lo, hi, at in spans:
                    wide_s[k, at : at + hi - lo, :] = block[lo:hi, k * LANES : (k + 1) * LANES]
            for e in range(extras):
                wide_s[0, line + e : line + e + 1, :padded_out] = across[valid + e : valid + e + 1]
            if a == 0 and b == half:
                line = size + special + plan.bias_row
                ones = valid + extras
                wide_s[0, line : line + 1, :padded_out] = across[ones : ones + 1]
    short = size // pack
    lane = lax.broadcasted_iota(jnp.int32, (1, LANES), 1)
    for h in range(2):
        packed = wide_s[main, h * size : h * size + short, :]
        for g in range(1, pack):
            at = h * size + g * short
            moved = pltpu.roll(wide_s[main, at : at + short, :], g * valid, 1)
            packed = jnp.where(lane >= g * valid, moved, packed)
        packed_s[h * short : (h + 1) * short, :] = packed
    pair, core = place_ref[1], place_ref[2]
    main_rows = size // pairs
    rest_rows = main_rows // pack
    for s in range(pairs):
        for out, side in ((keep_ref, core), (send_ref, 1 - core)):
            piece = 2 * (pair ^ s) + side
            at = 0
            for k in range(main):
                source = pl.ds(pl.multiple_of(piece * main_rows, main_rows), main_rows)
                out[s, at : at + main_rows, :] = wide_s[k, source, :].astype(out.dtype)
                at += main_rows
            source = pl.ds(pl.multiple_of(piece * rest_rows, rest_rows), rest_rows)
            out[s, at : at + rest_rows, :] = packed_s[source, :].astype(out.dtype)
        spot = 2 * size - main_rows
        fix_rows(
            plan, send_ref, s, 2 * (pair ^ s) + 1 - core,
            lambda lo, hi: wide_s[0, spot + lo : spot + hi, :]
            if main
            else packed_s[spot + lo : spot + hi, :],
        )


def core_add_kernel(plan, keep_ref, got_ref, mine_ref, *out_refs):
    place_ref = here()
    mine_ref[...] = keep_ref[0] + got_ref[0].astype(jnp.float32)
    pair, core = place_ref[1], place_ref[2]
    for s in range(1, plan.pairs):
        out = out_refs[s - 1]
        out[0] = (keep_ref[s] + got_ref[s].astype(jnp.float32)).astype(out.dtype)
        fix_rows(
            plan, out, 0, 2 * (pair ^ s) + core,
            lambda lo, hi: keep_ref[s, lo:hi, :] + got_ref[s, lo:hi, :].astype(jnp.float32),
        )


def pair_add_kernel(plan, factor, mine_ref, *refs):
    place_ref = here()
    out = refs[-1]

    def value(lo, hi):
        total = mine_ref[lo:hi, :]
        for ref in refs[:-1]:
            total = total + ref[0, lo:hi, :].astype(jnp.float32)
        return total * factor

    out[0] = value(0, mine_ref.shape[0]).astype(out.dtype)
    fix_rows(plan, out, 0, 2 * place_ref[1] + place_ref[2], value)


def out_grad_kernel(plan, g_ref, out_ref, row_s):
    lon_dev, offset = plan.lon_dev, plan.offset
    rows_out, out_chan = out_ref.shape[1:]
    width = plan.points // rows_out
    per = LANES // width
    padded_out = g_ref.shape[0]
    for j in range(rows_out // per):
        tile = g_ref[:, j * LANES : (j + 1) * LANES].astype(jnp.float32)
        tile = jnp.concatenate(
            [tile, jnp.zeros((LANES - padded_out, LANES), jnp.float32)], axis=0
        )
        row_s[j * per : (j + 1) * per] = jnp.transpose(tile).reshape(per, width, LANES)
    for x in range(lon_dev):
        out_ref[x] = row_s[:, offset + x, :out_chan].astype(out_ref.dtype)


def owned_kernel(plan, start_ref, score_ref, out_ref, row_s):
    lon_dev, offset, points = plan.lon_dev, plan.offset, plan.points
    rows_out = plan.rows_out
    width = points // rows_out
    capacity = out_ref.shape[1] // lon_dev
    member = here()[0]
    first = start_ref[0, member]
    count = start_ref[0, member + 1] - first
    lane = lax.broadcasted_iota(jnp.int32, (1, points), 1)
    row_s[...] = jnp.zeros(row_s.shape, jnp.float32)
    score = score_ref[...]
    for i in range(rows_out):
        moved = pltpu.roll(score, (points - i * width - offset) % points, 1)
        row_s[i : i + 1, :] = jnp.where(lane < lon_dev, moved, 0.0)[:, :LANES]
    reach = round_up(capacity * lon_dev, LANES)
    total = jnp.zeros((1, reach), jnp.float32)
    blank = jnp.zeros((1, reach - LANES), jnp.float32)
    for t in range(capacity):
        row = jnp.where(t < count, row_s[pl.ds(first + t, 1), :], 0.0)
        row = jnp.concatenate([row, blank], axis=1)
        total = total + (pltpu.roll(row, t * lon_dev, 1) if t else row)
    out_ref[...] = total[:, : capacity * lon_dev]


def assemble_kernel(plan, second, layout, final, *refs):
    members, main, rest = plan.members, plan.main, plan.rest
    out_chan, padded_out, pairs = plan.out_chan, plan.padded_out, plan.pairs
    pack, valid, sub = plan.pack, plan.valid, plan.sub
    size, extras, per_half = plan.half_rows, plan.extras, plan.per_half
    special = plan.special
    member, pair, core = here()
    piece_refs = refs[: len(layout)]
    refs = refs[len(layout) :]
    own_half = lax.div(pair, pairs // 2)
    this_half = 1 - own_half if second else own_half
    low = this_half == 0
    main_rows = size // pairs
    rest_rows = main_rows // pack
    split = size - special - SPECIAL
    begin = special + SPECIAL
    known_ref = carry_ref = None
    if second:
        carry_ref, _, *refs = refs
        if final == "late":
            known_ref, *refs = refs
    out_ref, other_ref, main_s, packed_s, main_stage, rest_stage, sems = refs
    if known_ref is not None:
        packed_s[...] = known_ref[:members]
    shown = []
    for d, _, _ in layout:
        if d not in shown:
            shown.append(d)
    for ref, (d, s, other) in zip(piece_refs, layout):
        side = 1 - core if other else core
        piece = lax.rem(2 * (pair ^ s) + side, pairs)
        row = 0
        for k in range(main):
            spot = pl.ds(pl.multiple_of(piece * main_rows, ROWS), main_rows)
            main_s[shown.index(d) * main + k, spot, :] = ref[0, row : row + main_rows, :].astype(
                jnp.float32
            )
            row += main_rows
        spot = pl.ds(pl.multiple_of(piece * rest_rows, ROWS), rest_rows)
        packed_s[member ^ d, spot, :] = ref[0, row : row + rest_rows, :].astype(jnp.float32)
    lines = packed_s[0, special:begin, :] if not main else None
    for at, d in enumerate(shown if main else ()):
        found = main_s[at * main, special:begin, :]
        if lines is None:
            lines = found if known_ref is None else known_ref[members, :SPECIAL, :]
        lines = jnp.where(member == d, found, lines)
    copies = []

    def emit(source, stage, lanes):
        spans = [(pl.ds(0, per_half), pl.ds(this_half * per_half, per_half))]
        if second:
            spans.append((pl.ds(per_half, 1), pl.ds(2 * per_half, 1)))
        for from_span, to_span in spans:
            copy = pltpu.make_async_copy(
                source.at[stage, from_span],
                out_ref.at[to_span, :, lanes],
                sems.at[len(copies)],
            )
            copy.start()
            copies.append(copy)

    def fill(stage_ref, stage, lanes, tile, block):
        for i in range(per_half):
            stage_ref[stage, i, :, lanes] = tile[i * padded_out : i * padded_out + out_chan]
        mine = tile[begin:size]
        if second:
            theirs = carry_ref[block, SPECIAL:, :]
            stage_ref[stage, per_half, :split, lanes] = jnp.where(low, mine, theirs)
            stage_ref[stage, per_half, split:, lanes] = jnp.where(low, theirs, mine)[
                : out_chan - split
            ]
        else:
            other_ref[block, SPECIAL:, :] = mine

    if not second:
        other_ref[:, :SPECIAL, :] = jnp.zeros(
            (other_ref.shape[0], SPECIAL, LANES), jnp.float32
        )
        other_ref[0, :SPECIAL, :] = lines
    for at, d in enumerate(shown if main else ()):
        for k in range(main):
            block = k * members + (member ^ d)
            fill(main_stage, at * main + k, slice(None), main_s[at * main + k], block)
            emit(
                main_stage,
                at * main + k,
                pl.ds(pl.multiple_of(block * LANES, LANES), LANES),
            )
    if final == "early":
        other_ref[:members] = packed_s[...]
        other_ref[members] = jnp.zeros(other_ref.shape[1:], jnp.float32)
        other_ref[members, :SPECIAL, :] = lines
    else:
        lane = lax.broadcasted_iota(jnp.int32, (1, LANES), 1)
        base = main * members
        for k in range(rest):
            tiles = []
            for g in range(pack):
                tile = None
                for owner in range(members):
                    shift = (owner * sub - g * valid - k * sub) % LANES
                    value = packed_s[owner]
                    if shift:
                        value = pltpu.roll(value, shift, 1)
                    tile = (
                        value if tile is None else jnp.where(lane >= owner * sub, value, tile)
                    )
                tiles.append(tile)
            tile = tiles[0] if pack == 1 else jnp.concatenate(tiles, axis=0)
            fill(rest_stage, 0, slice(k * LANES, (k + 1) * LANES), tile, base + k)
        blank = jnp.zeros((LANES - SPECIAL, LANES), jnp.float32)

        def put_columns(rows, first, count, tap):
            columns = jnp.transpose(jnp.concatenate([rows, blank], axis=0))
            for i in range(count):
                for e in range(extras):
                    at = first + i * extras + e
                    lanes = slice(rest * LANES + e, rest * LANES + e + 1)
                    rest_stage[0, tap + i, :, lanes] = columns[:out_chan, at : at + 1]

        put_columns(lines, 0, per_half, 0)
        if second:
            top = jnp.where(low, carry_ref[0, :SPECIAL, :], lines)
            put_columns(top, per_half * extras, 1, per_half)
            line = plan.bias_row
            other_ref[...] = (top[line : line + 1] + top[line + 1 : line + 2])[:, :out_chan]
        emit(rest_stage, 0, pl.ds(base * LANES, rest * LANES + extras))
    for copy in copies:
        copy.wait()


def body(fields, weight, out_bias, observed, widths, owner_start):
    _, in_chan, rows_in, lon_dev = fields.shape
    taps, _, out_chan, _ = weight.shape
    half = taps // 2
    halo = 2 * half
    members = lax.axis_size("member")
    lon_count = lax.axis_size("lon")
    pairs = lon_count // 2
    rows_out = rows_in - taps + 1
    offset = round_up(halo, ROWS)
    slots = round_up(offset + lon_dev + halo, 2 * ROWS)
    points = rows_out * slots
    padded_out = round_up(out_chan, 2 * ROWS)
    full_blocks = in_chan // LANES
    main, rest = full_blocks // members, full_blocks % members
    sub = LANES // members
    valid = rest * sub
    pack = LANES // valid if rows_in % (LANES // valid) == 0 else 1
    extras = in_chan - full_blocks * LANES
    stack = taps * padded_out
    total_taps = taps * taps
    per_half = total_taps // 2
    special = per_half * padded_out
    half_rows = round_up(
        special + SPECIAL + round_up(-(-out_chan // 2), ROWS), ROWS * pack * pairs
    )
    bias_row = (per_half + 1) * extras
    assert rest and total_taps % 2 and bias_row + 2 <= SPECIAL
    assert 2 * slots == LANES and rows_in % 2 == 0
    wide = round_up(in_chan, LANES)
    plan = types.SimpleNamespace(
        members=members, taps=taps, half=half, offset=offset, lon_dev=lon_dev, out_chan=out_chan,
        padded_out=padded_out, rows_out=rows_out, points=points, main=main, rest=rest, pairs=pairs,
        pack=pack, valid=valid, sub=sub, extras=extras, half_rows=half_rows, per_half=per_half,
        special=special, bias_row=bias_row, rows_in=rows_in, slots=slots,
        special_row=special - (pairs - 1) * (half_rows // pairs),
    )
    factor = 1.0 / math.sqrt(members * rows_out * lon_dev * lon_count)

    def swap_lon(value, d):
        return lax.ppermute(value, "lon", [(i, i ^ d) for i in range(lon_count)])

    def swap_far(value):
        step = [(i, (i + 1 if i % 2 else i - 1) % lon_count) for i in range(lon_count)]
        return lax.ppermute(value, "lon", step)

    def swap_member(value, d):
        return lax.ppermute(value, "member", [(i, i ^ d) for i in range(members)])

    any_space = pl.BlockSpec(memory_space=pl.ANY)
    field = jnp.transpose(fields[0], (1, 2, 0))
    packed_rows = main * rows_in + rows_in // pack + 1
    edge = jax.ShapeDtypeStruct((rows_in, halo, in_chan), jnp.bfloat16)
    seen = jnp.transpose(observed, (2, 1, 0))
    strip = jax.ShapeDtypeStruct((half, rows_out, out_chan), jnp.float32)
    near, far, *packed = pl.pallas_call(
        functools.partial(pack_kernel, plan),
        out_shape=[edge, edge]
        + [jax.ShapeDtypeStruct((packed_rows, lon_dev, LANES), jnp.bfloat16)] * members,
        in_specs=[vmem()],
        out_specs=[vmem()] * (members + 2),
        cost_estimate=cost(0, 4_000_000),
        compiler_params=limit(16),
        name="pack",
    )(field)
    far = swap_far(far)
    near = swap_lon(near, 1)
    traded = [packed[0]]
    for d in range(1, members):
        traded.append(swap_member(packed[d], d))

    seen_near, seen_far = pl.pallas_call(
        strips_kernel,
        out_shape=[strip, strip],
        in_specs=[vmem()],
        out_specs=[vmem()] * 2,
        cost_estimate=cost(0, 400_000),
        compiler_params=limit(4),
        name="strips",
    )(seen)
    seen_far = swap_far(seen_far)
    seen_near = swap_lon(seen_near, 1)
    weight_flat = weight.reshape(total_taps, out_chan, in_chan)
    w_all = pl.pallas_call(
        stage_kernel,
        out_shape=jax.ShapeDtypeStruct((total_taps, padded_out, wide), jnp.bfloat16),
        in_specs=[vmem()],
        out_specs=vmem(),
        cost_estimate=cost(0, 5_000_000),
        compiler_params=limit(8),
        name="stage",
    )(weight_flat)
    own_outputs = pl.pallas_call(
        functools.partial(forward_kernel, plan),
        out_shape=jax.ShapeDtypeStruct((padded_out, points), jnp.bfloat16),
        in_specs=[vmem()] * 5,
        out_specs=vmem(),
        scratch_shapes=[
            pltpu.VMEM((rows_in, slots, wide), jnp.bfloat16),
            pltpu.VMEM((stack, points), jnp.float32),
        ],
        cost_estimate=cost(2 * taps * stack * points * wide, 6_000_000),
        compiler_params=limit(20),
        name="forward",
    )(field, near, far, w_all, out_bias[None, :])
    outputs = [own_outputs]
    for d in range(1, members):
        outputs.append(swap_member(own_outputs, d))

    tiles = main + 1
    x_even, x_odd, truth, own_copy = pl.pallas_call(
        functools.partial(prep_kernel, plan),
        out_shape=(
            jax.ShapeDtypeStruct((rows_in // 2, members, LANES, tiles * LANES), jnp.bfloat16),
            jax.ShapeDtypeStruct(((rows_in - 2) // 2, members, LANES, tiles * LANES), jnp.bfloat16),
            jax.ShapeDtypeStruct((padded_out, points), jnp.float32),
            jax.ShapeDtypeStruct((padded_out, points), jnp.bfloat16),
        ),
        in_specs=[vmem()] * (members + 4),
        out_specs=[vmem()] * 4,
        scratch_shapes=[pltpu.VMEM((rows_out, slots, LANES), jnp.float32)],
        cost_estimate=cost(0, 4_000_000),
        compiler_params=limit(20),
        name="prep",
    )(seen, seen_near, seen_far, own_outputs, *traded)
    outputs[0] = own_copy

    main_rows = half_rows // pairs
    piece_rows = main * main_rows + main_rows // pack
    piece = jax.ShapeDtypeStruct((1, piece_rows, LANES), jnp.bfloat16)
    grad_own, score, send, keep = pl.pallas_call(
        functools.partial(gradient_kernel, plan),
        out_shape=(
            jax.ShapeDtypeStruct((padded_out, points), jnp.bfloat16),
            jax.ShapeDtypeStruct((1, points), jnp.float32),
            jax.ShapeDtypeStruct((pairs, piece_rows, LANES), jnp.bfloat16),
            jax.ShapeDtypeStruct((pairs, piece_rows, LANES), jnp.float32),
        ),
        in_specs=[vmem()] * (members + 4),
        out_specs=[vmem()] * 4,
        scratch_shapes=[
            pltpu.VMEM((members, padded_out, points), jnp.bfloat16),
            pltpu.VMEM((stack, members * points), jnp.bfloat16),
            pltpu.VMEM((tiles, 2 * half_rows, LANES), jnp.float32),
            pltpu.VMEM((2 * half_rows // pack, LANES), jnp.float32),
        ],
        cost_estimate=cost(
            2 * taps * stack * points * members * tiles * LANES, 6_000_000, 1_000_000
        ),
        compiler_params=limit(32),
        name="gradient",
    )(*outputs, x_even, x_odd, truth, widths[None, :])

    mine, *out_pieces = pl.pallas_call(
        functools.partial(core_add_kernel, plan),
        out_shape=[jax.ShapeDtypeStruct((piece_rows, LANES), jnp.float32)] + [piece] * (pairs - 1),
        in_specs=[vmem(), vmem()],
        out_specs=[vmem()] * pairs,
        cost_estimate=cost(0, 1_500_000),
        compiler_params=limit(16),
        name="core_add",
    )(keep, swap_lon(send, 1))
    got = []
    for at, value in enumerate(out_pieces, 1):
        got.append(swap_lon(value, 2 * at))
    final = pl.pallas_call(
        functools.partial(pair_add_kernel, plan, factor),
        out_shape=piece,
        in_specs=[vmem()] * pairs,
        out_specs=vmem(),
        cost_estimate=cost(0, 600_000),
        compiler_params=limit(16),
        name="pair_add",
    )(mine, *got)

    gathered = [final]
    for at in range(1, pairs):
        gathered.append(swap_lon(final, 2 * at))
    grad_shape = jax.ShapeDtypeStruct((total_taps, out_chan, in_chan), jnp.float32)
    blocks = full_blocks
    tail_rows = half_rows - special
    halves = []
    for second in range(2):
        group = range(second * pairs // 2, (second + 1) * pairs // 2)
        column = jnp.concatenate([gathered[s] for s in group])
        held = []
        for d in range(members):
            value = column
            if d:
                value = swap_member(column, d)
            held.append((d, (value, swap_lon(value, 1))))
        halves.append((group, held))
    rest_lanes = rest * LANES + extras
    short = half_rows // pack

    def assemble(second, final, held, extra_inputs, other_shape):
        group = halves[second][0]
        arrays, layout = [], []
        for d, both in held:
            for other, value in enumerate(both):
                arrays.append(value)
                layout += [(d, s, bool(other)) for s in group]
        count, each = len(arrays), len(group)
        stages = max(len(held) * main, 1)
        taps_held = per_half + second

        def kernel(*refs):
            pieces = [ref.at[pl.ds(at, 1)] for ref in refs[:count] for at in range(each)]
            assemble_kernel(plan, second, tuple(layout), final, *pieces, *refs[count:])

        specs = [vmem()] * count
        if second:
            specs += [vmem(), any_space] + [vmem()] * (len(extra_inputs) - 2)
        return pl.pallas_call(
            kernel,
            out_shape=[grad_shape, jax.ShapeDtypeStruct(other_shape, jnp.float32)],
            in_specs=specs,
            out_specs=[any_space, vmem()],
            scratch_shapes=[
                pltpu.VMEM((stages, half_rows, LANES), jnp.float32),
                pltpu.VMEM((members, short, LANES), jnp.float32),
                pltpu.VMEM((stages, taps_held, out_chan, LANES), jnp.float32),
                pltpu.VMEM((1, taps_held, out_chan, rest_lanes), jnp.float32),
                pltpu.SemaphoreType.DMA((2 * stages + 2,)),
            ],
            input_output_aliases={count + 1: 0} if second else {},
            cost_estimate=cost(0, 5_000_000),
            compiler_params=limit(24),
            name="assemble",
        )(*arrays, *extra_inputs)

    weight_grad, carry = assemble(0, "all", halves[0][1], (), (blocks, tail_rows, LANES))
    held = halves[1][1]
    if main:
        weight_grad, known = assemble(
            1, "early", held[:-1], (carry, weight_grad), (members + 1, short, LANES)
        )
        weight_grad, bias_out = assemble(
            1, "late", held[-1:], (carry, weight_grad, known), (1, out_chan)
        )
    else:
        weight_grad, bias_out = assemble(1, "all", held, (carry, weight_grad), (1, out_chan))
    bias_grad = bias_out[0]
    weight_grad = weight_grad.reshape(taps, taps, out_chan, in_chan)

    assert BLOCK == lon_dev
    out_grad = pl.pallas_call(
        functools.partial(out_grad_kernel, plan),
        out_shape=jax.ShapeDtypeStruct((lon_dev, rows_out, out_chan), jnp.bfloat16),
        in_specs=[vmem()],
        out_specs=vmem(),
        scratch_shapes=[pltpu.VMEM((rows_out, slots, LANES), jnp.float32)],
        cost_estimate=cost(0, 400_000),
        compiler_params=limit(8),
        name="out_grad",
    )(grad_own)
    out_grad = jnp.transpose(out_grad, (2, 1, 0))[None]
    capacity = max(2, 3 * rows_out // members)
    owned_score = pl.pallas_call(
        functools.partial(owned_kernel, plan),
        out_shape=jax.ShapeDtypeStruct((1, capacity * lon_dev), jnp.float32),
        in_specs=[smem(), vmem()],
        out_specs=vmem(),
        scratch_shapes=[pltpu.VMEM((round_up(rows_out + capacity, ROWS), LANES), jnp.float32)],
        cost_estimate=cost(0, 100_000),
        compiler_params=limit(8),
        name="owned",
    )(owner_start, score)
    owned_score = owned_score[None]
    return (out_grad, owned_score, weight_grad, bias_grad)


def solution(mesh):
    in_specs = (P("member", None, None, "lon"), P(), P(), P(None, None, "lon"), P(), P("lon", None))
    out_specs = (P("member", None, None, "lon"), P("lon", "member", None), P(), P())
    return jax.shard_map(body, mesh=mesh, in_specs=in_specs, out_specs=out_specs, check_vma=False)
```

```python
import functools
import math
import types

import jax
import jax.numpy as jnp
from jax import lax
from jax.experimental import pallas as pl
from jax.experimental.pallas import tpu as pltpu
from jax.sharding import PartitionSpec as P


BLOCK = 45
LANES = 128
ROWS = 8
SPECIAL = 16


NT = (((1,), (1,)), ((), ()))
NN = (((1,), (0,)), ((), ()))


def round_up(value, unit):
    return -(-value // unit) * unit


def vmem():
    return pl.BlockSpec(memory_space=pltpu.VMEM)


def smem():
    return pl.BlockSpec(memory_space=pltpu.SMEM)


def limit(mib):
    return pltpu.CompilerParams(vmem_limit_bytes=mib << 20)


def here():
    lon = lax.axis_index("lon")
    return lax.axis_index("member"), lax.div(lon, 2), lax.rem(lon, 2)


def cost(flops, moved, special=0):
    return pl.CostEstimate(flops=flops, bytes_accessed=moved, transcendentals=special)


def column_of(row_ref, fill):
    count = row_ref.shape[1]
    row = jnp.concatenate(
        [row_ref[...], jnp.full((1, LANES - count), fill, jnp.float32)], axis=1
    )
    return jnp.transpose(jnp.broadcast_to(row, (LANES, LANES)))[:, :1]


def strips_kernel(seen_ref, near_ref, far_ref):
    even = here()[2] == 0
    width = near_ref.shape[0]
    start = seen_ref[:width]
    end = seen_ref[seen_ref.shape[0] - width :]
    far_ref[...] = jnp.where(even, start, end)
    near_ref[...] = jnp.where(even, end, start)


def pack_kernel(plan, f_ref, near_ref, far_ref, *out_refs):
    members, main, rest = plan.members, plan.main, plan.rest
    pack, valid, sub = plan.pack, plan.valid, plan.sub
    rows_in, lon_dev, in_chan = f_ref.shape
    place_ref = here()
    halo = 2 * plan.half
    even = place_ref[2] == 0
    start_edge = f_ref[:, :halo, :].astype(jnp.float32)
    final = (lon_dev - halo) // ROWS * ROWS
    end_edge = f_ref[:, final:, :].astype(jnp.float32)[:, lon_dev - halo - final :]
    far_ref[...] = jnp.where(even, start_edge, end_edge).astype(far_ref.dtype)
    near_ref[...] = jnp.where(even, end_edge, start_edge).astype(near_ref.dtype)
    group = rows_in // pack
    base = main * members
    lane = lax.broadcasted_iota(jnp.int32, (1, 1, LANES), 2)
    full = (base + rest) * LANES
    slab = jnp.zeros((1, lon_dev, LANES), jnp.float32)
    for e in range(in_chan - full):
        for r in range(rows_in):
            value = f_ref[r : r + 1, :, full + e : full + e + 1].astype(jnp.float32)
            slab = jnp.where(lane == e * rows_in + r, value, slab)
    for d in range(members):
        owner = place_ref[0] ^ d
        out = out_refs[d]
        for k in range(main):
            spot = pl.ds(pl.multiple_of((k * members + owner) * LANES, LANES), LANES)
            out[k * rows_in : (k + 1) * rows_in] = f_ref[:, :, spot]
        for i in range(group):
            row = None
            for g in range(pack):
                for k in range(rest):
                    tile = f_ref[
                        g * group + i, :, (base + k) * LANES : (base + k + 1) * LANES
                    ].astype(jnp.float32)
                    start = g * valid + k * sub
                    moved = pltpu.roll(tile, lax.rem(start - owner * sub + LANES, LANES), 1)
                    row = moved if row is None else jnp.where(lane[0] >= start, moved, row)
            out[main * rows_in + i] = row.astype(out.dtype)
        out[main * rows_in + group] = slab[0].astype(out.dtype)


def stage_kernel(w_ref, w_out):
    _, out_chan, in_chan = w_ref.shape
    full = in_chan // LANES * LANES
    w_out[:, :, full:] = jnp.zeros(
        (w_out.shape[0], w_out.shape[1], w_out.shape[2] - full), w_out.dtype
    )
    w_out[:, :out_chan, :in_chan] = w_ref[...]


def forward_kernel(
    plan, f_s, near_ref, far_ref, w_s, b_ref, o_ref, x_s, acc_s,
):
    taps, half, offset = plan.taps, plan.half, plan.offset
    lon_dev, halo = plan.lon_dev, 2 * plan.half
    rows_in, slots, wide = x_s.shape
    out_chan, in_chan = plan.out_chan, near_ref.shape[2]
    padded_out = w_s.shape[1]
    rows_out = rows_in - taps + 1
    points = rows_out * slots
    bulk = lon_dev // ROWS * ROWS
    full = in_chan // LANES * LANES
    x_s[:, :, full:] = jnp.zeros((rows_in, slots, wide - full), x_s.dtype)
    x_s[:, offset : offset + bulk, :in_chan] = f_s[:, :bulk, :]
    near = near_ref[...].astype(jnp.float32)
    far = far_ref[...].astype(jnp.float32)
    even = here()[2] == 0
    first = jnp.concatenate(
        [
            jnp.zeros((rows_in, offset - halo, in_chan), jnp.float32),
            jnp.where(even, far, near),
        ],
        axis=1,
    )
    x_s[:, :offset, :in_chan] = first.astype(x_s.dtype)
    tail = slots - offset - bulk
    final = jnp.concatenate(
        [
            f_s[:, bulk:, :].astype(jnp.float32),
            jnp.where(even, near, far),
            jnp.zeros((rows_in, tail - (lon_dev - bulk) - halo, in_chan), jnp.float32),
        ],
        axis=1,
    )
    x_s[:, offset + bulk :, :in_chan] = final.astype(x_s.dtype)
    for a in range(taps):
        part = lax.dot_general(
            w_s[a * taps : (a + 1) * taps].reshape(taps * padded_out, wide),
            x_s[a : a + rows_out].reshape(points, wide),
            NT,
            preferred_element_type=jnp.float32,
        )
        if a == 0:
            acc_s[...] = part
        else:
            acc_s[...] += part
    slot = lax.broadcasted_iota(jnp.int32, (1, points), 1) % slots
    inside = (slot >= offset - half) & (slot < offset + lon_dev + half)
    bias = column_of(b_ref, 0.0)
    for lo in range(0, padded_out, 2 * ROWS):
        rows = slice(lo, lo + 2 * ROWS)
        total = jnp.zeros((2 * ROWS, points), jnp.float32) + bias[rows]
        for b in range(taps):
            piece = acc_s[b * padded_out + lo : b * padded_out + lo + 2 * ROWS, :]
            shift = (half - b) % points
            total = total + (pltpu.roll(piece, shift, 1) if shift else piece)
        row = lo + lax.broadcasted_iota(jnp.int32, (2 * ROWS, 1), 0)
        keep = inside & (row < out_chan)
        o_ref[rows, :] = jnp.where(keep, total, 0.0).astype(o_ref.dtype)


def prep_kernel(plan, obs_ref, near_ref, far_ref, own_ref, *refs):
    truth_ref, own_out_ref, row_s = refs[-3:]
    refs = refs[:-3]
    own_out_ref[...] = own_ref[...]
    half, offset, padded_out = plan.half, plan.offset, plan.padded_out
    even = here()[2] == 0
    near, far = near_ref[...], far_ref[...]
    out_chan = obs_ref.shape[2]
    total_rows = obs_ref.shape[1]
    width = plan.points // total_rows
    per = LANES // width
    row_s[...] = jnp.zeros(row_s.shape, jnp.float32)
    for x in range(half):
        row_s[:, offset - half + x, :out_chan] = jnp.where(even, far[x], near[x])
        row_s[:, offset + plan.lon_dev + x, :out_chan] = jnp.where(even, near[x], far[x])
    for x in range(plan.lon_dev):
        row_s[:, offset + x, :out_chan] = obs_ref[x]
    for j in range(total_rows // per):
        tile = row_s[j * per : (j + 1) * per].reshape(LANES, LANES)
        truth_ref[:, j * LANES : (j + 1) * LANES] = jnp.transpose(tile)[:padded_out]
    members, main = plan.members, plan.main
    pack, valid, extras = plan.pack, plan.valid, plan.extras
    out_ref = refs[-1]
    _, rows_in, slots, _ = out_ref.shape
    lon_dev = plan.lon_dev
    bulk = lon_dev // ROWS * ROWS
    group = rows_in // pack
    lane = lax.broadcasted_iota(jnp.int32, (1, LANES), 1)
    out_ref[:, :, bulk:, :] = jnp.zeros(
        (members, rows_in, slots - bulk, out_ref.shape[3]), out_ref.dtype
    )
    for d in range(members):
        ref = refs[d]
        for k in range(main):
            out_ref[d, :, :lon_dev, k * LANES : (k + 1) * LANES] = ref[
                k * rows_in : (k + 1) * rows_in
            ]
        slab = ref[main * rows_in + group].astype(jnp.float32)
        for g in range(pack):
            for i in range(group):
                value = ref[main * rows_in + i].astype(jnp.float32)
                if g:
                    value = pltpu.roll(value, LANES - g * valid, 1)
                r = g * group + i
                for e in range(extras):
                    shift = (valid + e - (e * rows_in + r)) % LANES
                    moved = pltpu.roll(slab, shift, 1) if shift else slab
                    value = jnp.where(lane == valid + e, moved, value)
                value = jnp.where(lane == valid + extras, 1.0, value)
                out_ref[d, r, :lon_dev, main * LANES :] = value.astype(out_ref.dtype)


def split_bias(tile, row_high):
    row = lax.broadcasted_iota(jnp.int32, tile.shape, 0)
    size = tile.shape[0]
    total = jnp.where(row == row_high, tile + pltpu.roll(tile, size - 1, 0), tile)
    left = total - total.astype(jnp.bfloat16).astype(jnp.float32)
    return jnp.where(row == row_high + 1, pltpu.roll(left, 1, 0), total)


def fix_rows(plan, ref, index, piece, value_of):
    @pl.when(piece == 2 * plan.pairs - 1)
    def _():
        lo = plan.special_row
        tile = value_of(lo, lo + SPECIAL)
        ref[index, lo : lo + SPECIAL, :] = split_bias(tile, plan.bias_row).astype(ref.dtype)


def gradient_kernel(plan, *refs):
    members, taps, half = plan.members, plan.taps, plan.half
    out_chan, padded_out, points = plan.out_chan, plan.padded_out, plan.points
    main, pairs, pack, valid = plan.main, plan.pairs, plan.pack, plan.valid
    rows_out, size, extras = plan.rows_out, plan.half_rows, plan.extras
    per_half, special = plan.per_half, plan.special
    place_ref = here()
    y_refs = refs[:members]
    x_ref, obs_ref, wid_ref = refs[members : 3 + members]
    g_ref, score_ref, send_ref, keep_ref = refs[3 + members : 7 + members]
    g_s, gs_s, wide_s, packed_s = refs[7 + members :]
    step = 2 * LANES
    width_all = column_of(wid_ref, 1.0)
    for left in range(0, points, step):
        tally = jnp.zeros((ROWS, step), jnp.float32)
        for lo in range(0, padded_out, 2 * ROWS):
            rows = slice(lo, lo + 2 * ROWS)
            cols = slice(left, left + step)
            shape = (2 * ROWS, step)
            width = width_all[rows]
            inverse = 1.0 / (width * width)
            values = [y[rows, cols].astype(jnp.float32) for y in y_refs]
            target = obs_ref[rows, cols]
            pair_sum = jnp.full(shape, float(members), jnp.float32)
            pull = [jnp.zeros(shape, jnp.float32) for _ in values]
            for x in range(members):
                for y in range(x + 1, members):
                    spread = values[x] - values[y]
                    kernel_pair = jnp.exp(-0.5 * spread * spread * inverse)
                    pair_sum = pair_sum + 2.0 * kernel_pair
                    weighted = kernel_pair * spread
                    pull[x] = pull[x] + weighted
                    pull[y] = pull[y] - weighted
            obs_sum = jnp.zeros(shape, jnp.float32)
            for x in range(members):
                misfit = values[x] - target
                kernel_obs = jnp.exp(-0.5 * misfit * misfit * inverse)
                obs_sum = obs_sum + kernel_obs
                grad = inverse * (misfit * kernel_obs - pull[x] / members)
                g_s[x, rows, cols] = grad.astype(jnp.bfloat16)
            terms = pair_sum / (2.0 * members * members) - obs_sum / members
            row = lo + lax.broadcasted_iota(jnp.int32, (2 * ROWS, 1), 0)
            terms = jnp.where(row < out_chan, terms, 0.0)
            tally = tally + terms[:ROWS] + terms[ROWS:]
        score_ref[:, left : left + step] = jnp.sum(tally, axis=0, keepdims=True) / out_chan
    g_ref[...] = g_s[0]
    for x in range(members):
        for lo in range(0, padded_out, 2 * ROWS):
            grad = g_s[x, lo : lo + 2 * ROWS, :].astype(jnp.float32)
            for b in range(taps):
                shift = (b - half - plan.offset) % points
                moved = pltpu.roll(grad, shift, 1) if shift else grad
                start = b * padded_out + lo
                gs_s[x, start : start + 2 * ROWS, :] = moved.astype(jnp.bfloat16)
    tiles = main + 1
    split = size - special - SPECIAL
    for h in range(2):
        wide_s[:, h * size + special : (h + 1) * size, :] = jnp.zeros(
            (tiles, size - special, LANES), jnp.float32
        )
    for a in range(taps):
        total = None
        for x in range(members):
            part = lax.dot_general(
                gs_s[x],
                x_ref[x, a : a + rows_out].reshape(points, tiles * LANES),
                NN,
                preferred_element_type=jnp.float32,
            )
            total = part if total is None else total + part
        for b in range(taps):
            tap = a * taps + b
            block = total[b * padded_out : (b + 1) * padded_out]
            across = jnp.transpose(block[:, main * LANES :])
            if tap < 2 * per_half:
                h, i = tap // per_half, tap % per_half
                spans = [(0, padded_out, h * size + i * padded_out)]
                line = h * size + special + i * extras
            else:
                first = size - split
                spans = [(0, split, first), (split, padded_out, size + first)]
                line = size + special + per_half * extras
            for k in range(tiles):
                for lo, hi, at in spans:
                    wide_s[k, at : at + hi - lo, :] = block[lo:hi, k * LANES : (k + 1) * LANES]
            for e in range(extras):
                wide_s[0, line + e : line + e + 1, :padded_out] = across[valid + e : valid + e + 1]
            if a == 0 and b == half:
                line = size + special + plan.bias_row
                ones = valid + extras
                wide_s[0, line : line + 1, :padded_out] = across[ones : ones + 1]
    short = size // pack
    lane = lax.broadcasted_iota(jnp.int32, (1, LANES), 1)
    for h in range(2):
        packed = wide_s[main, h * size : h * size + short, :]
        for g in range(1, pack):
            at = h * size + g * short
            moved = pltpu.roll(wide_s[main, at : at + short, :], g * valid, 1)
            packed = jnp.where(lane >= g * valid, moved, packed)
        packed_s[h * short : (h + 1) * short, :] = packed
    pair, core = place_ref[1], place_ref[2]
    main_rows = size // pairs
    rest_rows = main_rows // pack
    for s in range(pairs):
        for out, side in ((keep_ref, core), (send_ref, 1 - core)):
            piece = 2 * (pair ^ s) + side
            at = 0
            for k in range(main):
                source = pl.ds(pl.multiple_of(piece * main_rows, main_rows), main_rows)
                out[s, at : at + main_rows, :] = wide_s[k, source, :].astype(out.dtype)
                at += main_rows
            source = pl.ds(pl.multiple_of(piece * rest_rows, rest_rows), rest_rows)
            out[s, at : at + rest_rows, :] = packed_s[source, :].astype(out.dtype)
        spot = 2 * size - main_rows
        fix_rows(
            plan, send_ref, s, 2 * (pair ^ s) + 1 - core,
            lambda lo, hi: wide_s[0, spot + lo : spot + hi, :]
            if main
            else packed_s[spot + lo : spot + hi, :],
        )


def core_add_kernel(plan, keep_ref, got_ref, mine_ref, *out_refs):
    place_ref = here()
    mine_ref[...] = keep_ref[0] + got_ref[0].astype(jnp.float32)
    pair, core = place_ref[1], place_ref[2]
    for s in range(1, plan.pairs):
        out = out_refs[s - 1]
        out[0] = (keep_ref[s] + got_ref[s].astype(jnp.float32)).astype(out.dtype)
        fix_rows(
            plan, out, 0, 2 * (pair ^ s) + core,
            lambda lo, hi: keep_ref[s, lo:hi, :] + got_ref[s, lo:hi, :].astype(jnp.float32),
        )


def pair_add_kernel(plan, factor, mine_ref, *refs):
    place_ref = here()
    out = refs[-1]

    def value(lo, hi):
        total = mine_ref[lo:hi, :]
        for ref in refs[:-1]:
            total = total + ref[0, lo:hi, :].astype(jnp.float32)
        return total * factor

    out[0] = value(0, mine_ref.shape[0]).astype(out.dtype)
    fix_rows(plan, out, 0, 2 * place_ref[1] + place_ref[2], value)


def out_grad_kernel(plan, g_ref, out_ref, row_s):
    lon_dev, offset = plan.lon_dev, plan.offset
    rows_out, out_chan = out_ref.shape[1:]
    width = plan.points // rows_out
    per = LANES // width
    padded_out = g_ref.shape[0]
    for j in range(rows_out // per):
        tile = g_ref[:, j * LANES : (j + 1) * LANES].astype(jnp.float32)
        tile = jnp.concatenate(
            [tile, jnp.zeros((LANES - padded_out, LANES), jnp.float32)], axis=0
        )
        row_s[j * per : (j + 1) * per] = jnp.transpose(tile).reshape(per, width, LANES)
    for x in range(lon_dev):
        out_ref[x] = row_s[:, offset + x, :out_chan].astype(out_ref.dtype)


def owned_kernel(plan, start_ref, score_ref, out_ref, row_s):
    lon_dev, offset, points = plan.lon_dev, plan.offset, plan.points
    rows_out = plan.rows_out
    width = points // rows_out
    capacity = out_ref.shape[1] // lon_dev
    member = here()[0]
    first = start_ref[0, member]
    count = start_ref[0, member + 1] - first
    lane = lax.broadcasted_iota(jnp.int32, (1, points), 1)
    row_s[...] = jnp.zeros(row_s.shape, jnp.float32)
    score = score_ref[...]
    for i in range(rows_out):
        moved = pltpu.roll(score, (points - i * width - offset) % points, 1)
        row_s[i : i + 1, :] = jnp.where(lane < lon_dev, moved, 0.0)[:, :LANES]
    reach = round_up(capacity * lon_dev, LANES)
    total = jnp.zeros((1, reach), jnp.float32)
    blank = jnp.zeros((1, reach - LANES), jnp.float32)
    for t in range(capacity):
        row = jnp.where(t < count, row_s[pl.ds(first + t, 1), :], 0.0)
        row = jnp.concatenate([row, blank], axis=1)
        total = total + (pltpu.roll(row, t * lon_dev, 1) if t else row)
    out_ref[...] = total[:, : capacity * lon_dev]


def assemble_kernel(plan, second, layout, final, *refs):
    members, main, rest = plan.members, plan.main, plan.rest
    out_chan, padded_out, pairs = plan.out_chan, plan.padded_out, plan.pairs
    pack, valid, sub = plan.pack, plan.valid, plan.sub
    size, extras, per_half = plan.half_rows, plan.extras, plan.per_half
    special = plan.special
    member, pair, core = here()
    piece_refs = refs[: len(layout)]
    refs = refs[len(layout) :]
    own_half = lax.div(pair, pairs // 2)
    this_half = 1 - own_half if second else own_half
    low = this_half == 0
    main_rows = size // pairs
    rest_rows = main_rows // pack
    split = size - special - SPECIAL
    begin = special + SPECIAL
    known_ref = carry_ref = None
    if second:
        carry_ref, _, *refs = refs
        if final == "late":
            known_ref, *refs = refs
    out_ref, other_ref, main_s, packed_s, main_stage, rest_stage, sems = refs
    if known_ref is not None:
        packed_s[...] = known_ref[:members]
    shown = []
    for d, _, _ in layout:
        if d not in shown:
            shown.append(d)
    for ref, (d, s, other) in zip(piece_refs, layout):
        side = 1 - core if other else core
        piece = lax.rem(2 * (pair ^ s) + side, pairs)
        row = 0
        for k in range(main):
            spot = pl.ds(pl.multiple_of(piece * main_rows, ROWS), main_rows)
            main_s[shown.index(d) * main + k, spot, :] = ref[0, row : row + main_rows, :].astype(
                jnp.float32
            )
            row += main_rows
        spot = pl.ds(pl.multiple_of(piece * rest_rows, ROWS), rest_rows)
        packed_s[member ^ d, spot, :] = ref[0, row : row + rest_rows, :].astype(jnp.float32)
    lines = packed_s[0, special:begin, :] if not main else None
    for at, d in enumerate(shown if main else ()):
        found = main_s[at * main, special:begin, :]
        if lines is None:
            lines = found if known_ref is None else known_ref[members, :SPECIAL, :]
        lines = jnp.where(member == d, found, lines)
    copies = []

    def emit(source, stage, lanes):
        spans = [(pl.ds(0, per_half), pl.ds(this_half * per_half, per_half))]
        if second:
            spans.append((pl.ds(per_half, 1), pl.ds(2 * per_half, 1)))
        for from_span, to_span in spans:
            copy = pltpu.make_async_copy(
                source.at[stage, from_span],
                out_ref.at[to_span, :, lanes],
                sems.at[len(copies)],
            )
            copy.start()
            copies.append(copy)

    def fill(stage_ref, stage, lanes, tile, block):
        for i in range(per_half):
            stage_ref[stage, i, :, lanes] = tile[i * padded_out : i * padded_out + out_chan]
        mine = tile[begin:size]
        if second:
            theirs = carry_ref[block, SPECIAL:, :]
            stage_ref[stage, per_half, :split, lanes] = jnp.where(low, mine, theirs)
            stage_ref[stage, per_half, split:, lanes] = jnp.where(low, theirs, mine)[
                : out_chan - split
            ]
        else:
            other_ref[block, SPECIAL:, :] = mine

    if not second:
        other_ref[:, :SPECIAL, :] = jnp.zeros(
            (other_ref.shape[0], SPECIAL, LANES), jnp.float32
        )
        other_ref[0, :SPECIAL, :] = lines
    for at, d in enumerate(shown if main else ()):
        for k in range(main):
            block = k * members + (member ^ d)
            fill(main_stage, at * main + k, slice(None), main_s[at * main + k], block)
            emit(
                main_stage,
                at * main + k,
                pl.ds(pl.multiple_of(block * LANES, LANES), LANES),
            )
    if final == "early":
        other_ref[:members] = packed_s[...]
        other_ref[members] = jnp.zeros(other_ref.shape[1:], jnp.float32)
        other_ref[members, :SPECIAL, :] = lines
    else:
        lane = lax.broadcasted_iota(jnp.int32, (1, LANES), 1)
        base = main * members
        for k in range(rest):
            tiles = []
            for g in range(pack):
                tile = None
                for owner in range(members):
                    shift = (owner * sub - g * valid - k * sub) % LANES
                    value = packed_s[owner]
                    if shift:
                        value = pltpu.roll(value, shift, 1)
                    tile = (
                        value if tile is None else jnp.where(lane >= owner * sub, value, tile)
                    )
                tiles.append(tile)
            tile = tiles[0] if pack == 1 else jnp.concatenate(tiles, axis=0)
            fill(rest_stage, 0, slice(k * LANES, (k + 1) * LANES), tile, base + k)
        blank = jnp.zeros((LANES - SPECIAL, LANES), jnp.float32)

        def put_columns(rows, first, count, tap):
            columns = jnp.transpose(jnp.concatenate([rows, blank], axis=0))
            for i in range(count):
                for e in range(extras):
                    at = first + i * extras + e
                    lanes = slice(rest * LANES + e, rest * LANES + e + 1)
                    rest_stage[0, tap + i, :, lanes] = columns[:out_chan, at : at + 1]

        put_columns(lines, 0, per_half, 0)
        if second:
            top = jnp.where(low, carry_ref[0, :SPECIAL, :], lines)
            put_columns(top, per_half * extras, 1, per_half)
            line = plan.bias_row
            other_ref[...] = (top[line : line + 1] + top[line + 1 : line + 2])[:, :out_chan]
        emit(rest_stage, 0, pl.ds(base * LANES, rest * LANES + extras))
    for copy in copies:
        copy.wait()


def body(fields, weight, out_bias, observed, widths, owner_start):
    _, in_chan, rows_in, lon_dev = fields.shape
    taps, _, out_chan, _ = weight.shape
    half = taps // 2
    halo = 2 * half
    members = lax.axis_size("member")
    lon_count = lax.axis_size("lon")
    pairs = lon_count // 2
    rows_out = rows_in - taps + 1
    offset = round_up(halo, ROWS)
    slots = round_up(offset + lon_dev + halo, 2 * ROWS)
    points = rows_out * slots
    padded_out = round_up(out_chan, 2 * ROWS)
    full_blocks = in_chan // LANES
    main, rest = full_blocks // members, full_blocks % members
    sub = LANES // members
    valid = rest * sub
    pack = LANES // valid if rows_in % (LANES // valid) == 0 else 1
    extras = in_chan - full_blocks * LANES
    stack = taps * padded_out
    total_taps = taps * taps
    per_half = total_taps // 2
    special = per_half * padded_out
    half_rows = round_up(
        special + SPECIAL + round_up(-(-out_chan // 2), ROWS), ROWS * pack * pairs
    )
    bias_row = (per_half + 1) * extras
    assert rest and total_taps % 2 and bias_row + 2 <= SPECIAL
    wide = round_up(in_chan, LANES)
    plan = types.SimpleNamespace(
        members=members, taps=taps, half=half, offset=offset, lon_dev=lon_dev, out_chan=out_chan,
        padded_out=padded_out, rows_out=rows_out, points=points, main=main, rest=rest, pairs=pairs,
        pack=pack, valid=valid, sub=sub, extras=extras, half_rows=half_rows, per_half=per_half,
        special=special, bias_row=bias_row,
        special_row=special - (pairs - 1) * (half_rows // pairs),
    )
    factor = 1.0 / math.sqrt(members * rows_out * lon_dev * lon_count)

    def swap_lon(value, d):
        return lax.ppermute(value, "lon", [(i, i ^ d) for i in range(lon_count)])

    def swap_far(value):
        step = [(i, (i + 1 if i % 2 else i - 1) % lon_count) for i in range(lon_count)]
        return lax.ppermute(value, "lon", step)

    def swap_member(value, d):
        return lax.ppermute(value, "member", [(i, i ^ d) for i in range(members)])

    any_space = pl.BlockSpec(memory_space=pl.ANY)
    field = jnp.transpose(fields[0], (1, 2, 0))
    packed_rows = main * rows_in + rows_in // pack + 1
    edge = jax.ShapeDtypeStruct((rows_in, halo, in_chan), jnp.bfloat16)
    seen = jnp.transpose(observed, (2, 1, 0))
    strip = jax.ShapeDtypeStruct((half, rows_out, out_chan), jnp.float32)
    near, far, *packed = pl.pallas_call(
        functools.partial(pack_kernel, plan),
        out_shape=[edge, edge]
        + [jax.ShapeDtypeStruct((packed_rows, lon_dev, LANES), jnp.bfloat16)] * members,
        in_specs=[vmem()],
        out_specs=[vmem()] * (members + 2),
        cost_estimate=cost(0, 4_000_000),
        compiler_params=limit(16),
        name="pack",
    )(field)
    far = swap_far(far)
    near = swap_lon(near, 1)
    traded = [packed[0]]
    for d in range(1, members):
        traded.append(swap_member(packed[d], d))

    seen_near, seen_far = pl.pallas_call(
        strips_kernel,
        out_shape=[strip, strip],
        in_specs=[vmem()],
        out_specs=[vmem()] * 2,
        cost_estimate=cost(0, 400_000),
        compiler_params=limit(4),
        name="strips",
    )(seen)
    seen_far = swap_far(seen_far)
    seen_near = swap_lon(seen_near, 1)
    weight_flat = weight.reshape(total_taps, out_chan, in_chan)
    w_all = pl.pallas_call(
        stage_kernel,
        out_shape=jax.ShapeDtypeStruct((total_taps, padded_out, wide), jnp.bfloat16),
        in_specs=[vmem()],
        out_specs=vmem(),
        cost_estimate=cost(0, 5_000_000),
        compiler_params=limit(8),
        name="stage",
    )(weight_flat)
    own_outputs = pl.pallas_call(
        functools.partial(forward_kernel, plan),
        out_shape=jax.ShapeDtypeStruct((padded_out, points), jnp.bfloat16),
        in_specs=[vmem()] * 5,
        out_specs=vmem(),
        scratch_shapes=[
            pltpu.VMEM((rows_in, slots, wide), jnp.bfloat16),
            pltpu.VMEM((stack, points), jnp.float32),
        ],
        cost_estimate=cost(2 * taps * stack * points * wide, 6_000_000),
        compiler_params=limit(20),
        name="forward",
    )(field, near, far, w_all, out_bias[None, :])
    outputs = [own_outputs]
    for d in range(1, members):
        outputs.append(swap_member(own_outputs, d))

    tiles = main + 1
    x_all, truth, own_copy = pl.pallas_call(
        functools.partial(prep_kernel, plan),
        out_shape=(
            jax.ShapeDtypeStruct((members, rows_in, slots, tiles * LANES), jnp.bfloat16),
            jax.ShapeDtypeStruct((padded_out, points), jnp.float32),
            jax.ShapeDtypeStruct((padded_out, points), jnp.bfloat16),
        ),
        in_specs=[vmem()] * (members + 4),
        out_specs=[vmem()] * 3,
        scratch_shapes=[pltpu.VMEM((rows_out, slots, LANES), jnp.float32)],
        cost_estimate=cost(0, 4_000_000),
        compiler_params=limit(20),
        name="prep",
    )(seen, seen_near, seen_far, own_outputs, *traded)
    outputs[0] = own_copy

    main_rows = half_rows // pairs
    piece_rows = main * main_rows + main_rows // pack
    piece = jax.ShapeDtypeStruct((1, piece_rows, LANES), jnp.bfloat16)
    grad_own, score, send, keep = pl.pallas_call(
        functools.partial(gradient_kernel, plan),
        out_shape=(
            jax.ShapeDtypeStruct((padded_out, points), jnp.bfloat16),
            jax.ShapeDtypeStruct((1, points), jnp.float32),
            jax.ShapeDtypeStruct((pairs, piece_rows, LANES), jnp.bfloat16),
            jax.ShapeDtypeStruct((pairs, piece_rows, LANES), jnp.float32),
        ),
        in_specs=[vmem()] * (members + 3),
        out_specs=[vmem()] * 4,
        scratch_shapes=[
            pltpu.VMEM((members, padded_out, points), jnp.bfloat16),
            pltpu.VMEM((members, stack, points), jnp.bfloat16),
            pltpu.VMEM((tiles, 2 * half_rows, LANES), jnp.float32),
            pltpu.VMEM((2 * half_rows // pack, LANES), jnp.float32),
        ],
        cost_estimate=cost(
            2 * taps * stack * points * members * tiles * LANES, 6_000_000, 1_000_000
        ),
        compiler_params=limit(32),
        name="gradient",
    )(*outputs, x_all, truth, widths[None, :])

    mine, *out_pieces = pl.pallas_call(
        functools.partial(core_add_kernel, plan),
        out_shape=[jax.ShapeDtypeStruct((piece_rows, LANES), jnp.float32)] + [piece] * (pairs - 1),
        in_specs=[vmem(), vmem()],
        out_specs=[vmem()] * pairs,
        cost_estimate=cost(0, 1_500_000),
        compiler_params=limit(16),
        name="core_add",
    )(keep, swap_lon(send, 1))
    got = []
    for at, value in enumerate(out_pieces, 1):
        got.append(swap_lon(value, 2 * at))
    final = pl.pallas_call(
        functools.partial(pair_add_kernel, plan, factor),
        out_shape=piece,
        in_specs=[vmem()] * pairs,
        out_specs=vmem(),
        cost_estimate=cost(0, 600_000),
        compiler_params=limit(16),
        name="pair_add",
    )(mine, *got)

    gathered = [final]
    for at in range(1, pairs):
        gathered.append(swap_lon(final, 2 * at))
    grad_shape = jax.ShapeDtypeStruct((total_taps, out_chan, in_chan), jnp.float32)
    blocks = full_blocks
    tail_rows = half_rows - special
    halves = []
    for second in range(2):
        group = range(second * pairs // 2, (second + 1) * pairs // 2)
        column = jnp.concatenate([gathered[s] for s in group])
        middle = len(group) // 2
        held = []
        for d in range(members):
            parts = [(column, tuple(group))]
            if members == 4 and d == 3 and second == 0 and middle:
                parts = []
                for way, span in ((1, slice(0, middle)), (2, slice(middle, len(group)))):
                    value = swap_member(held[way][1][0][0][0][span], 3 - way)
                    parts.append((value, tuple(group)[span]))
            elif d:
                parts = [(swap_member(column, d), tuple(group))]
            held.append(
                (d, [((value, swap_lon(value, 1)), shifts) for value, shifts in parts])
            )
        halves.append((group, held))
    rest_lanes = rest * LANES + extras
    short = half_rows // pack

    def assemble(second, final, held, extra_inputs, other_shape):
        arrays, layout, spots = [], [], []
        for d, parts in held:
            for both, shifts in parts:
                for other, value in enumerate(both):
                    spots += [(len(arrays), at) for at in range(len(shifts))]
                    arrays.append(value)
                    layout += [(d, s, bool(other)) for s in shifts]
        count = len(arrays)
        stages = max(len(held) * main, 1)
        taps_held = per_half + second

        def kernel(*refs):
            pieces = [refs[which].at[pl.ds(at, 1)] for which, at in spots]
            assemble_kernel(plan, second, tuple(layout), final, *pieces, *refs[count:])

        specs = [vmem()] * count
        if second:
            specs += [vmem(), any_space] + [vmem()] * (len(extra_inputs) - 2)
        return pl.pallas_call(
            kernel,
            out_shape=[grad_shape, jax.ShapeDtypeStruct(other_shape, jnp.float32)],
            in_specs=specs,
            out_specs=[any_space, vmem()],
            scratch_shapes=[
                pltpu.VMEM((stages, half_rows, LANES), jnp.float32),
                pltpu.VMEM((members, short, LANES), jnp.float32),
                pltpu.VMEM((stages, taps_held, out_chan, LANES), jnp.float32),
                pltpu.VMEM((1, taps_held, out_chan, rest_lanes), jnp.float32),
                pltpu.SemaphoreType.DMA((2 * stages + 2,)),
            ],
            input_output_aliases={count + 1: 0} if second else {},
            cost_estimate=cost(0, 5_000_000),
            compiler_params=limit(24),
            name="assemble",
        )(*arrays, *extra_inputs)

    weight_grad, carry = assemble(0, "all", halves[0][1], (), (blocks, tail_rows, LANES))
    held = halves[1][1]
    if main:
        weight_grad, known = assemble(
            1, "early", held[:-1], (carry, weight_grad), (members + 1, short, LANES)
        )
        weight_grad, bias_out = assemble(
            1, "late", held[-1:], (carry, weight_grad, known), (1, out_chan)
        )
    else:
        weight_grad, bias_out = assemble(1, "all", held, (carry, weight_grad), (1, out_chan))
    bias_grad = bias_out[0]
    weight_grad = weight_grad.reshape(taps, taps, out_chan, in_chan)

    assert BLOCK == lon_dev
    out_grad = pl.pallas_call(
        functools.partial(out_grad_kernel, plan),
        out_shape=jax.ShapeDtypeStruct((lon_dev, rows_out, out_chan), jnp.bfloat16),
        in_specs=[vmem()],
        out_specs=vmem(),
        scratch_shapes=[pltpu.VMEM((rows_out, slots, LANES), jnp.float32)],
        cost_estimate=cost(0, 400_000),
        compiler_params=limit(8),
        name="out_grad",
    )(grad_own)
    out_grad = jnp.transpose(out_grad, (2, 1, 0))[None]
    capacity = max(2, 3 * rows_out // members)
    owned_score = pl.pallas_call(
        functools.partial(owned_kernel, plan),
        out_shape=jax.ShapeDtypeStruct((1, capacity * lon_dev), jnp.float32),
        in_specs=[smem(), vmem()],
        out_specs=vmem(),
        scratch_shapes=[pltpu.VMEM((round_up(rows_out + capacity, ROWS), LANES), jnp.float32)],
        cost_estimate=cost(0, 100_000),
        compiler_params=limit(8),
        name="owned",
    )(owner_start, score)
    owned_score = owned_score[None]
    return (out_grad, owned_score, weight_grad, bias_grad)


def solution(mesh):
    in_specs = (P("member", None, None, "lon"), P(), P(), P(None, None, "lon"), P(), P("lon", None))
    out_specs = (P("member", None, None, "lon"), P("lon", "member", None), P(), P())
    return jax.shard_map(body, mesh=mesh, in_specs=in_specs, out_specs=out_specs, check_vma=False)
```
